32 devices in a mesh: tm: 4 (over z), gx: 2 (over x), gy: 4 (over y, core).
Axes of the slice: x: 2, y: 2, z: 4, core: 2. Of those that a mesh axis runs over, the one named last changes fastest.
Arguments:
- state_starts: float32 [4, 64, 64, 512], P('tm', None, 'gx', 'gy'), may hold values from -4 to 4, as said below
- diffusivity: float32 [64], replicated, may hold values from 0.3 to 1.2
- wind: float32 [2, 64], replicated, may hold values from -0.6 to 0.6
Outputs:
- segment_ends: float32 [4, 64, 64, 512], P('tm', None, 'gx', 'gy')
The draws below stay inside these ranges and needn't reach their ends.
Inputs may be any that keep to these rules, and one draw needn't show every extreme that they name: `state_starts`: states of order one.
All inputs are finite; a program needn't handle non-finite values.
Results may differ from the reference program's by a relative error of at most 0.0001.
Values sent between devices are 32-bit elements; how exact they have to be, the bound alone decides.
A program may use at most 64 MiB of HBM per device.

```python
import math
import jax
import jax.numpy as jnp

L = 64
SUB = 4
SEGMENTS = 4
NX = 64
NY = 512


def draw_state_starts(key, part):
    shape = (SEGMENTS, L, NX, NY)
    return jnp.clip(jax.random.normal(key, shape, jnp.float32), -4.0, 4.0)


def setup_inputs(seed: int = 0) -> dict:
    arg_keys = jax.random.split(jax.random.key(seed), 4)
    return {
        "state_starts": draw_state_starts(jax.random.fold_in(arg_keys[3], 71), 0),
        "diffusivity": jnp.clip(jnp.exp(jax.random.uniform(arg_keys[1], (L,), jnp.float32, math.log(0.3), math.log(1.2))), 0.3, 1.2),
        "wind": jnp.clip(jax.random.uniform(arg_keys[2], (2, L), jnp.float32, -0.6, 0.6), -0.6, 0.6),
    }


time_step = 0.2
weights_low = (0.375, 0.125, 0.0, 0.0)
weights_mid = (0.625, 0.875, 0.875, 0.625)
weights_high = (0.0, 0.0, 0.125, 0.375)


def advance(padded, diffuse, wind_east, wind_north, factor):
    centre = padded[:, 1:-1, 1:-1]
    east = padded[:, 2:, 1:-1]
    west = padded[:, :-2, 1:-1]
    north = padded[:, 1:-1, 2:]
    south = padded[:, 1:-1, :-2]
    laplace = east + west + north + south - 4.0 * centre
    slope = wind_east * (east - west) * 0.5 + wind_north * (north - south) * 0.5
    return centre + time_step * (factor * diffuse * laplace - centre * slope)


def pad_zero(field):
    return jnp.pad(field, ((0, 0), (1, 1), (1, 1)))


def restrict(field):
    levels, rows, cols = field.shape
    return field.reshape(levels, rows // 4, 4, cols // 4, 4).mean(axis=(2, 4))


def prolong(padded):
    levels, rows_ext, cols_ext = padded.shape
    coarse_rows = rows_ext - 2
    coarse_cols = cols_ext - 2
    parts = [weights_low[offset] * padded[:, :-2, :] + weights_mid[offset] * padded[:, 1:-1, :] + weights_high[offset] * padded[:, 2:, :] for offset in range(4)]
    along = jnp.stack(parts, axis=2).reshape(levels, 4 * coarse_rows, cols_ext)
    parts = [weights_low[offset] * along[:, :, :-2] + weights_mid[offset] * along[:, :, 1:-1] + weights_high[offset] * along[:, :, 2:] for offset in range(4)]
    return jnp.stack(parts, axis=3).reshape(levels, 4 * coarse_rows, 4 * coarse_cols)


def reference(state_starts, diffusivity, wind):
    diffuse = diffusivity[:, None, None]
    wind_east = wind[0][:, None, None]
    wind_north = wind[1][:, None, None]
    fine_ends = []
    old_images = []
    coarse_first = restrict(state_starts[0])
    for segment in range(SEGMENTS):
        field = state_starts[segment]
        for substep in range(SUB):
            field = advance(pad_zero(field), diffuse, wind_east, wind_north, 1.0)
        fine_ends.append(field)
        coarse_old = restrict(state_starts[segment])
        old_images.append(advance(pad_zero(coarse_old), diffuse, wind_east, wind_north, 0.25))
    coarse = coarse_first
    results = []
    for segment in range(SEGMENTS):
        change = advance(pad_zero(coarse), diffuse, wind_east, wind_north, 0.25) - old_images[segment]
        ending = fine_ends[segment] + prolong(pad_zero(change))
        results.append(ending)
        coarse = restrict(ending)
    return jnp.stack(results)
```

```python
import functools

import jax
import jax.numpy as jnp
from jax import lax
from jax.experimental import pallas as pl
from jax.experimental.pallas import tpu as pltpu
from jax.sharding import PartitionSpec as P

SUB = 4
REACH = SUB
RATIO = 4
LANES = 128
EDGE = 8
FRONT = 2 * EDGE
COARSE_REACH = 2

time_step = 0.2
weights_low = (0.375, 0.125, 0.0, 0.0)
weights_mid = (0.625, 0.875, 0.875, 0.625)
weights_high = (0.0, 0.0, 0.125, 0.375)
mean_side, mean_mid = 0.125, 0.75

PLANE = tuple((dx, dy) for dx in (-1, 0, 1) for dy in (-1, 0, 1))
AROUND = tuple(d for d in PLANE if d != (0, 0))


def conjunction(conditions):
    total = True
    for condition in conditions:
        total = condition if total is True else jnp.logical_and(total, condition)
    return total


def kernel(
    sizes, levels, rows, cols,
    x_hbm, diff_hbm, wind_hbm, out_ref,
    x_ref, diff_ref, wind_ref, load_sems, ready,
    first, second, x_send, x_recv, y_send, y_recv, corner_recv,
    old_wide, new_wide, extended, old_image, change,
    sent, fine_mean, line, fine_line, spread_rows, turned,
    fine_out, fine_in, old_out, old_in, chain_out, chain_in, *strip_refs,
):
    n_tm, n_gx, n_gy = sizes
    tm, gx, gy = lax.axis_index("tm"), lax.axis_index("gx"), lax.axis_index("gy")
    packs = LANES // levels
    part = rows // packs
    part_c = part // RATIO
    cols_c = cols // RATIO
    wide = part + 2 * REACH
    wide_c = part_c + 2 * COARSE_REACH
    end = FRONT + cols
    end_c = FRONT + cols_c

    def there(dz, dx, dy):
        tests = []
        for place, move, count in ((tm, dz, n_tm), (gx, dx, n_gx), (gy, dy, n_gy)):
            if move < 0:
                tests.append(place > 0)
            if move > 0:
                tests.append(place < count - 1)
        return conjunction(tests)

    def guarded(condition, action):
        if condition is True:
            action()
        else:
            pl.when(condition)(action)

    def target(dz, dx, dy):
        return (tm + dz, gx + dx, gy + dy)

    loads = [
        pltpu.make_async_copy(source, landing, load_sems.at[k])
        for k, (source, landing) in enumerate(((x_hbm, x_ref), (diff_hbm, diff_ref), (wind_hbm, wind_ref)))
    ]
    for load in loads:
        load.start()

    barrier = pltpu.get_barrier_semaphore()
    partners = [(0, dx, dy) for dx, dy in AROUND] + [(-1, 0, 0), (1, 0, 0)]
    partners.sort(key=lambda move: -sum(map(abs, move)))
    awaited = jnp.int32(0)
    for move in partners:
        def greet(move=move):
            pl.semaphore_signal(barrier, inc=1, device_id=target(*move), device_id_type=pl.DeviceIdType.MESH)
        guarded(there(*move), greet)
        awaited = awaited + there(*move).astype(jnp.int32)

    def send_all(copies, dz, moves):
        for move in moves:
            guarded(there(dz, *move), lambda move=move: copies[move].start())

    def sends_done(copies, dz, moves):
        for move in moves:
            guarded(there(dz, *move), lambda move=move: copies[move].wait_send())

    def all_arrived(copies, dz, moves):
        for dx, dy in moves:
            guarded(there(-dz, -dx, -dy), lambda move=(dx, dy): copies[move].wait_recv())

    def remote(source, landing, out_sem, in_sem, move):
        return pltpu.make_async_remote_copy(
            src_ref=source, dst_ref=landing, send_sem=out_sem, recv_sem=in_sem,
            device_id=target(*move), device_id_type=pl.DeviceIdType.MESH,
        )

    def index_of(move):
        return (move[0] + 1) * 3 + move[1] + 1

    fine_copies = {}
    for move in AROUND:
        dx, dy = move
        k = index_of(move)
        if dy == 0:
            source, landing = (buffer.at[(dx + 1) // 2, pl.ds(0, REACH // 2)] for buffer in (x_send, x_recv))
        elif dx == 0:
            source, landing = y_send.at[(dy + 1) // 2], y_recv.at[(1 - dy) // 2]
        else:
            source = y_send.at[(dy + 1) // 2, pl.ds(0 if dx < 0 else part - REACH, REACH)]
            landing = corner_recv.at[(1 - dx) // 2, (1 - dy) // 2]
        fine_copies[move] = remote(source, landing, fine_out.at[k], fine_in.at[k], (0, dx, dy))
    later_copies = {}
    for dx in (-1, 1):
        k = 9 + (dx + 1) // 2
        source, landing = (buffer.at[(dx + 1) // 2, pl.ds(REACH // 2, REACH // 2)] for buffer in (x_send, x_recv))
        later_copies[dx, 0] = remote(source, landing, fine_out.at[k], fine_in.at[k], (0, dx, 0))

    def coarse_copies(main, wide_in, strips, out_sems, in_sems, dz):
        row_out, row_in, side_out, side_in, corner_out, corner_in = strips
        copies = {}
        for dx, dy in PLANE if dz else AROUND:
            k = index_of((dx, dy))
            towards_x, towards_y = (dx + 1) // 2, (dy + 1) // 2
            if dx == 0 and dy == 0:
                source, landing = main, wide_in.at[pl.ds(COARSE_REACH, part_c), pl.ds(FRONT, cols_c)]
            elif dy == 0:
                source, landing = row_out.at[towards_x], row_in.at[towards_x, pl.ds(FRONT, cols_c)]
            elif dx == 0:
                source, landing = side_out.at[towards_y], side_in.at[towards_y]
            else:
                source, landing = corner_out.at[towards_x, towards_y], corner_in.at[towards_x, towards_y]
            copies[dx, dy] = remote(source, landing, out_sems.at[k], in_sems.at[k], (dz, dx, dy))
        return copies

    old_strips, new_strips = strip_refs[:6], strip_refs[6:]
    old_copies = coarse_copies(None, old_wide, old_strips, old_out, old_in, 0)
    chain_copies = coarse_copies(sent, new_wide, new_strips, chain_out, chain_in, 1)

    lane = lax.broadcasted_iota(jnp.int32, (1, LANES), 1)
    pack = lane // levels

    def packed(row):
        return jnp.concatenate([row] * packs, axis=1)

    def advance(source, row, start, count, consts):
        keep, spread, along_x, along_y = consts
        centre = source[row, pl.ds(start, count), :]
        east = source[row + 1, pl.ds(start, count), :]
        west = source[row - 1, pl.ds(start, count), :]
        north = source[row, pl.ds(start + 1, count), :]
        south = source[row, pl.ds(start - 1, count), :]
        pushed = along_x * (east - west) + along_y * (north - south)
        return centre * (keep - pushed) + spread * ((east + west) + (north + south))

    def native_row(x):
        if x < 0:
            return x_recv[1, x + REACH]
        if x >= rows:
            return x_recv[0, x - rows]
        return x_ref[pl.ds(x, levels, stride=rows), :]

    def bring_in(row):
        stacked = jnp.concatenate([native_row(p * part + row - REACH) for p in range(packs)], axis=0)
        first[row, pl.ds(FRONT, cols), :] = stacked.T

    for load in loads:
        load.wait()
    diffuse = packed(diff_ref[...])
    east_wind = packed(wind_ref[0:1, :])
    north_wind = packed(wind_ref[1:2, :])

    def constants(factor):
        spread = (time_step * factor) * diffuse
        return 1.0 - 4.0 * spread, spread, (0.5 * time_step) * east_wind, (0.5 * time_step) * north_wind

    fine_constants = constants(1.0)
    coarse_constants = constants(0.25)

    for r in range(REACH):
        x_send[0, r] = native_row(r)
        x_send[1, r] = native_row(rows - REACH + r)
    x_moves = tuple(m for m in AROUND if m[1] == 0)
    y_moves = tuple(m for m in AROUND if m[1] != 0)
    low_lanes = lane < levels
    high_lanes = lane >= LANES - levels
    pl.semaphore_wait(barrier, awaited)

    @pl.when(tm > 0)
    def _():
        pl.semaphore_signal(ready, inc=1, device_id=target(-1, 0, 0), device_id_type=pl.DeviceIdType.MESH)

    side_moves = tuple(m for m in AROUND if m[0] == 0)
    corner_moves = tuple(m for m in y_moves if m[0] != 0)
    send_all(fine_copies, 0, x_moves)
    for row in range(REACH, REACH + part):
        bring_in(row)
    for row in range(part):
        y_send[0, row] = first[REACH + row, pl.ds(FRONT, REACH), :]
        y_send[1, row] = first[REACH + row, pl.ds(end - REACH, REACH), :]
    send_all(fine_copies, 0, side_moves + corner_moves)

    def restricted(source, row):
        total = source[REACH + row * RATIO, pl.ds(FRONT, cols), :]
        for r in range(1, RATIO):
            total = total + source[REACH + row * RATIO + r, pl.ds(FRONT, cols), :]
        fine_line[...] = total
        mean = fine_line[pl.ds(0, cols_c, stride=RATIO), :]
        for o in range(1, RATIO):
            mean = mean + fine_line[pl.ds(o, cols_c, stride=RATIO), :]
        return mean * (1.0 / RATIO**2)

    def swapped(value):
        return pltpu.roll(value, levels, 1)

    def pack_strips(row_of, strips):
        row_out, _, side_out, _, corner_out, _ = strips
        row_out[0] = jnp.where(low_lanes, row_of(0, 0, cols_c), swapped(row_of(1, 0, cols_c)))
        row_out[1] = jnp.where(low_lanes, swapped(row_of(part_c - 2, 0, cols_c)), row_of(part_c - 1, 0, cols_c))
        for side, col in ((0, 0), (1, cols_c - COARSE_REACH)):
            for row in range(part_c):
                side_out[side, pl.ds(COARSE_REACH * row, COARSE_REACH), :] = row_of(row, col, COARSE_REACH)
            for towards in range(2):
                corner_out[towards, side, pl.ds(0, COARSE_REACH), :] = row_out[towards, pl.ds(col, COARSE_REACH), :]

    def old_row(row, col, count):
        return old_wide[COARSE_REACH + row, pl.ds(FRONT + col, count), :]

    for row in range(part_c):
        old_wide[COARSE_REACH + row, pl.ds(FRONT, cols_c), :] = restricted(first, row)
    pack_strips(old_row, old_strips)
    send_all(old_copies, 0, AROUND)
    send_all(later_copies, 0, x_moves)

    def inside_x(row, reach, length):
        place = (gx * packs + pack) * length + (row - reach)
        return jnp.logical_and(place >= 0, place < n_gx * packs * length)

    def inside_y(start, count, length):
        place = gy * length + (start - FRONT) + lax.broadcasted_iota(jnp.int32, (count, LANES), 0)
        return jnp.logical_and(place >= 0, place < n_gy * length)

    edges = ((FRONT - EDGE, inside_y(FRONT - EDGE, EDGE, cols)), (end, inside_y(end, EDGE, cols)))
    reaches = ((FRONT - REACH, inside_y(FRONT - REACH, REACH, cols)), (end, inside_y(end, REACH, cols)))
    halo_rows = [*range(REACH), *range(REACH + part, wide)]
    half = cols // 2

    def update(source, dest, row, consts, last):
        for start, count in ((FRONT, half), (FRONT + half, cols - half)):
            dest[row, pl.ds(start, count), :] = advance(source, row, start, count, consts)
        if not last:
            for start, mask in edges:
                value = advance(source, row, start, EDGE, consts)
                dest[row, pl.ds(start, EDGE), :] = jnp.where(mask, value, 0.0)

    buffers = (first, second)

    all_arrived(fine_copies, 0, side_moves)
    for side, (start, mask) in enumerate(reaches):
        for row in range(part):
            first[REACH + row, pl.ds(start, REACH), :] = jnp.where(mask, y_recv[side, row], 0.0)
    for step in range(1, SUB + 1):
        def inner_row(row, step=step):
            update(buffers[(step - 1) % 2], buffers[step % 2], row, fine_constants, step == SUB)

        pl.loop(REACH + step, REACH + part - step, unroll=2)(inner_row)

    count_c = cols_c + 2 * EDGE
    begin_c = FRONT - EDGE
    mask_y = inside_y(begin_c, count_c, cols_c)

    def extend(buffer, strips):
        _, row_in, _, side_in, _, corner_in = strips
        for side, col in ((0, end_c), (1, FRONT - COARSE_REACH)):
            for row in range(part_c):
                buffer[COARSE_REACH + row, pl.ds(col, COARSE_REACH), :] = side_in[
                    side, pl.ds(COARSE_REACH * row, COARSE_REACH), :
                ]
            for towards in range(2):
                row_in[towards, pl.ds(col, COARSE_REACH), :] = corner_in[towards, side, pl.ds(0, COARSE_REACH), :]

        def own(row):
            return buffer[COARSE_REACH + row, pl.ds(begin_c, count_c), :]

        above, below = (row_in[towards, pl.ds(begin_c, count_c), :] for towards in (0, 1))
        values = [
            jnp.where(low_lanes, below, swapped(own(part_c - 2))),
            swapped(jnp.where(high_lanes, below, own(part_c - 1))),
            *[own(row) for row in range(part_c)],
            swapped(jnp.where(low_lanes, above, own(0))),
            jnp.where(high_lanes, above, swapped(own(1))),
        ]
        for row, value in enumerate(values):
            mask = mask_y
            if not COARSE_REACH <= row < COARSE_REACH + part_c:
                mask = jnp.logical_and(mask_y, inside_x(row, COARSE_REACH, part_c))
            extended[row, pl.ds(begin_c, count_c), :] = jnp.where(mask, value, 0.0)

    all_arrived(old_copies, 0, AROUND)
    sends_done(old_copies, 0, AROUND)
    extend(old_wide, old_strips)
    for row in range(1, wide_c - 1):
        old_image[row - 1] = advance(extended, row, begin_c, count_c, coarse_constants)


    def compute_change():
        for row in range(1, wide_c - 1):
            moved = advance(extended, row, begin_c, count_c, coarse_constants) - old_image[row - 1]
            mask = jnp.logical_and(mask_y, inside_x(row, COARSE_REACH, part_c))
            change[row - 1, pl.ds(begin_c, count_c), :] = jnp.where(mask, moved, 0.0)

    def change_row(row):
        return change[row, pl.ds(begin_c, count_c), :]

    def smoothed(row):
        line[pl.ds(begin_c, count_c), :] = (
            mean_side * (change_row(row) + change_row(row + 2)) + mean_mid * change_row(row + 1)
        )
        sides = line[pl.ds(FRONT - 1, cols_c), :] + line[pl.ds(FRONT + 1, cols_c), :]
        return mean_side * sides + mean_mid * line[pl.ds(FRONT, cols_c), :]

    @pl.when(tm == 0)
    def _():
        compute_change()
        for row in range(part_c):
            sent[row] = smoothed(row)

    all_arrived(fine_copies, 0, x_moves)
    all_arrived(later_copies, 0, x_moves)
    for row in halo_rows:
        bring_in(row)
        inner = first[row, pl.ds(FRONT, cols), :]
        first[row, pl.ds(FRONT, cols), :] = jnp.where(inside_x(row, REACH, part), inner, 0.0)
    all_arrived(fine_copies, 0, corner_moves)
    for side, (start, mask_side) in enumerate(reaches):
        for row in halo_rows:
            if row < REACH:
                here = jnp.where(high_lanes, corner_recv[0, side, row], y_recv[side, row + part - REACH])
                here = pltpu.roll(here, levels, 1)
            else:
                here = jnp.where(low_lanes, corner_recv[1, side, row - part - REACH], y_recv[side, row - part - REACH])
                here = pltpu.roll(here, LANES - levels, 1)
            mask = jnp.logical_and(mask_side, inside_x(row, REACH, part))
            first[row, pl.ds(start, REACH), :] = jnp.where(mask, here, 0.0)
    for step in range(1, SUB + 1):
        def outer_row(row, step=step):
            for shifted in (row, row + part + REACH - 2 * step):
                mask_x = inside_x(shifted, REACH, part)
                consts = tuple(jnp.where(mask_x, c, 0.0) for c in fine_constants)
                update(buffers[(step - 1) % 2], buffers[step % 2], shifted, consts, step == SUB)

        pl.loop(step, REACH + step)(outer_row)
    fine = buffers[SUB % 2]

    for row in range(part_c):
        fine_mean[row] = restricted(fine, row)

    def write_fine():
        for row in range(part):
            turned[row] = fine[REACH + row, pl.ds(FRONT, cols), :].T

    def pass_on():
        pl.semaphore_wait(ready, 1)
        pack_strips(lambda row, col, count: sent[row, pl.ds(col, count), :], new_strips)
        send_all(chain_copies, 1, AROUND)
        send_all(chain_copies, 1, ((0, 0),))

    @pl.when(jnp.logical_and(tm == 0, tm < n_tm - 1))
    def _():
        for row in range(part_c):
            sent[row] = fine_mean[row] + sent[row]
        pass_on()

    write_fine()

    @pl.when(tm > 0)
    def _():
        all_arrived(chain_copies, 1, PLANE)
        extend(new_wide, new_strips)
        compute_change()

    @pl.when(jnp.logical_and(tm > 0, tm < n_tm - 1))
    def _():
        for row in range(part_c):
            sent[row] = fine_mean[row] + smoothed(row)
        pass_on()

    coarse_col = lax.broadcasted_iota(jnp.int32, (count_c, cols), 0) - EDGE
    fine_col = lax.broadcasted_iota(jnp.int32, (count_c, cols), 1)
    offset_of = fine_col & (RATIO - 1)
    apart = coarse_col - (fine_col >> (RATIO.bit_length() - 1))
    spreading = jnp.zeros((count_c, cols), jnp.float32)
    for o in range(RATIO):
        for distance, weights in ((-1, weights_low), (0, weights_mid), (1, weights_high)):
            chosen = jnp.logical_and(offset_of == o, apart == distance)
            spreading = jnp.where(chosen, weights[o], spreading)
    spreading = jnp.concatenate([spreading.astype(jnp.bfloat16)] * 3, axis=0)
    for row in range(part_c + 2):
        rest, pieces = change_row(row), []
        for _ in range(3):
            piece = rest.astype(jnp.bfloat16).astype(jnp.float32)
            pieces.append(piece)
            rest = rest - piece
        split = jnp.concatenate(pieces, axis=0).T.astype(jnp.bfloat16)
        spread_rows[row] = jnp.dot(split, spreading, preferred_element_type=jnp.float32)

    for row in range(part):
        at, o = row // RATIO, row % RATIO
        total = turned[row] + weights_mid[o] * spread_rows[at + 1]
        if weights_low[o]:
            total = total + weights_low[o] * spread_rows[at]
        if weights_high[o]:
            total = total + weights_high[o] * spread_rows[at + 2]
        for p in range(packs):
            out_ref[pl.ds(p * part + row, levels, stride=rows), :] = total[p * levels : (p + 1) * levels]

    sends_done(fine_copies, 0, AROUND)
    sends_done(later_copies, 0, x_moves)
    pl.when(tm < n_tm - 1)(lambda: sends_done(chain_copies, 1, PLANE))


def shards(sizes, state_starts, diffusivity, wind):
    _, levels, rows, cols = state_starts.shape
    packs = LANES // levels
    if packs != 2 or levels * packs != LANES:
        raise ValueError(levels)
    part = rows // packs
    part_c = part // RATIO
    cols_c = cols // RATIO
    wide, wide_c = part + 2 * REACH, part_c + 2 * COARSE_REACH
    vmem = functools.partial(pltpu.VMEM, dtype=jnp.float32)
    scratch = [
        vmem((levels * rows, cols)),
        vmem((1, levels)),
        vmem((2, levels)),
        pltpu.SemaphoreType.DMA((3,)),
        pltpu.SemaphoreType.REGULAR,
        vmem((wide, cols + 2 * FRONT, LANES)),
        vmem((wide, cols + 2 * FRONT, LANES)),
        vmem((2, REACH, levels, cols)),
        vmem((2, REACH, levels, cols)),
        vmem((2, part, REACH, LANES)),
        vmem((2, part, REACH, LANES)),
        vmem((2, 2, REACH, REACH, LANES)),
        vmem((wide_c, cols_c + 2 * FRONT, LANES)),
        vmem((wide_c, cols_c + 2 * FRONT, LANES)),
        vmem((wide_c, cols_c + 2 * FRONT, LANES)),
        vmem((wide_c - 2, cols_c + 2 * EDGE, LANES)),
        vmem((wide_c - 2, cols_c + 2 * FRONT, LANES)),
        vmem((part_c, cols_c, LANES)),
        vmem((part_c, cols_c, LANES)),
        vmem((cols_c + 2 * FRONT, LANES)),
        vmem((cols, LANES)),
        vmem((part_c + 2, LANES, cols)),
        vmem((part, LANES, cols)),
    ] + [pltpu.SemaphoreType.DMA((11,))] * 2 + [pltpu.SemaphoreType.DMA((9,))] * 4
    scratch += [
        vmem((2, cols_c, LANES)),
        vmem((2, cols_c + 2 * FRONT, LANES)),
        vmem((2, COARSE_REACH * part_c, LANES)),
        vmem((2, COARSE_REACH * part_c, LANES)),
        vmem((2, 2, EDGE, LANES)),
        vmem((2, 2, EDGE, LANES)),
    ] * 2
    in_vmem = pl.BlockSpec(memory_space=pltpu.VMEM)
    ending = pl.pallas_call(
        functools.partial(kernel, sizes, levels, rows, cols),
        out_shape=pltpu.VMEM((levels * rows, cols), jnp.float32),
        in_specs=[pl.BlockSpec(memory_space=pl.ANY)] * 3,
        out_specs=in_vmem,
        scratch_shapes=scratch,
        compiler_params=pltpu.CompilerParams(collective_id=0, has_side_effects=True),
        name="parareal",
    )(state_starts.reshape(levels * rows, cols), diffusivity.reshape(1, levels), wind)
    return ending.reshape(1, levels, rows, cols)


def solution(mesh):
    sizes = tuple(mesh.shape[axis] for axis in ("tm", "gx", "gy"))
    placed = (P("tm", None, "gx", "gy"), P(), P())
    return jax.shard_map(
        functools.partial(shards, sizes),
        mesh=mesh, in_specs=placed, out_specs=P("tm", None, "gx", "gy"), check_vma=False,
    )
```

```python
import functools

import jax
import jax.numpy as jnp
from jax import lax
from jax.experimental import pallas as pl
from jax.experimental.pallas import tpu as pltpu
from jax.sharding import PartitionSpec as P

SUB = 4
REACH = SUB
RATIO = 4
LANES = 128
EDGE = 8
FRONT = 2 * EDGE
COARSE_REACH = 2
BLOCKS = 4

time_step = 0.2
weights_low = (0.375, 0.125, 0.0, 0.0)
weights_mid = (0.625, 0.875, 0.875, 0.625)
weights_high = (0.0, 0.0, 0.125, 0.375)
mean_side, mean_mid = 0.125, 0.75

PLANE = tuple((dx, dy) for dx in (-1, 0, 1) for dy in (-1, 0, 1))
AROUND = tuple(d for d in PLANE if d != (0, 0))


def conjunction(conditions):
    total = True
    for condition in conditions:
        total = condition if total is True else jnp.logical_and(total, condition)
    return total


def kernel(
    sizes, levels, rows, cols,
    x_hbm, diff_hbm, wind_hbm, turned, spread_rows,
    x_ref, diff_ref, wind_ref, load_sems, ready,
    first, second, x_send, x_recv, y_send, y_recv, corner_recv,
    old_wide, new_wide, extended, old_image, change,
    sent, fine_mean, line, fine_line,
    fine_out, fine_in, old_out, old_in, chain_out, chain_in, *strip_refs,
):
    n_tm, n_gx, n_gy = sizes
    tm, gx, gy = lax.axis_index("tm"), lax.axis_index("gx"), lax.axis_index("gy")
    packs = LANES // levels
    part = rows // packs
    part_c = part // RATIO
    cols_c = cols // RATIO
    wide = part + 2 * REACH
    wide_c = part_c + 2 * COARSE_REACH
    end = FRONT + cols
    end_c = FRONT + cols_c

    def there(dz, dx, dy):
        tests = []
        for place, move, count in ((tm, dz, n_tm), (gx, dx, n_gx), (gy, dy, n_gy)):
            if move < 0:
                tests.append(place > 0)
            if move > 0:
                tests.append(place < count - 1)
        return conjunction(tests)

    def guarded(condition, action):
        if condition is True:
            action()
        else:
            pl.when(condition)(action)

    def target(dz, dx, dy):
        return (tm + dz, gx + dx, gy + dy)

    loads = [
        pltpu.make_async_copy(source, landing, load_sems.at[k])
        for k, (source, landing) in enumerate(((x_hbm, x_ref), (diff_hbm, diff_ref), (wind_hbm, wind_ref)))
    ]
    for load in loads:
        load.start()

    barrier = pltpu.get_barrier_semaphore()
    partners = [(0, dx, dy) for dx, dy in AROUND] + [(-1, 0, 0), (1, 0, 0)]
    partners.sort(key=lambda move: -sum(map(abs, move)))
    awaited = jnp.int32(0)
    for move in partners:
        def greet(move=move):
            pl.semaphore_signal(barrier, inc=1, device_id=target(*move), device_id_type=pl.DeviceIdType.MESH)
        guarded(there(*move), greet)
        awaited = awaited + there(*move).astype(jnp.int32)

    def send_all(copies, dz, moves):
        for move in moves:
            guarded(there(dz, *move), lambda move=move: copies[move].start())

    def sends_done(copies, dz, moves):
        for move in moves:
            guarded(there(dz, *move), lambda move=move: copies[move].wait_send())

    def all_arrived(copies, dz, moves):
        for dx, dy in moves:
            guarded(there(-dz, -dx, -dy), lambda move=(dx, dy): copies[move].wait_recv())

    def remote(source, landing, out_sem, in_sem, move):
        return pltpu.make_async_remote_copy(
            src_ref=source, dst_ref=landing, send_sem=out_sem, recv_sem=in_sem,
            device_id=target(*move), device_id_type=pl.DeviceIdType.MESH,
        )

    def index_of(move):
        return (move[0] + 1) * 3 + move[1] + 1

    fine_copies = {}
    for move in AROUND:
        dx, dy = move
        k = index_of(move)
        if dy == 0:
            source, landing = (buffer.at[(dx + 1) // 2, pl.ds(0, REACH // 2)] for buffer in (x_send, x_recv))
        elif dx == 0:
            source, landing = y_send.at[(dy + 1) // 2], y_recv.at[(1 - dy) // 2]
        else:
            source = y_send.at[(dy + 1) // 2, pl.ds(0 if dx < 0 else part - REACH, REACH)]
            landing = corner_recv.at[(1 - dx) // 2, (1 - dy) // 2]
        fine_copies[move] = remote(source, landing, fine_out.at[k], fine_in.at[k], (0, dx, dy))
    later_copies = {}
    for dx in (-1, 1):
        k = 9 + (dx + 1) // 2
        source, landing = (buffer.at[(dx + 1) // 2, pl.ds(REACH // 2, REACH // 2)] for buffer in (x_send, x_recv))
        later_copies[dx, 0] = remote(source, landing, fine_out.at[k], fine_in.at[k], (0, dx, 0))

    def coarse_copies(main, wide_in, strips, out_sems, in_sems, dz):
        row_out, row_in, side_out, side_in, corner_out, corner_in = strips
        copies = {}
        for dx, dy in PLANE if dz else AROUND:
            k = index_of((dx, dy))
            towards_x, towards_y = (dx + 1) // 2, (dy + 1) // 2
            if dx == 0 and dy == 0:
                source, landing = main, wide_in.at[pl.ds(COARSE_REACH, part_c), pl.ds(FRONT, cols_c)]
            elif dy == 0:
                source, landing = row_out.at[towards_x], row_in.at[towards_x, pl.ds(FRONT, cols_c)]
            elif dx == 0:
                source, landing = side_out.at[towards_y], side_in.at[towards_y]
            else:
                source, landing = corner_out.at[towards_x, towards_y], corner_in.at[towards_x, towards_y]
            copies[dx, dy] = remote(source, landing, out_sems.at[k], in_sems.at[k], (dz, dx, dy))
        return copies

    old_strips, new_strips = strip_refs[:6], strip_refs[6:]
    old_copies = coarse_copies(None, old_wide, old_strips, old_out, old_in, 0)
    chain_copies = coarse_copies(sent, new_wide, new_strips, chain_out, chain_in, 1)

    lane = lax.broadcasted_iota(jnp.int32, (1, LANES), 1)
    pack = lane // levels

    def packed(row):
        return jnp.concatenate([row] * packs, axis=1)

    def advance(source, row, start, count, consts):
        keep, spread, along_x, along_y = consts
        centre = source[row, pl.ds(start, count), :]
        east = source[row + 1, pl.ds(start, count), :]
        west = source[row - 1, pl.ds(start, count), :]
        north = source[row, pl.ds(start + 1, count), :]
        south = source[row, pl.ds(start - 1, count), :]
        pushed = along_x * (east - west) + along_y * (north - south)
        return centre * (keep - pushed) + spread * ((east + west) + (north + south))

    def native_row(x):
        if x < 0:
            return x_recv[1, x + REACH]
        if x >= rows:
            return x_recv[0, x - rows]
        return x_ref[pl.ds(x, levels, stride=rows), :]

    def bring_in(row):
        stacked = jnp.concatenate([native_row(p * part + row - REACH) for p in range(packs)], axis=0)
        first[row, pl.ds(FRONT, cols), :] = stacked.T

    for load in loads:
        load.wait()
    diffuse = packed(diff_ref[...])
    east_wind = packed(wind_ref[0:1, :])
    north_wind = packed(wind_ref[1:2, :])

    def constants(factor):
        spread = (time_step * factor) * diffuse
        return 1.0 - 4.0 * spread, spread, (0.5 * time_step) * east_wind, (0.5 * time_step) * north_wind

    fine_constants = constants(1.0)
    coarse_constants = constants(0.25)

    for r in range(REACH):
        x_send[0, r] = native_row(r)
        x_send[1, r] = native_row(rows - REACH + r)
    x_moves = tuple(m for m in AROUND if m[1] == 0)
    y_moves = tuple(m for m in AROUND if m[1] != 0)
    low_lanes = lane < levels
    high_lanes = lane >= LANES - levels
    pl.semaphore_wait(barrier, awaited)

    @pl.when(tm > 0)
    def _():
        pl.semaphore_signal(ready, inc=1, device_id=target(-1, 0, 0), device_id_type=pl.DeviceIdType.MESH)

    side_moves = tuple(m for m in AROUND if m[0] == 0)
    corner_moves = tuple(m for m in y_moves if m[0] != 0)
    send_all(fine_copies, 0, x_moves)
    for row in range(REACH, REACH + part):
        bring_in(row)
    for row in range(part):
        y_send[0, row] = first[REACH + row, pl.ds(FRONT, REACH), :]
        y_send[1, row] = first[REACH + row, pl.ds(end - REACH, REACH), :]
    send_all(fine_copies, 0, side_moves + corner_moves)

    def restricted(source, row):
        total = source[REACH + row * RATIO, pl.ds(FRONT, cols), :]
        for r in range(1, RATIO):
            total = total + source[REACH + row * RATIO + r, pl.ds(FRONT, cols), :]
        fine_line[...] = total
        mean = fine_line[pl.ds(0, cols_c, stride=RATIO), :]
        for o in range(1, RATIO):
            mean = mean + fine_line[pl.ds(o, cols_c, stride=RATIO), :]
        return mean * (1.0 / RATIO**2)

    def swapped(value):
        return pltpu.roll(value, levels, 1)

    def pack_strips(row_of, strips):
        row_out, _, side_out, _, corner_out, _ = strips
        row_out[0] = jnp.where(low_lanes, row_of(0, 0, cols_c), swapped(row_of(1, 0, cols_c)))
        row_out[1] = jnp.where(low_lanes, swapped(row_of(part_c - 2, 0, cols_c)), row_of(part_c - 1, 0, cols_c))
        for side, col in ((0, 0), (1, cols_c - COARSE_REACH)):
            for row in range(part_c):
                side_out[side, pl.ds(COARSE_REACH * row, COARSE_REACH), :] = row_of(row, col, COARSE_REACH)
            for towards in range(2):
                corner_out[towards, side, pl.ds(0, COARSE_REACH), :] = row_out[towards, pl.ds(col, COARSE_REACH), :]

    def old_row(row, col, count):
        return old_wide[COARSE_REACH + row, pl.ds(FRONT + col, count), :]

    for row in range(part_c):
        old_wide[COARSE_REACH + row, pl.ds(FRONT, cols_c), :] = restricted(first, row)
    pack_strips(old_row, old_strips)
    send_all(old_copies, 0, AROUND)
    send_all(later_copies, 0, x_moves)

    def inside_x(row, reach, length):
        place = (gx * packs + pack) * length + (row - reach)
        return jnp.logical_and(place >= 0, place < n_gx * packs * length)

    def inside_y(start, count, length):
        place = gy * length + (start - FRONT) + lax.broadcasted_iota(jnp.int32, (count, LANES), 0)
        return jnp.logical_and(place >= 0, place < n_gy * length)

    edges = ((FRONT - EDGE, inside_y(FRONT - EDGE, EDGE, cols)), (end, inside_y(end, EDGE, cols)))
    reaches = ((FRONT - REACH, inside_y(FRONT - REACH, REACH, cols)), (end, inside_y(end, REACH, cols)))
    halo_rows = [*range(REACH), *range(REACH + part, wide)]
    half = cols // 2

    def update(source, dest, row, consts, last):
        for start, count in ((FRONT, half), (FRONT + half, cols - half)):
            dest[row, pl.ds(start, count), :] = advance(source, row, start, count, consts)
        if not last:
            for start, mask in edges:
                value = advance(source, row, start, EDGE, consts)
                dest[row, pl.ds(start, EDGE), :] = jnp.where(mask, value, 0.0)

    buffers = (first, second)

    all_arrived(fine_copies, 0, side_moves)
    for side, (start, mask) in enumerate(reaches):
        for row in range(part):
            first[REACH + row, pl.ds(start, REACH), :] = jnp.where(mask, y_recv[side, row], 0.0)
    for step in range(1, SUB + 1):
        def inner_row(row, step=step):
            update(buffers[(step - 1) % 2], buffers[step % 2], row, fine_constants, step == SUB)

        pl.loop(REACH + step, REACH + part - step, unroll=2)(inner_row)

    count_c = cols_c + 2 * EDGE
    begin_c = FRONT - EDGE
    mask_y = inside_y(begin_c, count_c, cols_c)

    def extend(buffer, strips):
        _, row_in, _, side_in, _, corner_in = strips
        for side, col in ((0, end_c), (1, FRONT - COARSE_REACH)):
            for row in range(part_c):
                buffer[COARSE_REACH + row, pl.ds(col, COARSE_REACH), :] = side_in[
                    side, pl.ds(COARSE_REACH * row, COARSE_REACH), :
                ]
            for towards in range(2):
                row_in[towards, pl.ds(col, COARSE_REACH), :] = corner_in[towards, side, pl.ds(0, COARSE_REACH), :]

        def own(row):
            return buffer[COARSE_REACH + row, pl.ds(begin_c, count_c), :]

        above, below = (row_in[towards, pl.ds(begin_c, count_c), :] for towards in (0, 1))
        values = [
            jnp.where(low_lanes, below, swapped(own(part_c - 2))),
            swapped(jnp.where(high_lanes, below, own(part_c - 1))),
            *[own(row) for row in range(part_c)],
            swapped(jnp.where(low_lanes, above, own(0))),
            jnp.where(high_lanes, above, swapped(own(1))),
        ]
        for row, value in enumerate(values):
            mask = mask_y
            if not COARSE_REACH <= row < COARSE_REACH + part_c:
                mask = jnp.logical_and(mask_y, inside_x(row, COARSE_REACH, part_c))
            extended[row, pl.ds(begin_c, count_c), :] = jnp.where(mask, value, 0.0)

    all_arrived(old_copies, 0, AROUND)
    sends_done(old_copies, 0, AROUND)
    extend(old_wide, old_strips)
    for row in range(1, wide_c - 1):
        old_image[row - 1] = advance(extended, row, begin_c, count_c, coarse_constants)


    def compute_change():
        for row in range(1, wide_c - 1):
            moved = advance(extended, row, begin_c, count_c, coarse_constants) - old_image[row - 1]
            mask = jnp.logical_and(mask_y, inside_x(row, COARSE_REACH, part_c))
            change[row - 1, pl.ds(begin_c, count_c), :] = jnp.where(mask, moved, 0.0)

    def change_row(row):
        return change[row, pl.ds(begin_c, count_c), :]

    def smoothed(row):
        line[pl.ds(begin_c, count_c), :] = (
            mean_side * (change_row(row) + change_row(row + 2)) + mean_mid * change_row(row + 1)
        )
        sides = line[pl.ds(FRONT - 1, cols_c), :] + line[pl.ds(FRONT + 1, cols_c), :]
        return mean_side * sides + mean_mid * line[pl.ds(FRONT, cols_c), :]

    @pl.when(tm == 0)
    def _():
        compute_change()
        for row in range(part_c):
            sent[row] = smoothed(row)

    all_arrived(fine_copies, 0, x_moves)
    all_arrived(later_copies, 0, x_moves)
    for row in halo_rows:
        bring_in(row)
        inner = first[row, pl.ds(FRONT, cols), :]
        first[row, pl.ds(FRONT, cols), :] = jnp.where(inside_x(row, REACH, part), inner, 0.0)
    all_arrived(fine_copies, 0, corner_moves)
    for side, (start, mask_side) in enumerate(reaches):
        for row in halo_rows:
            if row < REACH:
                here = jnp.where(high_lanes, corner_recv[0, side, row], y_recv[side, row + part - REACH])
                here = pltpu.roll(here, levels, 1)
            else:
                here = jnp.where(low_lanes, corner_recv[1, side, row - part - REACH], y_recv[side, row - part - REACH])
                here = pltpu.roll(here, LANES - levels, 1)
            mask = jnp.logical_and(mask_side, inside_x(row, REACH, part))
            first[row, pl.ds(start, REACH), :] = jnp.where(mask, here, 0.0)
    for step in range(1, SUB + 1):
        def outer_row(row, step=step):
            for shifted in (row, row + part + REACH - 2 * step):
                mask_x = inside_x(shifted, REACH, part)
                consts = tuple(jnp.where(mask_x, c, 0.0) for c in fine_constants)
                update(buffers[(step - 1) % 2], buffers[step % 2], shifted, consts, step == SUB)

        pl.loop(step, REACH + step)(outer_row)
    fine = buffers[SUB % 2]

    for row in range(part_c):
        fine_mean[row] = restricted(fine, row)

    def write_fine():
        for row in range(part):
            turned[row] = fine[REACH + row, pl.ds(FRONT, cols), :].T

    def pass_on():
        pl.semaphore_wait(ready, 1)
        pack_strips(lambda row, col, count: sent[row, pl.ds(col, count), :], new_strips)
        send_all(chain_copies, 1, AROUND)
        send_all(chain_copies, 1, ((0, 0),))

    @pl.when(jnp.logical_and(tm == 0, tm < n_tm - 1))
    def _():
        for row in range(part_c):
            sent[row] = fine_mean[row] + sent[row]
        pass_on()

    write_fine()

    @pl.when(tm > 0)
    def _():
        all_arrived(chain_copies, 1, PLANE)
        extend(new_wide, new_strips)
        compute_change()

    @pl.when(jnp.logical_and(tm > 0, tm < n_tm - 1))
    def _():
        for row in range(part_c):
            sent[row] = fine_mean[row] + smoothed(row)
        pass_on()

    coarse_col = lax.broadcasted_iota(jnp.int32, (count_c, cols), 0) - EDGE
    fine_col = lax.broadcasted_iota(jnp.int32, (count_c, cols), 1)
    offset_of = fine_col & (RATIO - 1)
    apart = coarse_col - (fine_col >> (RATIO.bit_length() - 1))
    spreading = jnp.zeros((count_c, cols), jnp.float32)
    for o in range(RATIO):
        for distance, weights in ((-1, weights_low), (0, weights_mid), (1, weights_high)):
            chosen = jnp.logical_and(offset_of == o, apart == distance)
            spreading = jnp.where(chosen, weights[o], spreading)
    spreading = jnp.concatenate([spreading.astype(jnp.bfloat16)] * 3, axis=0)
    for row in range(part_c + 2):
        rest, pieces = change_row(row), []
        for _ in range(3):
            piece = rest.astype(jnp.bfloat16).astype(jnp.float32)
            pieces.append(piece)
            rest = rest - piece
        split = jnp.concatenate(pieces, axis=0).T.astype(jnp.bfloat16)
        spread_rows[row] = jnp.dot(split, spreading, preferred_element_type=jnp.float32)

    sends_done(fine_copies, 0, AROUND)
    sends_done(later_copies, 0, x_moves)
    pl.when(tm < n_tm - 1)(lambda: sends_done(chain_copies, 1, PLANE))


def closing(levels, rows, turned, spread_rows, out_hbm, filled, sems):
    packs = LANES // levels
    part = rows // packs
    blocks = filled.shape[0]
    block = levels // blocks
    copies = []
    for k in range(blocks):
        for row in range(part):
            at, o = row // RATIO, row % RATIO
            for p in range(packs):
                here = pl.ds(p * levels + k * block, block)
                total = turned[row, here, :] + weights_mid[o] * spread_rows[at + 1, here, :]
                if weights_low[o]:
                    total = total + weights_low[o] * spread_rows[at, here, :]
                if weights_high[o]:
                    total = total + weights_high[o] * spread_rows[at + 2, here, :]
                filled[k, pl.ds(p * part + row, block, stride=rows), :] = total
        copy = pltpu.make_async_copy(filled.at[k], out_hbm.at[pl.ds(k * block * rows, block * rows)], sems.at[k])
        copy.start()
        copies.append(copy)
    for copy in copies:
        copy.wait()


def shards(sizes, state_starts, diffusivity, wind):
    _, levels, rows, cols = state_starts.shape
    packs = LANES // levels
    if packs != 2 or levels * packs != LANES:
        raise ValueError(levels)
    part = rows // packs
    part_c = part // RATIO
    cols_c = cols // RATIO
    wide, wide_c = part + 2 * REACH, part_c + 2 * COARSE_REACH
    vmem = functools.partial(pltpu.VMEM, dtype=jnp.float32)
    scratch = [
        vmem((levels * rows, cols)),
        vmem((1, levels)),
        vmem((2, levels)),
        pltpu.SemaphoreType.DMA((3,)),
        pltpu.SemaphoreType.REGULAR,
        vmem((wide, cols + 2 * FRONT, LANES)),
        vmem((wide, cols + 2 * FRONT, LANES)),
        vmem((2, REACH, levels, cols)),
        vmem((2, REACH, levels, cols)),
        vmem((2, part, REACH, LANES)),
        vmem((2, part, REACH, LANES)),
        vmem((2, 2, REACH, REACH, LANES)),
        vmem((wide_c, cols_c + 2 * FRONT, LANES)),
        vmem((wide_c, cols_c + 2 * FRONT, LANES)),
        vmem((wide_c, cols_c + 2 * FRONT, LANES)),
        vmem((wide_c - 2, cols_c + 2 * EDGE, LANES)),
        vmem((wide_c - 2, cols_c + 2 * FRONT, LANES)),
        vmem((part_c, cols_c, LANES)),
        vmem((part_c, cols_c, LANES)),
        vmem((cols_c + 2 * FRONT, LANES)),
        vmem((cols, LANES)),
    ] + [pltpu.SemaphoreType.DMA((11,))] * 2 + [pltpu.SemaphoreType.DMA((9,))] * 4
    scratch += [
        vmem((2, cols_c, LANES)),
        vmem((2, cols_c + 2 * FRONT, LANES)),
        vmem((2, COARSE_REACH * part_c, LANES)),
        vmem((2, COARSE_REACH * part_c, LANES)),
        vmem((2, 2, EDGE, LANES)),
        vmem((2, 2, EDGE, LANES)),
    ] * 2
    in_vmem = pl.BlockSpec(memory_space=pltpu.VMEM)
    turned, spread_rows = pl.pallas_call(
        functools.partial(kernel, sizes, levels, rows, cols),
        out_shape=(vmem((part, LANES, cols)), vmem((part_c + 2, LANES, cols))),
        in_specs=[pl.BlockSpec(memory_space=pl.ANY)] * 3,
        out_specs=(in_vmem, in_vmem),
        scratch_shapes=scratch,
        compiler_params=pltpu.CompilerParams(collective_id=0, has_side_effects=True),
        name="parareal",
    )(state_starts.reshape(levels * rows, cols), diffusivity.reshape(1, levels), wind)
    ending = pl.pallas_call(
        functools.partial(closing, levels, rows),
        out_shape=jax.ShapeDtypeStruct((levels * rows, cols), jnp.float32),
        in_specs=[in_vmem, in_vmem],
        out_specs=pl.BlockSpec(memory_space=pl.ANY),
        scratch_shapes=[
            vmem((BLOCKS, levels // BLOCKS * rows, cols)),
            pltpu.SemaphoreType.DMA((BLOCKS,)),
        ],
        name="closing",
    )(*(pltpu.with_memory_space_constraint(array, pltpu.VMEM) for array in (turned, spread_rows)))
    return ending.reshape(1, levels, rows, cols)


def solution(mesh):
    sizes = tuple(mesh.shape[axis] for axis in ("tm", "gx", "gy"))
    placed = (P("tm", None, "gx", "gy"), P(), P())
    return jax.shard_map(
        functools.partial(shards, sizes),
        mesh=mesh, in_specs=placed, out_specs=P("tm", None, "gx", "gy"), check_vma=False,
    )
```

```python
import functools

import jax
import jax.numpy as jnp
from jax import lax
from jax.experimental import pallas as pl
from jax.experimental.pallas import tpu as pltpu
from jax.sharding import PartitionSpec as P

SUB = 4
REACH = SUB
RATIO = 4
LANES = 128
EDGE = 8
FRONT = 2 * EDGE
COARSE_REACH = 2

time_step = 0.2
weights_low = (0.375, 0.125, 0.0, 0.0)
weights_mid = (0.625, 0.875, 0.875, 0.625)
weights_high = (0.0, 0.0, 0.125, 0.375)
mean_side, mean_mid = 0.125, 0.75

PLANE = tuple((dx, dy) for dx in (-1, 0, 1) for dy in (-1, 0, 1))
AROUND = tuple(d for d in PLANE if d != (0, 0))


def conjunction(conditions):
    total = True
    for condition in conditions:
        total = condition if total is True else jnp.logical_and(total, condition)
    return total


def kernel(
    sizes, levels, rows, cols,
    x_hbm, diff_hbm, wind_hbm, turned, change,
    x_ref, diff_ref, wind_ref, load_sems, small_sems, ready,
    first, second, x_recv, y_send, y_recv, corner_recv,
    old_wide, new_wide, extended, old_image,
    sent, fine_mean, line, fine_line,
    x_out, x_in, fine_out, fine_in, old_out, old_in, chain_out, chain_in, *strip_refs,
):
    n_tm, n_gx, n_gy = sizes
    tm, gx, gy = lax.axis_index("tm"), lax.axis_index("gx"), lax.axis_index("gy")
    packs = LANES // levels
    part = rows // packs
    part_c = part // RATIO
    cols_c = cols // RATIO
    wide = part + 2 * REACH
    wide_c = part_c + 2 * COARSE_REACH
    end = FRONT + cols
    end_c = FRONT + cols_c

    def there(dz, dx, dy):
        tests = []
        for place, move, count in ((tm, dz, n_tm), (gx, dx, n_gx), (gy, dy, n_gy)):
            if move < 0:
                tests.append(place > 0)
            if move > 0:
                tests.append(place < count - 1)
        return conjunction(tests)

    def guarded(condition, action):
        if condition is True:
            action()
        else:
            pl.when(condition)(action)

    def target(dz, dx, dy):
        return (tm + dz, gx + dx, gy + dy)

    small_loads = [
        pltpu.make_async_copy(source, landing, small_sems.at[k])
        for k, (source, landing) in enumerate(((diff_hbm, diff_ref), (wind_hbm, wind_ref)))
    ]
    loads = {x: pltpu.make_async_copy(x_hbm.at[:, x], x_ref.at[x], load_sems.at[x]) for x in range(rows)}
    by_row = [p * part + row for row in range(part) for p in range(packs)]
    for x in by_row:
        loads[x].start()
    for load in small_loads:
        load.start()

    barrier = pltpu.get_barrier_semaphore()
    partners = [(0, dx, dy) for dx, dy in AROUND] + [(-1, 0, 0), (1, 0, 0)]
    partners.sort(key=lambda move: -sum(map(abs, move)))
    awaited = jnp.int32(0)
    for move in partners:
        def greet(move=move):
            pl.semaphore_signal(barrier, inc=1, device_id=target(*move), device_id_type=pl.DeviceIdType.MESH)
        guarded(there(*move), greet)
        awaited = awaited + there(*move).astype(jnp.int32)

    def send_all(copies, dz, moves):
        for move in moves:
            guarded(there(dz, *move), lambda move=move: copies[move].start())

    def sends_done(copies, dz, moves):
        for move in moves:
            guarded(there(dz, *move), lambda move=move: copies[move].wait_send())

    def all_arrived(copies, dz, moves):
        for dx, dy in moves:
            guarded(there(-dz, -dx, -dy), lambda move=(dx, dy): copies[move].wait_recv())

    def remote(source, landing, out_sem, in_sem, move):
        return pltpu.make_async_remote_copy(
            src_ref=source, dst_ref=landing, send_sem=out_sem, recv_sem=in_sem,
            device_id=target(*move), device_id_type=pl.DeviceIdType.MESH,
        )

    def index_of(move):
        return (move[0] + 1) * 3 + move[1] + 1

    fine_copies = {}
    for move in AROUND:
        dx, dy = move
        k = index_of(move)
        if dy == 0:
            continue
        if dx == 0:
            source, landing = y_send.at[(dy + 1) // 2], y_recv.at[(1 - dy) // 2]
        else:
            source = y_send.at[(dy + 1) // 2, pl.ds(0 if dx < 0 else part - REACH, REACH)]
            landing = corner_recv.at[(1 - dx) // 2, (1 - dy) // 2]
        fine_copies[move] = remote(source, landing, fine_out.at[k], fine_in.at[k], (0, dx, dy))
    x_copies = []
    for r in range(REACH):
        copies = {}
        for dx in (-1, 1):
            towards = (dx + 1) // 2
            k = towards * REACH + r
            source = x_hbm.at[:, r if dx < 0 else rows - REACH + r]
            copies[dx, 0] = remote(source, x_recv.at[towards, r], x_out.at[k], x_in.at[k], (0, dx, 0))
        x_copies.append(copies)

    def coarse_copies(main, wide_in, strips, out_sems, in_sems, dz):
        row_out, row_in, side_out, side_in, corner_out, corner_in = strips
        copies = {}
        for dx, dy in PLANE if dz else AROUND:
            k = index_of((dx, dy))
            towards_x, towards_y = (dx + 1) // 2, (dy + 1) // 2
            if dx == 0 and dy == 0:
                source, landing = main, wide_in.at[pl.ds(COARSE_REACH, part_c), pl.ds(FRONT, cols_c)]
            elif dy == 0:
                source, landing = row_out.at[towards_x], row_in.at[towards_x, pl.ds(FRONT, cols_c)]
            elif dx == 0:
                source, landing = side_out.at[towards_y], side_in.at[towards_y]
            else:
                source, landing = corner_out.at[towards_x, towards_y], corner_in.at[towards_x, towards_y]
            copies[dx, dy] = remote(source, landing, out_sems.at[k], in_sems.at[k], (dz, dx, dy))
        return copies

    old_strips, new_strips = strip_refs[:6], strip_refs[6:]
    old_copies = coarse_copies(None, old_wide, old_strips, old_out, old_in, 0)
    chain_copies = coarse_copies(sent, new_wide, new_strips, chain_out, chain_in, 1)

    lane = lax.broadcasted_iota(jnp.int32, (1, LANES), 1)
    pack = lane // levels

    def packed(row):
        return jnp.concatenate([row] * packs, axis=1)

    def advance(source, row, start, count, consts):
        keep, spread, along_x, along_y = consts
        centre = source[row, pl.ds(start, count), :]
        east = source[row + 1, pl.ds(start, count), :]
        west = source[row - 1, pl.ds(start, count), :]
        north = source[row, pl.ds(start + 1, count), :]
        south = source[row, pl.ds(start - 1, count), :]
        pushed = along_x * (east - west) + along_y * (north - south)
        return centre * (keep - pushed) + spread * ((east + west) + (north + south))

    def native_row(x):
        if x < 0:
            return x_recv[1, x + REACH]
        if x >= rows:
            return x_recv[0, x - rows]
        return x_ref[x]

    def bring_in(row):
        stacked = jnp.concatenate([native_row(p * part + row - REACH) for p in range(packs)], axis=0)
        first[row, pl.ds(FRONT, cols), :] = stacked.T

    x_moves = tuple(m for m in AROUND if m[1] == 0)
    y_moves = tuple(m for m in AROUND if m[1] != 0)
    low_lanes = lane < levels
    high_lanes = lane >= LANES - levels
    pl.semaphore_wait(barrier, awaited)

    @pl.when(tm > 0)
    def _():
        pl.semaphore_signal(ready, inc=1, device_id=target(-1, 0, 0), device_id_type=pl.DeviceIdType.MESH)

    side_moves = tuple(m for m in AROUND if m[0] == 0)
    corner_moves = tuple(m for m in y_moves if m[0] != 0)
    for copies in x_copies[: REACH // 2]:
        send_all(copies, 0, x_moves)
    for load in small_loads:
        load.wait()
    diffuse = packed(diff_ref[...])
    east_wind = packed(wind_ref[0:1, :])
    north_wind = packed(wind_ref[1:2, :])

    def constants(factor):
        spread = (time_step * factor) * diffuse
        return 1.0 - 4.0 * spread, spread, (0.5 * time_step) * east_wind, (0.5 * time_step) * north_wind

    fine_constants = constants(1.0)
    coarse_constants = constants(0.25)

    for row in range(REACH, REACH + part):
        for p in range(packs):
            loads[p * part + row - REACH].wait()
        bring_in(row)
    for row in range(part):
        y_send[0, row] = first[REACH + row, pl.ds(FRONT, REACH), :]
        y_send[1, row] = first[REACH + row, pl.ds(end - REACH, REACH), :]
    send_all(fine_copies, 0, side_moves + corner_moves)

    def restricted(source, row):
        total = source[REACH + row * RATIO, pl.ds(FRONT, cols), :]
        for r in range(1, RATIO):
            total = total + source[REACH + row * RATIO + r, pl.ds(FRONT, cols), :]
        fine_line[...] = total
        mean = fine_line[pl.ds(0, cols_c, stride=RATIO), :]
        for o in range(1, RATIO):
            mean = mean + fine_line[pl.ds(o, cols_c, stride=RATIO), :]
        return mean * (1.0 / RATIO**2)

    def swapped(value):
        return pltpu.roll(value, levels, 1)

    def pack_strips(row_of, strips):
        row_out, _, side_out, _, corner_out, _ = strips
        row_out[0] = jnp.where(low_lanes, row_of(0, 0, cols_c), swapped(row_of(1, 0, cols_c)))
        row_out[1] = jnp.where(low_lanes, swapped(row_of(part_c - 2, 0, cols_c)), row_of(part_c - 1, 0, cols_c))
        for side, col in ((0, 0), (1, cols_c - COARSE_REACH)):
            for row in range(part_c):
                side_out[side, pl.ds(COARSE_REACH * row, COARSE_REACH), :] = row_of(row, col, COARSE_REACH)
            for towards in range(2):
                corner_out[towards, side, pl.ds(0, COARSE_REACH), :] = row_out[towards, pl.ds(col, COARSE_REACH), :]

    def old_row(row, col, count):
        return old_wide[COARSE_REACH + row, pl.ds(FRONT + col, count), :]

    for row in range(part_c):
        old_wide[COARSE_REACH + row, pl.ds(FRONT, cols_c), :] = restricted(first, row)
    pack_strips(old_row, old_strips)
    send_all(old_copies, 0, AROUND)
    for copies in x_copies[REACH // 2 :]:
        send_all(copies, 0, x_moves)

    def inside_x(row, reach, length):
        place = (gx * packs + pack) * length + (row - reach)
        return jnp.logical_and(place >= 0, place < n_gx * packs * length)

    def inside_y(start, count, length):
        place = gy * length + (start - FRONT) + lax.broadcasted_iota(jnp.int32, (count, LANES), 0)
        return jnp.logical_and(place >= 0, place < n_gy * length)

    edges = ((FRONT - EDGE, inside_y(FRONT - EDGE, EDGE, cols)), (end, inside_y(end, EDGE, cols)))
    reaches = ((FRONT - REACH, inside_y(FRONT - REACH, REACH, cols)), (end, inside_y(end, REACH, cols)))
    halo_rows = [*range(REACH), *range(REACH + part, wide)]
    half = cols // 2

    def update(source, dest, row, consts, last):
        for start, count in ((FRONT, half), (FRONT + half, cols - half)):
            dest[row, pl.ds(start, count), :] = advance(source, row, start, count, consts)
        if not last:
            for start, mask in edges:
                value = advance(source, row, start, EDGE, consts)
                dest[row, pl.ds(start, EDGE), :] = jnp.where(mask, value, 0.0)

    buffers = (first, second)

    all_arrived(fine_copies, 0, side_moves)
    for side, (start, mask) in enumerate(reaches):
        for row in range(part):
            first[REACH + row, pl.ds(start, REACH), :] = jnp.where(mask, y_recv[side, row], 0.0)
    for step in range(1, SUB + 1):
        def inner_row(row, step=step):
            update(buffers[(step - 1) % 2], buffers[step % 2], row, fine_constants, step == SUB)

        pl.loop(REACH + step, REACH + part - step, unroll=2)(inner_row)

    count_c = cols_c + 2 * EDGE
    begin_c = FRONT - EDGE
    mask_y = inside_y(begin_c, count_c, cols_c)

    def extend(buffer, strips):
        _, row_in, _, side_in, _, corner_in = strips
        for side, col in ((0, end_c), (1, FRONT - COARSE_REACH)):
            for row in range(part_c):
                buffer[COARSE_REACH + row, pl.ds(col, COARSE_REACH), :] = side_in[
                    side, pl.ds(COARSE_REACH * row, COARSE_REACH), :
                ]
            for towards in range(2):
                row_in[towards, pl.ds(col, COARSE_REACH), :] = corner_in[towards, side, pl.ds(0, COARSE_REACH), :]

        def own(row):
            return buffer[COARSE_REACH + row, pl.ds(begin_c, count_c), :]

        above, below = (row_in[towards, pl.ds(begin_c, count_c), :] for towards in (0, 1))
        values = [
            jnp.where(low_lanes, below, swapped(own(part_c - 2))),
            swapped(jnp.where(high_lanes, below, own(part_c - 1))),
            *[own(row) for row in range(part_c)],
            swapped(jnp.where(low_lanes, above, own(0))),
            jnp.where(high_lanes, above, swapped(own(1))),
        ]
        for row, value in enumerate(values):
            mask = mask_y
            if not COARSE_REACH <= row < COARSE_REACH + part_c:
                mask = jnp.logical_and(mask_y, inside_x(row, COARSE_REACH, part_c))
            extended[row, pl.ds(begin_c, count_c), :] = jnp.where(mask, value, 0.0)

    all_arrived(old_copies, 0, AROUND)
    sends_done(old_copies, 0, AROUND)
    extend(old_wide, old_strips)
    for row in range(1, wide_c - 1):
        old_image[row - 1] = advance(extended, row, begin_c, count_c, coarse_constants)


    def compute_change():
        for row in range(1, wide_c - 1):
            moved = advance(extended, row, begin_c, count_c, coarse_constants) - old_image[row - 1]
            mask = jnp.logical_and(mask_y, inside_x(row, COARSE_REACH, part_c))
            change[row - 1, pl.ds(begin_c, count_c), :] = jnp.where(mask, moved, 0.0)

    def change_row(row):
        return change[row, pl.ds(begin_c, count_c), :]

    def smoothed(row):
        line[pl.ds(begin_c, count_c), :] = (
            mean_side * (change_row(row) + change_row(row + 2)) + mean_mid * change_row(row + 1)
        )
        sides = line[pl.ds(FRONT - 1, cols_c), :] + line[pl.ds(FRONT + 1, cols_c), :]
        return mean_side * sides + mean_mid * line[pl.ds(FRONT, cols_c), :]

    @pl.when(tm == 0)
    def _():
        compute_change()
        for row in range(part_c):
            sent[row] = smoothed(row)

    for copies in x_copies:
        all_arrived(copies, 0, x_moves)
    for row in halo_rows:
        bring_in(row)
        inner = first[row, pl.ds(FRONT, cols), :]
        first[row, pl.ds(FRONT, cols), :] = jnp.where(inside_x(row, REACH, part), inner, 0.0)
    all_arrived(fine_copies, 0, corner_moves)
    for side, (start, mask_side) in enumerate(reaches):
        for row in halo_rows:
            if row < REACH:
                here = jnp.where(high_lanes, corner_recv[0, side, row], y_recv[side, row + part - REACH])
                here = pltpu.roll(here, levels, 1)
            else:
                here = jnp.where(low_lanes, corner_recv[1, side, row - part - REACH], y_recv[side, row - part - REACH])
                here = pltpu.roll(here, LANES - levels, 1)
            mask = jnp.logical_and(mask_side, inside_x(row, REACH, part))
            first[row, pl.ds(start, REACH), :] = jnp.where(mask, here, 0.0)
    for step in range(1, SUB + 1):
        def outer_row(row, step=step):
            for shifted in (row, row + part + REACH - 2 * step):
                mask_x = inside_x(shifted, REACH, part)
                consts = tuple(jnp.where(mask_x, c, 0.0) for c in fine_constants)
                update(buffers[(step - 1) % 2], buffers[step % 2], shifted, consts, step == SUB)

        pl.loop(step, REACH + step)(outer_row)
    fine = buffers[SUB % 2]

    for row in range(part_c):
        fine_mean[row] = restricted(fine, row)

    def write_fine():
        for row in range(part):
            turned[row] = fine[REACH + row, pl.ds(FRONT, cols), :].T

    def pass_on():
        pl.semaphore_wait(ready, 1)
        pack_strips(lambda row, col, count: sent[row, pl.ds(col, count), :], new_strips)
        send_all(chain_copies, 1, AROUND)
        send_all(chain_copies, 1, ((0, 0),))

    @pl.when(jnp.logical_and(tm == 0, tm < n_tm - 1))
    def _():
        for row in range(part_c):
            sent[row] = fine_mean[row] + sent[row]
        pass_on()

    write_fine()

    @pl.when(tm > 0)
    def _():
        all_arrived(chain_copies, 1, PLANE)
        extend(new_wide, new_strips)
        compute_change()

    @pl.when(jnp.logical_and(tm > 0, tm < n_tm - 1))
    def _():
        for row in range(part_c):
            sent[row] = fine_mean[row] + smoothed(row)
        pass_on()

    sends_done(fine_copies, 0, y_moves)
    for copies in x_copies:
        sends_done(copies, 0, x_moves)
    pl.when(tm < n_tm - 1)(lambda: sends_done(chain_copies, 1, PLANE))


def closing(levels, rows, turned, change, out_hbm, filled, spread_rows, sems):
    packs = LANES // levels
    part, _, cols = turned.shape
    part_c = part // RATIO
    count_c = cols // RATIO + 2 * EDGE
    coarse_col = lax.broadcasted_iota(jnp.int32, (count_c, cols), 0) - EDGE
    fine_col = lax.broadcasted_iota(jnp.int32, (count_c, cols), 1)
    offset_of = fine_col & (RATIO - 1)
    apart = coarse_col - (fine_col >> (RATIO.bit_length() - 1))
    spreading = jnp.zeros((count_c, cols), jnp.float32)
    for o in range(RATIO):
        for distance, weights in ((-1, weights_low), (0, weights_mid), (1, weights_high)):
            chosen = jnp.logical_and(offset_of == o, apart == distance)
            spreading = jnp.where(chosen, weights[o], spreading)
    spreading = jnp.concatenate([spreading.astype(jnp.bfloat16)] * 3, axis=0)
    def spread_row(row):
        rest, pieces = change[row, pl.ds(FRONT - EDGE, count_c), :], []
        for _ in range(3):
            piece = rest.astype(jnp.bfloat16).astype(jnp.float32)
            pieces.append(piece)
            rest = rest - piece
        split = jnp.concatenate(pieces, axis=0).T.astype(jnp.bfloat16)
        return jnp.dot(split, spreading, preferred_element_type=jnp.float32)

    for row in range(2):
        spread_rows[row] = spread_row(row)
    copies = []
    for row in range(part):
        at, o = row // RATIO, row % RATIO
        if o == 0:
            spread_rows[at + 2] = spread_row(at + 2)
        total = turned[row] + weights_mid[o] * spread_rows[at + 1]
        if weights_low[o]:
            total = total + weights_low[o] * spread_rows[at]
        if weights_high[o]:
            total = total + weights_high[o] * spread_rows[at + 2]
        filled[row] = total
        for p in range(packs):
            x = p * part + row
            copy = pltpu.make_async_copy(filled.at[row, pl.ds(p * levels, levels)], out_hbm.at[:, x], sems.at[x])
            copy.start()
            copies.append(copy)
    for copy in copies:
        copy.wait()


def shards(sizes, state_starts, diffusivity, wind):
    _, levels, rows, cols = state_starts.shape
    packs = LANES // levels
    if packs != 2 or levels * packs != LANES:
        raise ValueError(levels)
    part = rows // packs
    part_c = part // RATIO
    cols_c = cols // RATIO
    wide, wide_c = part + 2 * REACH, part_c + 2 * COARSE_REACH
    vmem = functools.partial(pltpu.VMEM, dtype=jnp.float32)
    scratch = [
        vmem((rows, levels, cols)),
        vmem((1, levels)),
        vmem((2, levels)),
        pltpu.SemaphoreType.DMA((rows,)),
        pltpu.SemaphoreType.DMA((2,)),
        pltpu.SemaphoreType.REGULAR,
        vmem((wide, cols + 2 * FRONT, LANES)),
        vmem((wide, cols + 2 * FRONT, LANES)),
        vmem((2, REACH, levels, cols)),
        vmem((2, part, REACH, LANES)),
        vmem((2, part, REACH, LANES)),
        vmem((2, 2, REACH, REACH, LANES)),
        vmem((wide_c, cols_c + 2 * FRONT, LANES)),
        vmem((wide_c, cols_c + 2 * FRONT, LANES)),
        vmem((wide_c, cols_c + 2 * FRONT, LANES)),
        vmem((wide_c - 2, cols_c + 2 * EDGE, LANES)),
        vmem((part_c, cols_c, LANES)),
        vmem((part_c, cols_c, LANES)),
        vmem((cols_c + 2 * FRONT, LANES)),
        vmem((cols, LANES)),
    ] + [pltpu.SemaphoreType.DMA((2 * REACH,))] * 2 + [pltpu.SemaphoreType.DMA((9,))] * 6
    scratch += [
        vmem((2, cols_c, LANES)),
        vmem((2, cols_c + 2 * FRONT, LANES)),
        vmem((2, COARSE_REACH * part_c, LANES)),
        vmem((2, COARSE_REACH * part_c, LANES)),
        vmem((2, 2, EDGE, LANES)),
        vmem((2, 2, EDGE, LANES)),
    ] * 2
    in_vmem = pl.BlockSpec(memory_space=pltpu.VMEM)
    handed = pl.pallas_call(
        functools.partial(kernel, sizes, levels, rows, cols),
        out_shape=(vmem((part, LANES, cols)), vmem((part_c + 2, cols_c + 2 * FRONT, LANES))),
        in_specs=[pl.BlockSpec(memory_space=pl.ANY)] * 3,
        out_specs=(in_vmem, in_vmem),
        scratch_shapes=scratch,
        compiler_params=pltpu.CompilerParams(collective_id=0, has_side_effects=True),
        name="parareal",
    )(state_starts.reshape(levels, rows, cols), diffusivity.reshape(1, levels), wind)
    ending = pl.pallas_call(
        functools.partial(closing, levels, rows),
        out_shape=jax.ShapeDtypeStruct((levels, rows, cols), jnp.float32),
        in_specs=[in_vmem, in_vmem],
        out_specs=pl.BlockSpec(memory_space=pl.ANY),
        scratch_shapes=[
            vmem((part, LANES, cols)),
            vmem((part_c + 2, LANES, cols)),
            pltpu.SemaphoreType.DMA((rows,)),
        ],
        name="closing",
    )(*(pltpu.with_memory_space_constraint(array, pltpu.VMEM) for array in handed))
    return ending.reshape(1, levels, rows, cols)


def solution(mesh):
    sizes = tuple(mesh.shape[axis] for axis in ("tm", "gx", "gy"))
    placed = (P("tm", None, "gx", "gy"), P(), P())
    return jax.shard_map(
        functools.partial(shards, sizes),
        mesh=mesh, in_specs=placed, out_specs=P("tm", None, "gx", "gy"), check_vma=False,
    )
```

```python
import functools

import jax
import jax.numpy as jnp
from jax import lax
from jax.experimental import pallas as pl
from jax.experimental.pallas import tpu as pltpu
from jax.sharding import PartitionSpec as P

SUB = 4
REACH = SUB
RATIO = 4
LANES = 128
EDGE = 8
FRONT = 2 * EDGE
COARSE_REACH = 2

time_step = 0.2
weights_low = (0.375, 0.125, 0.0, 0.0)
weights_mid = (0.625, 0.875, 0.875, 0.625)
weights_high = (0.0, 0.0, 0.125, 0.375)
mean_side, mean_mid = 0.125, 0.75

PLANE = tuple((dx, dy) for dx in (-1, 0, 1) for dy in (-1, 0, 1))
AROUND = tuple(d for d in PLANE if d != (0, 0))
x_moves = tuple(d for d in AROUND if d[1] == 0)
y_moves = tuple(d for d in AROUND if d[1] != 0)
side_moves = tuple(d for d in y_moves if d[0] == 0)
corner_moves = tuple(d for d in y_moves if d[0] != 0)


def conjunction(conditions):
    total = True
    for condition in conditions:
        total = condition if total is True else jnp.logical_and(total, condition)
    return total


def kernel(
    sizes, levels, rows, cols,
    x_hbm, diff_hbm, wind_hbm, turned, change,
    x_ref, small_ref, load_sem, small_sem, ready,
    first, second, x_recv, y_send, y_recv, corner_recv,
    old_wide, new_wide, extended, old_image,
    sent, fine_mean, line, fine_line,
    out_sem, x_in, fine_in, old_in, chain_in, *strip_refs,
):
    n_tm, n_gx, n_gy = sizes
    tm, gx, gy = lax.axis_index("tm"), lax.axis_index("gx"), lax.axis_index("gy")
    packs = LANES // levels
    part = rows // packs
    part_c = part // RATIO
    cols_c = cols // RATIO
    wide = part + 2 * REACH
    wide_c = part_c + 2 * COARSE_REACH
    end = FRONT + cols
    end_c = FRONT + cols_c

    def there(dz, dx, dy):
        tests = []
        for place, move, count in ((tm, dz, n_tm), (gx, dx, n_gx), (gy, dy, n_gy)):
            if move < 0:
                tests.append(place > 0)
            if move > 0:
                tests.append(place < count - 1)
        return conjunction(tests)

    def guarded(condition, action):
        if condition is True:
            action()
        else:
            pl.when(condition)(action)

    def target(dz, dx, dy):
        return (tm + dz, gx + dx, gy + dy)

    for x in range(rows):
        pltpu.make_async_copy(x_hbm.at[:, x], x_ref.at[x], load_sem).start()
    for source, landing in ((diff_hbm, small_ref.at[pl.ds(0, 1)]), (wind_hbm, small_ref.at[pl.ds(1, 2)])):
        pltpu.make_async_copy(source, landing, small_sem).start()

    barrier = pltpu.get_barrier_semaphore()
    partners = [(0, dx, dy) for dx, dy in AROUND] + [(-1, 0, 0), (1, 0, 0)]
    partners.sort(key=lambda move: -sum(map(abs, move)))
    awaited = jnp.int32(0)
    for move in partners:
        def greet(move=move):
            pl.semaphore_signal(barrier, inc=1, device_id=target(*move), device_id_type=pl.DeviceIdType.MESH)
        guarded(there(*move), greet)
        awaited = awaited + there(*move).astype(jnp.int32)

    def send_all(copies, dz, moves):
        for move in moves:
            guarded(there(dz, *move), lambda move=move: copies[move].start())

    def sends_done(copies, dz, moves):
        for move in moves:
            guarded(there(dz, *move), lambda move=move: copies[move].wait_send())

    def all_arrived(copies, dz, moves):
        for dx, dy in moves:
            guarded(there(-dz, -dx, -dy), lambda move=(dx, dy): copies[move].wait_recv())

    def remote(source, landing, in_sem, move):
        return pltpu.make_async_remote_copy(
            src_ref=source, dst_ref=landing, send_sem=out_sem, recv_sem=in_sem,
            device_id=target(*move), device_id_type=pl.DeviceIdType.MESH,
        )

    fine_copies = {}
    for move in AROUND:
        dx, dy = move
        if dy == 0:
            continue
        k = y_moves.index(move)
        if dx == 0:
            source, landing = y_send.at[(dy + 1) // 2], y_recv.at[(1 - dy) // 2]
        else:
            source = y_send.at[(dy + 1) // 2, pl.ds(0 if dx < 0 else part - REACH, REACH)]
            landing = corner_recv.at[(1 - dx) // 2, (1 - dy) // 2]
        fine_copies[move] = remote(source, landing, fine_in.at[k], (0, dx, dy))
    x_copies = []
    for r in range(REACH):
        copies = {}
        for dx in (-1, 1):
            towards = (dx + 1) // 2
            source = x_hbm.at[:, r if dx < 0 else rows - REACH + r]
            copies[dx, 0] = remote(source, x_recv.at[towards, r], x_in.at[towards], (0, dx, 0))
        x_copies.append(copies)

    def coarse_copies(main, wide_in, strips, in_sems, dz):
        row_out, row_in, side_out, side_in, corner_out, corner_in = strips
        copies = {}
        for dx, dy in PLANE if dz else AROUND:
            k = (PLANE if dz else AROUND).index((dx, dy))
            towards_x, towards_y = (dx + 1) // 2, (dy + 1) // 2
            if dx == 0 and dy == 0:
                source, landing = main, wide_in.at[pl.ds(COARSE_REACH, part_c), pl.ds(FRONT, cols_c)]
            elif dy == 0:
                source, landing = row_out.at[towards_x], row_in.at[towards_x, pl.ds(FRONT, cols_c)]
            elif dx == 0:
                source, landing = side_out.at[towards_y], side_in.at[towards_y]
            else:
                source, landing = corner_out.at[towards_x, towards_y], corner_in.at[towards_x, towards_y]
            copies[dx, dy] = remote(source, landing, in_sems.at[k], (dz, dx, dy))
        return copies

    old_strips, new_strips = strip_refs[:6], strip_refs[6:]
    old_copies = coarse_copies(None, old_wide, old_strips, old_in, 0)
    chain_copies = coarse_copies(sent, new_wide, new_strips, chain_in, 1)

    lane = lax.broadcasted_iota(jnp.int32, (1, LANES), 1)
    pack = lane // levels

    def packed(row):
        return jnp.concatenate([row] * packs, axis=1)

    def advance(source, row, start, count, consts):
        keep, spread, along_x, along_y = consts
        centre = source[row, pl.ds(start, count), :]
        east = source[row + 1, pl.ds(start, count), :]
        west = source[row - 1, pl.ds(start, count), :]
        north = source[row, pl.ds(start + 1, count), :]
        south = source[row, pl.ds(start - 1, count), :]
        pushed = along_x * (east - west) + along_y * (north - south)
        return centre * (keep - pushed) + spread * ((east + west) + (north + south))

    def native_row(x):
        if x < 0:
            return x_recv[1, x + REACH]
        if x >= rows:
            return x_recv[0, x - rows]
        return x_ref[x]

    def bring_in(row):
        stacked = jnp.concatenate([native_row(p * part + row - REACH) for p in range(packs)], axis=0)
        first[row, pl.ds(FRONT, cols), :] = stacked.T

    low_lanes = lane < levels
    high_lanes = lane >= LANES - levels
    pl.semaphore_wait(barrier, awaited)

    @pl.when(tm > 0)
    def _():
        pl.semaphore_signal(ready, inc=1, device_id=target(-1, 0, 0), device_id_type=pl.DeviceIdType.MESH)

    for copies in x_copies[: REACH // 2]:
        send_all(copies, 0, x_moves)
    pltpu.make_async_copy(small_ref, small_ref, small_sem).wait()
    diffuse = packed(small_ref[0:1, :])
    east_wind = packed(small_ref[1:2, :])
    north_wind = packed(small_ref[2:3, :])

    def constants(factor):
        spread = (time_step * factor) * diffuse
        return 1.0 - 4.0 * spread, spread, (0.5 * time_step) * east_wind, (0.5 * time_step) * north_wind

    fine_constants = constants(1.0)
    coarse_constants = constants(0.25)

    pltpu.make_async_copy(x_ref, x_ref, load_sem).wait()
    for row in range(REACH, REACH + part):
        bring_in(row)
    for row in range(part):
        y_send[0, row] = first[REACH + row, pl.ds(FRONT, REACH), :]
        y_send[1, row] = first[REACH + row, pl.ds(end - REACH, REACH), :]
    send_all(fine_copies, 0, side_moves + corner_moves)

    def restricted(source, row):
        total = source[REACH + row * RATIO, pl.ds(FRONT, cols), :]
        for r in range(1, RATIO):
            total = total + source[REACH + row * RATIO + r, pl.ds(FRONT, cols), :]
        fine_line[...] = total
        mean = fine_line[pl.ds(0, cols_c, stride=RATIO), :]
        for o in range(1, RATIO):
            mean = mean + fine_line[pl.ds(o, cols_c, stride=RATIO), :]
        return mean * (1.0 / RATIO**2)

    def swapped(value):
        return pltpu.roll(value, levels, 1)

    def pack_strips(row_of, strips):
        row_out, _, side_out, _, corner_out, _ = strips
        row_out[0] = jnp.where(low_lanes, row_of(0, 0, cols_c), swapped(row_of(1, 0, cols_c)))
        row_out[1] = jnp.where(low_lanes, swapped(row_of(part_c - 2, 0, cols_c)), row_of(part_c - 1, 0, cols_c))
        for side, col in ((0, 0), (1, cols_c - COARSE_REACH)):
            for row in range(part_c):
                side_out[side, pl.ds(COARSE_REACH * row, COARSE_REACH), :] = row_of(row, col, COARSE_REACH)
            for towards in range(2):
                corner_out[towards, side, pl.ds(0, COARSE_REACH), :] = row_out[towards, pl.ds(col, COARSE_REACH), :]

    def old_row(row, col, count):
        return old_wide[COARSE_REACH + row, pl.ds(FRONT + col, count), :]

    for row in range(part_c):
        old_wide[COARSE_REACH + row, pl.ds(FRONT, cols_c), :] = restricted(first, row)
    pack_strips(old_row, old_strips)
    send_all(old_copies, 0, AROUND)
    for copies in x_copies[REACH // 2 :]:
        send_all(copies, 0, x_moves)

    def inside_x(row, reach, length):
        place = (gx * packs + pack) * length + (row - reach)
        return jnp.logical_and(place >= 0, place < n_gx * packs * length)

    def inside_y(start, count, length):
        place = gy * length + (start - FRONT) + lax.broadcasted_iota(jnp.int32, (count, LANES), 0)
        return jnp.logical_and(place >= 0, place < n_gy * length)

    edges = ((FRONT - EDGE, inside_y(FRONT - EDGE, EDGE, cols)), (end, inside_y(end, EDGE, cols)))
    reaches = ((FRONT - REACH, inside_y(FRONT - REACH, REACH, cols)), (end, inside_y(end, REACH, cols)))
    halo_rows = [*range(REACH), *range(REACH + part, wide)]
    half = cols // 2

    def update(source, dest, row, consts, last):
        for start, count in ((FRONT, half), (FRONT + half, cols - half)):
            dest[row, pl.ds(start, count), :] = advance(source, row, start, count, consts)
        if not last:
            for start, mask in edges:
                value = advance(source, row, start, EDGE, consts)
                dest[row, pl.ds(start, EDGE), :] = jnp.where(mask, value, 0.0)

    buffers = (first, second)

    all_arrived(fine_copies, 0, side_moves)
    for side, (start, mask) in enumerate(reaches):
        for row in range(part):
            first[REACH + row, pl.ds(start, REACH), :] = jnp.where(mask, y_recv[side, row], 0.0)
    for step in range(1, SUB + 1):
        def inner_row(row, step=step):
            update(buffers[(step - 1) % 2], buffers[step % 2], row, fine_constants, step == SUB)

        pl.loop(REACH + step, REACH + part - step, unroll=2)(inner_row)

    count_c = cols_c + 2 * EDGE
    begin_c = FRONT - EDGE
    mask_y = inside_y(begin_c, count_c, cols_c)

    def extend(buffer, strips):
        _, row_in, _, side_in, _, corner_in = strips
        for side, col in ((0, end_c), (1, FRONT - COARSE_REACH)):
            for row in range(part_c):
                buffer[COARSE_REACH + row, pl.ds(col, COARSE_REACH), :] = side_in[
                    side, pl.ds(COARSE_REACH * row, COARSE_REACH), :
                ]
            for towards in range(2):
                row_in[towards, pl.ds(col, COARSE_REACH), :] = corner_in[towards, side, pl.ds(0, COARSE_REACH), :]

        def own(row):
            return buffer[COARSE_REACH + row, pl.ds(begin_c, count_c), :]

        above, below = (row_in[towards, pl.ds(begin_c, count_c), :] for towards in (0, 1))
        values = [
            jnp.where(low_lanes, below, swapped(own(part_c - 2))),
            swapped(jnp.where(high_lanes, below, own(part_c - 1))),
            *[own(row) for row in range(part_c)],
            swapped(jnp.where(low_lanes, above, own(0))),
            jnp.where(high_lanes, above, swapped(own(1))),
        ]
        for row, value in enumerate(values):
            mask = mask_y
            if not COARSE_REACH <= row < COARSE_REACH + part_c:
                mask = jnp.logical_and(mask_y, inside_x(row, COARSE_REACH, part_c))
            extended[row, pl.ds(begin_c, count_c), :] = jnp.where(mask, value, 0.0)

    all_arrived(old_copies, 0, AROUND)
    extend(old_wide, old_strips)
    for row in range(1, wide_c - 1):
        old_image[row - 1] = advance(extended, row, begin_c, count_c, coarse_constants)


    def compute_change():
        for row in range(1, wide_c - 1):
            moved = advance(extended, row, begin_c, count_c, coarse_constants) - old_image[row - 1]
            mask = jnp.logical_and(mask_y, inside_x(row, COARSE_REACH, part_c))
            change[row - 1, pl.ds(begin_c, count_c), :] = jnp.where(mask, moved, 0.0)

    def change_row(row):
        return change[row, pl.ds(begin_c, count_c), :]

    def smoothed(row):
        line[pl.ds(begin_c, count_c), :] = (
            mean_side * (change_row(row) + change_row(row + 2)) + mean_mid * change_row(row + 1)
        )
        sides = line[pl.ds(FRONT - 1, cols_c), :] + line[pl.ds(FRONT + 1, cols_c), :]
        return mean_side * sides + mean_mid * line[pl.ds(FRONT, cols_c), :]

    @pl.when(tm == 0)
    def _():
        compute_change()
        for row in range(part_c):
            sent[row] = smoothed(row)

    for dx in (-1, 1):
        whole = x_recv.at[(dx + 1) // 2]
        guarded(there(0, -dx, 0), remote(whole, whole, x_in.at[(dx + 1) // 2], (0, dx, 0)).wait_recv)
    for row in halo_rows:
        bring_in(row)
        inner = first[row, pl.ds(FRONT, cols), :]
        first[row, pl.ds(FRONT, cols), :] = jnp.where(inside_x(row, REACH, part), inner, 0.0)
    all_arrived(fine_copies, 0, corner_moves)
    for side, (start, mask_side) in enumerate(reaches):
        for row in halo_rows:
            if row < REACH:
                here = jnp.where(high_lanes, corner_recv[0, side, row], y_recv[side, row + part - REACH])
                here = pltpu.roll(here, levels, 1)
            else:
                here = jnp.where(low_lanes, corner_recv[1, side, row - part - REACH], y_recv[side, row - part - REACH])
                here = pltpu.roll(here, LANES - levels, 1)
            mask = jnp.logical_and(mask_side, inside_x(row, REACH, part))
            first[row, pl.ds(start, REACH), :] = jnp.where(mask, here, 0.0)
    for step in range(1, SUB + 1):
        def outer_row(row, step=step):
            for shifted in (row, row + part + REACH - 2 * step):
                mask_x = inside_x(shifted, REACH, part)
                consts = tuple(jnp.where(mask_x, c, 0.0) for c in fine_constants)
                update(buffers[(step - 1) % 2], buffers[step % 2], shifted, consts, step == SUB)

        pl.loop(step, REACH + step)(outer_row)
    fine = buffers[SUB % 2]

    for row in range(part_c):
        fine_mean[row] = restricted(fine, row)

    def write_fine():
        for row in range(part):
            turned[row] = fine[REACH + row, pl.ds(FRONT, cols), :].T

    def pass_on():
        pl.semaphore_wait(ready, 1)
        pack_strips(lambda row, col, count: sent[row, pl.ds(col, count), :], new_strips)
        send_all(chain_copies, 1, AROUND)
        send_all(chain_copies, 1, ((0, 0),))

    @pl.when(jnp.logical_and(tm == 0, tm < n_tm - 1))
    def _():
        for row in range(part_c):
            sent[row] = fine_mean[row] + sent[row]
        pass_on()

    write_fine()

    @pl.when(tm > 0)
    def _():
        all_arrived(chain_copies, 1, PLANE)
        extend(new_wide, new_strips)
        compute_change()

    @pl.when(jnp.logical_and(tm > 0, tm < n_tm - 1))
    def _():
        for row in range(part_c):
            sent[row] = fine_mean[row] + smoothed(row)
        pass_on()

    sends_done(fine_copies, 0, y_moves)
    sends_done(old_copies, 0, AROUND)
    for copies in x_copies:
        sends_done(copies, 0, x_moves)
    pl.when(tm < n_tm - 1)(lambda: sends_done(chain_copies, 1, PLANE))


def closing(levels, rows, turned, change, out_hbm, filled, spread_rows, sem):
    packs = LANES // levels
    part, _, cols = turned.shape
    part_c = part // RATIO
    count_c = cols // RATIO + 2 * EDGE
    coarse_col = lax.broadcasted_iota(jnp.int32, (count_c, cols), 0) - EDGE
    fine_col = lax.broadcasted_iota(jnp.int32, (count_c, cols), 1)
    offset_of = fine_col & (RATIO - 1)
    apart = coarse_col - (fine_col >> (RATIO.bit_length() - 1))
    spreading = jnp.zeros((count_c, cols), jnp.float32)
    for o in range(RATIO):
        for distance, weights in ((-1, weights_low), (0, weights_mid), (1, weights_high)):
            chosen = jnp.logical_and(offset_of == o, apart == distance)
            spreading = jnp.where(chosen, weights[o], spreading)
    spreading = jnp.concatenate([spreading.astype(jnp.bfloat16)] * 3, axis=0)
    def spread_row(row):
        rest, pieces = change[row, pl.ds(FRONT - EDGE, count_c), :], []
        for _ in range(3):
            piece = rest.astype(jnp.bfloat16).astype(jnp.float32)
            pieces.append(piece)
            rest = rest - piece
        split = jnp.concatenate(pieces, axis=0).T.astype(jnp.bfloat16)
        return jnp.dot(split, spreading, preferred_element_type=jnp.float32)

    for row in range(2):
        spread_rows[row] = spread_row(row)
    for row in range(part):
        at, o = row // RATIO, row % RATIO
        if o == 0:
            spread_rows[at + 2] = spread_row(at + 2)
        total = turned[row] + weights_mid[o] * spread_rows[at + 1]
        if weights_low[o]:
            total = total + weights_low[o] * spread_rows[at]
        if weights_high[o]:
            total = total + weights_high[o] * spread_rows[at + 2]
        filled[row] = total
        for p in range(packs):
            x = p * part + row
            pltpu.make_async_copy(filled.at[row, pl.ds(p * levels, levels)], out_hbm.at[:, x], sem).start()
    pltpu.make_async_copy(filled, filled, sem).wait()


def shards(sizes, state_starts, diffusivity, wind):
    _, levels, rows, cols = state_starts.shape
    packs = LANES // levels
    if packs != 2 or levels * packs != LANES:
        raise ValueError(levels)
    part = rows // packs
    part_c = part // RATIO
    cols_c = cols // RATIO
    wide, wide_c = part + 2 * REACH, part_c + 2 * COARSE_REACH
    vmem = functools.partial(pltpu.VMEM, dtype=jnp.float32)
    scratch = [
        vmem((rows, levels, cols)),
        vmem((3, levels)),
        pltpu.SemaphoreType.DMA,
        pltpu.SemaphoreType.DMA,
        pltpu.SemaphoreType.REGULAR,
        vmem((wide, cols + 2 * FRONT, LANES)),
        vmem((wide, cols + 2 * FRONT, LANES)),
        vmem((2, REACH, levels, cols)),
        vmem((2, part, REACH, LANES)),
        vmem((2, part, REACH, LANES)),
        vmem((2, 2, REACH, REACH, LANES)),
        vmem((wide_c, cols_c + 2 * FRONT, LANES)),
        vmem((wide_c, cols_c + 2 * FRONT, LANES)),
        vmem((wide_c, cols_c + 2 * FRONT, LANES)),
        vmem((wide_c - 2, cols_c + 2 * EDGE, LANES)),
        vmem((part_c, cols_c, LANES)),
        vmem((part_c, cols_c, LANES)),
        vmem((cols_c + 2 * FRONT, LANES)),
        vmem((cols, LANES)),
        pltpu.SemaphoreType.DMA,
    ] + [pltpu.SemaphoreType.DMA((count,)) for count in (2, len(y_moves), len(AROUND), len(PLANE))]
    scratch += [
        vmem((2, cols_c, LANES)),
        vmem((2, cols_c + 2 * FRONT, LANES)),
        vmem((2, COARSE_REACH * part_c, LANES)),
        vmem((2, COARSE_REACH * part_c, LANES)),
        vmem((2, 2, EDGE, LANES)),
        vmem((2, 2, EDGE, LANES)),
    ] * 2
    in_vmem = pl.BlockSpec(memory_space=pltpu.VMEM)
    handed = pl.pallas_call(
        functools.partial(kernel, sizes, levels, rows, cols),
        out_shape=(vmem((part, LANES, cols)), vmem((part_c + 2, cols_c + 2 * FRONT, LANES))),
        in_specs=[pl.BlockSpec(memory_space=pl.ANY)] * 3,
        out_specs=(in_vmem, in_vmem),
        scratch_shapes=scratch,
        compiler_params=pltpu.CompilerParams(collective_id=0, has_side_effects=True),
        name="parareal",
    )(state_starts.reshape(levels, rows, cols), diffusivity.reshape(1, levels), wind)
    ending = pl.pallas_call(
        functools.partial(closing, levels, rows),
        out_shape=jax.ShapeDtypeStruct((levels, rows, cols), jnp.float32),
        in_specs=[in_vmem, in_vmem],
        out_specs=pl.BlockSpec(memory_space=pl.ANY),
        scratch_shapes=[
            vmem((part, LANES, cols)),
            vmem((part_c + 2, LANES, cols)),
            pltpu.SemaphoreType.DMA,
        ],
        name="closing",
    )(*(pltpu.with_memory_space_constraint(array, pltpu.VMEM) for array in handed))
    return ending.reshape(1, levels, rows, cols)


def solution(mesh):
    sizes = tuple(mesh.shape[axis] for axis in ("tm", "gx", "gy"))
    placed = (P("tm", None, "gx", "gy"), P(), P())
    return jax.shard_map(
        functools.partial(shards, sizes),
        mesh=mesh, in_specs=placed, out_specs=P("tm", None, "gx", "gy"), check_vma=False,
    )
```

```python
import functools

import jax
import jax.numpy as jnp
from jax import lax
from jax.experimental import pallas as pl
from jax.experimental.pallas import tpu as pltpu
from jax.sharding import PartitionSpec as P

SUB = 4
REACH = SUB
RATIO = 4
LANES = 128
EDGE = 8
FRONT = 2 * EDGE
COARSE_REACH = 2

time_step = 0.2
weights_low = (0.375, 0.125, 0.0, 0.0)
weights_mid = (0.625, 0.875, 0.875, 0.625)
weights_high = (0.0, 0.0, 0.125, 0.375)
mean_side, mean_mid = 0.125, 0.75

PLANE = tuple((dx, dy) for dx in (-1, 0, 1) for dy in (-1, 0, 1))
AROUND = tuple(d for d in PLANE if d != (0, 0))
x_moves = tuple(d for d in AROUND if d[1] == 0)
y_moves = tuple(d for d in AROUND if d[1] != 0)
side_moves = tuple(d for d in y_moves if d[0] == 0)
corner_moves = tuple(d for d in y_moves if d[0] != 0)


def conjunction(conditions):
    total = True
    for condition in conditions:
        total = condition if total is True else jnp.logical_and(total, condition)
    return total


def kernel(
    sizes, levels, rows, cols,
    x_hbm, diff_hbm, wind_hbm, turned, change,
    x_ref, small_ref, load_sems, small_sem, ready,
    first, second, x_recv, y_send, y_recv, corner_recv,
    old_wide, new_wide, extended, old_image,
    sent, fine_mean, line, fine_line,
    out_sem, near_in, far_in, fine_in, old_in, chain_in, *strip_refs,
):
    n_tm, n_gx, n_gy = sizes
    tm, gx, gy = lax.axis_index("tm"), lax.axis_index("gx"), lax.axis_index("gy")
    packs = LANES // levels
    part = rows // packs
    part_c = part // RATIO
    cols_c = cols // RATIO
    wide = part + 2 * REACH
    wide_c = part_c + 2 * COARSE_REACH
    end = FRONT + cols
    end_c = FRONT + cols_c

    def there(dz, dx, dy):
        tests = []
        for place, move, count in ((tm, dz, n_tm), (gx, dx, n_gx), (gy, dy, n_gy)):
            if move < 0:
                tests.append(place > 0)
            if move > 0:
                tests.append(place < count - 1)
        return conjunction(tests)

    def guarded(condition, action):
        if condition is True:
            action()
        else:
            pl.when(condition)(action)

    def target(dz, dx, dy):
        return (tm + dz, gx + dx, gy + dy)

    rows_first = [*range(REACH), *range(part - REACH, part)]
    rows_later = [*range(REACH, part - REACH)]
    for group, group_rows in enumerate((rows_first, rows_later)):
        for row in group_rows:
            for x in range(row, rows, part):
                pltpu.make_async_copy(x_hbm.at[:, x], x_ref.at[x], load_sems.at[group]).start()
    for source, landing in ((diff_hbm, small_ref.at[pl.ds(0, 1)]), (wind_hbm, small_ref.at[pl.ds(1, 2)])):
        pltpu.make_async_copy(source, landing, small_sem).start()

    barrier = pltpu.get_barrier_semaphore()
    partners = [(0, dx, dy) for dx, dy in AROUND] + [(-1, 0, 0), (1, 0, 0)]
    partners.sort(key=lambda move: -sum(map(abs, move)))
    awaited = jnp.int32(0)
    for move in partners:
        def greet(move=move):
            pl.semaphore_signal(barrier, inc=1, device_id=target(*move), device_id_type=pl.DeviceIdType.MESH)
        guarded(there(*move), greet)
        awaited = awaited + there(*move).astype(jnp.int32)

    def send_all(copies, dz, moves):
        for move in moves:
            guarded(there(dz, *move), lambda move=move: copies[move].start())

    def sends_done(copies, dz, moves):
        for move in moves:
            guarded(there(dz, *move), lambda move=move: copies[move].wait_send())

    def all_arrived(copies, dz, moves):
        for dx, dy in moves:
            guarded(there(-dz, -dx, -dy), lambda move=(dx, dy): copies[move].wait_recv())

    def remote(source, landing, in_sem, move):
        return pltpu.make_async_remote_copy(
            src_ref=source, dst_ref=landing, send_sem=out_sem, recv_sem=in_sem,
            device_id=target(*move), device_id_type=pl.DeviceIdType.MESH,
        )

    fine_copies = {}
    for move in y_moves:
        dx, dy = move
        if dx == 0:
            source, landing = y_send.at[(dy + 1) // 2], y_recv.at[(1 - dy) // 2]
        else:
            source = y_send.at[(dy + 1) // 2, pl.ds(0 if dx < 0 else part - REACH, REACH)]
            landing = corner_recv.at[(1 - dx) // 2, (1 - dy) // 2]
        fine_copies[move] = remote(source, landing, fine_in.at[y_moves.index(move)], (0, dx, dy))
    near, far = REACH // 2, REACH - REACH // 2
    near_copies, far_copies = {}, {}
    for dx in (-1, 1):
        low = dx < 0
        for copies, start, count, in_sems in (
            (near_copies, 0 if low else far, near, near_in), (far_copies, near if low else 0, far, far_in)
        ):
            source = x_ref.at[pl.ds(start if low else rows - REACH + start, count)]
            landing = x_recv.at[0 if low else 1, pl.ds(start, count)]
            copies[dx, 0] = remote(source, landing, in_sems.at[0 if low else 1], (0, dx, 0))

    def coarse_copies(main, wide_in, strips, in_sems, dz):
        row_out, row_in, side_out, side_in, corner_out, corner_in = strips
        copies = {}
        for dx, dy in PLANE if dz else AROUND:
            towards_x, towards_y = (dx + 1) // 2, (dy + 1) // 2
            if dx == 0 and dy == 0:
                source, landing = main, wide_in.at[pl.ds(COARSE_REACH, part_c), pl.ds(FRONT, cols_c)]
            elif dy == 0:
                source, landing = row_out.at[towards_x], row_in.at[towards_x, pl.ds(FRONT, cols_c)]
            elif dx == 0:
                source, landing = side_out.at[towards_y], side_in.at[towards_y]
            else:
                source, landing = corner_out.at[towards_x, towards_y], corner_in.at[towards_x, towards_y]
            k = (PLANE if dz else AROUND).index((dx, dy))
            copies[dx, dy] = remote(source, landing, in_sems.at[k], (dz, dx, dy))
        return copies

    old_strips, new_strips = strip_refs[:6], strip_refs[6:]
    old_copies = coarse_copies(None, old_wide, old_strips, old_in, 0)
    chain_copies = coarse_copies(sent, new_wide, new_strips, chain_in, 1)

    lane = lax.broadcasted_iota(jnp.int32, (1, LANES), 1)
    pack = lane // levels

    def packed(row):
        return jnp.concatenate([row] * packs, axis=1)

    def advance(source, row, start, count, consts):
        keep, spread, along_x, along_y = consts
        centre = source[row, pl.ds(start, count), :]
        east = source[row + 1, pl.ds(start, count), :]
        west = source[row - 1, pl.ds(start, count), :]
        north = source[row, pl.ds(start + 1, count), :]
        south = source[row, pl.ds(start - 1, count), :]
        pushed = along_x * (east - west) + along_y * (north - south)
        return centre * (keep - pushed) + spread * ((east + west) + (north + south))

    def native_row(x):
        if x < 0:
            return x_recv[1, x + REACH]
        if x >= rows:
            return x_recv[0, x - rows]
        return x_ref[x]

    def bring_in(row):
        stacked = jnp.concatenate([native_row(p * part + row - REACH) for p in range(packs)], axis=0)
        first[row, pl.ds(FRONT, cols), :] = stacked.T

    low_lanes = lane < levels
    high_lanes = lane >= LANES - levels
    pl.semaphore_wait(barrier, awaited)

    @pl.when(tm > 0)
    def _():
        pl.semaphore_signal(ready, inc=1, device_id=target(-1, 0, 0), device_id_type=pl.DeviceIdType.MESH)

    pltpu.make_async_copy(small_ref, small_ref, small_sem).wait()
    diffuse = packed(small_ref[0:1, :])
    east_wind = packed(small_ref[1:2, :])
    north_wind = packed(small_ref[2:3, :])

    def constants(factor):
        spread = (time_step * factor) * diffuse
        return 1.0 - 4.0 * spread, spread, (0.5 * time_step) * east_wind, (0.5 * time_step) * north_wind

    fine_constants = constants(1.0)
    coarse_constants = constants(0.25)

    def load_done(group, group_rows):
        whole = x_ref.at[pl.ds(0, packs * len(group_rows))]
        pltpu.make_async_copy(whole, whole, load_sems.at[group]).wait()

    def bring_own(group_rows):
        for row in group_rows:
            bring_in(REACH + row)
            y_send[0, row] = first[REACH + row, pl.ds(FRONT, REACH), :]
            y_send[1, row] = first[REACH + row, pl.ds(end - REACH, REACH), :]

    load_done(0, rows_first)
    bring_own(rows_first)
    send_all(fine_copies, 0, corner_moves)
    send_all(near_copies, 0, x_moves)
    load_done(1, rows_later)
    bring_own(rows_later)
    send_all(fine_copies, 0, side_moves)

    def restricted(source, row):
        total = source[REACH + row * RATIO, pl.ds(FRONT, cols), :]
        for r in range(1, RATIO):
            total = total + source[REACH + row * RATIO + r, pl.ds(FRONT, cols), :]
        fine_line[...] = total
        mean = fine_line[pl.ds(0, cols_c, stride=RATIO), :]
        for o in range(1, RATIO):
            mean = mean + fine_line[pl.ds(o, cols_c, stride=RATIO), :]
        return mean * (1.0 / RATIO**2)

    def swapped(value):
        return pltpu.roll(value, levels, 1)

    def pack_strips(row_of, strips):
        row_out, _, side_out, _, corner_out, _ = strips
        row_out[0] = jnp.where(low_lanes, row_of(0, 0, cols_c), swapped(row_of(1, 0, cols_c)))
        row_out[1] = jnp.where(low_lanes, swapped(row_of(part_c - 2, 0, cols_c)), row_of(part_c - 1, 0, cols_c))
        for side, col in ((0, 0), (1, cols_c - COARSE_REACH)):
            for row in range(part_c):
                side_out[side, pl.ds(COARSE_REACH * row, COARSE_REACH), :] = row_of(row, col, COARSE_REACH)
            for towards in range(2):
                corner_out[towards, side] = row_out[towards, pl.ds(col, COARSE_REACH), :]

    def old_row(row, col, count):
        return old_wide[COARSE_REACH + row, pl.ds(FRONT + col, count), :]

    for row in range(part_c):
        old_wide[COARSE_REACH + row, pl.ds(FRONT, cols_c), :] = restricted(first, row)
    pack_strips(old_row, old_strips)
    send_all(old_copies, 0, AROUND)
    send_all(far_copies, 0, x_moves)

    def inside_x(row, reach, length):
        place = (gx * packs + pack) * length + (row - reach)
        return jnp.logical_and(place >= 0, place < n_gx * packs * length)

    def inside_y(start, count, length):
        place = gy * length + (start - FRONT) + lax.broadcasted_iota(jnp.int32, (count, LANES), 0)
        return jnp.logical_and(place >= 0, place < n_gy * length)

    edges = ((FRONT - EDGE, inside_y(FRONT - EDGE, EDGE, cols)), (end, inside_y(end, EDGE, cols)))
    reaches = ((FRONT - REACH, inside_y(FRONT - REACH, REACH, cols)), (end, inside_y(end, REACH, cols)))
    half = cols // 2

    def fill(source, dest, row, start, count, consts):
        dest[row, pl.ds(start, count), :] = advance(source, row, start, count, consts)

    def fill_edges(source, dest, row, consts):
        for start, mask in edges:
            value = advance(source, row, start, EDGE, consts)
            dest[row, pl.ds(start, EDGE), :] = jnp.where(mask, value, 0.0)

    def update(source, dest, row, consts, last):
        for start, count in ((FRONT, half), (FRONT + half, cols - half)):
            fill(source, dest, row, start, count, consts)
        if not last:
            fill_edges(source, dest, row, consts)

    buffers = (first, second)

    def inner_steps(row_update):
        for step in range(1, SUB + 1):
            def inner_row(row, step=step):
                row_update(buffers[(step - 1) % 2], buffers[step % 2], row, step)

            pl.loop(REACH + step, REACH + part - step, unroll=2)(inner_row)

    def centre_update(source, dest, row, step):
        fill(source, dest, row, FRONT + EDGE * step, half - EDGE * step, fine_constants)
        fill(source, dest, row, FRONT + half, cols - half - EDGE * step, fine_constants)

    def sides_update(source, dest, row, step):
        fill(source, dest, row, FRONT, EDGE * step, fine_constants)
        fill(source, dest, row, end - EDGE * step, EDGE * step, fine_constants)
        if step < SUB:
            fill_edges(source, dest, row, fine_constants)

    inner_steps(centre_update)
    all_arrived(fine_copies, 0, side_moves)
    for side, (start, mask) in enumerate(reaches):
        for row in range(part):
            first[REACH + row, pl.ds(start, REACH), :] = jnp.where(mask, y_recv[side, row], 0.0)
    inner_steps(sides_update)

    def bring_halo(halo_rows):
        for row in halo_rows:
            bring_in(row)
            inner = first[row, pl.ds(FRONT, cols), :]
            first[row, pl.ds(FRONT, cols), :] = jnp.where(inside_x(row, REACH, part), inner, 0.0)
        for side, (start, mask_side) in enumerate(reaches):
            for row in halo_rows:
                if row < REACH:
                    here = jnp.where(high_lanes, corner_recv[0, side, row], y_recv[side, row + part - REACH])
                    here = pltpu.roll(here, levels, 1)
                else:
                    at = row - part - REACH
                    here = pltpu.roll(jnp.where(low_lanes, corner_recv[1, side, at], y_recv[side, at]), LANES - levels, 1)
                mask = jnp.logical_and(mask_side, inside_x(row, REACH, part))
                first[row, pl.ds(start, REACH), :] = jnp.where(mask, here, 0.0)

    def outer_steps(low_shift, high_shift, count):
        for step in range(1, SUB + 1):
            def outer_row(k, step=step):
                for row in (step + low_shift + k, part + REACH - step + high_shift + k):
                    mask_x = inside_x(row, REACH, part)
                    consts = tuple(jnp.where(mask_x, c, 0.0) for c in fine_constants)
                    update(buffers[(step - 1) % 2], buffers[step % 2], row, consts, step == SUB)

            pl.loop(0, count)(outer_row)

    all_arrived(near_copies, 0, x_moves)
    all_arrived(fine_copies, 0, corner_moves)
    bring_halo([*range(far, REACH), *range(REACH + part, REACH + part + near)])
    outer_steps(far, 0, near)

    count_c = cols_c + 2 * EDGE
    begin_c = FRONT - EDGE
    mask_y = inside_y(begin_c, count_c, cols_c)

    def extend(buffer, strips):
        _, row_in, _, side_in, _, corner_in = strips
        for side, col in ((0, end_c), (1, FRONT - COARSE_REACH)):
            for row in range(part_c):
                buffer[COARSE_REACH + row, pl.ds(col, COARSE_REACH), :] = side_in[
                    side, pl.ds(COARSE_REACH * row, COARSE_REACH), :
                ]
            for towards in range(2):
                row_in[towards, pl.ds(col, COARSE_REACH), :] = corner_in[towards, side]

        def own(row):
            return buffer[COARSE_REACH + row, pl.ds(begin_c, count_c), :]

        above, below = (row_in[towards, pl.ds(begin_c, count_c), :] for towards in (0, 1))
        values = [
            jnp.where(low_lanes, below, swapped(own(part_c - 2))),
            swapped(jnp.where(high_lanes, below, own(part_c - 1))),
            *[own(row) for row in range(part_c)],
            swapped(jnp.where(low_lanes, above, own(0))),
            jnp.where(high_lanes, above, swapped(own(1))),
        ]
        for row, value in enumerate(values):
            mask = mask_y
            if not COARSE_REACH <= row < COARSE_REACH + part_c:
                mask = jnp.logical_and(mask_y, inside_x(row, COARSE_REACH, part_c))
            extended[row, pl.ds(begin_c, count_c), :] = jnp.where(mask, value, 0.0)

    all_arrived(old_copies, 0, AROUND)
    extend(old_wide, old_strips)
    for row in range(1, wide_c - 1):
        old_image[row - 1] = advance(extended, row, begin_c, count_c, coarse_constants)


    def compute_change():
        for row in range(1, wide_c - 1):
            moved = advance(extended, row, begin_c, count_c, coarse_constants) - old_image[row - 1]
            mask = jnp.logical_and(mask_y, inside_x(row, COARSE_REACH, part_c))
            change[row - 1, pl.ds(begin_c, count_c), :] = jnp.where(mask, moved, 0.0)

    def change_row(row):
        return change[row, pl.ds(begin_c, count_c), :]

    def smoothed(row):
        line[pl.ds(begin_c, count_c), :] = (
            mean_side * (change_row(row) + change_row(row + 2)) + mean_mid * change_row(row + 1)
        )
        sides = line[pl.ds(FRONT - 1, cols_c), :] + line[pl.ds(FRONT + 1, cols_c), :]
        return mean_side * sides + mean_mid * line[pl.ds(FRONT, cols_c), :]

    @pl.when(tm == 0)
    def _():
        compute_change()
        for row in range(part_c):
            sent[row] = smoothed(row)

    all_arrived(far_copies, 0, x_moves)
    bring_halo([*range(far), *range(REACH + part + near, wide)])
    outer_steps(0, near, far)
    fine = buffers[SUB % 2]

    for row in range(part_c):
        fine_mean[row] = restricted(fine, row)

    def write_fine():
        for row in range(part):
            turned[row] = fine[REACH + row, pl.ds(FRONT, cols), :].T

    def pass_on():
        pl.semaphore_wait(ready, 1)
        pack_strips(lambda row, col, count: sent[row, pl.ds(col, count), :], new_strips)
        send_all(chain_copies, 1, AROUND)
        send_all(chain_copies, 1, ((0, 0),))

    @pl.when(jnp.logical_and(tm == 0, tm < n_tm - 1))
    def _():
        for row in range(part_c):
            sent[row] = fine_mean[row] + sent[row]
        pass_on()

    write_fine()

    @pl.when(tm > 0)
    def _():
        all_arrived(chain_copies, 1, PLANE)
        extend(new_wide, new_strips)
        compute_change()

    @pl.when(jnp.logical_and(tm > 0, tm < n_tm - 1))
    def _():
        for row in range(part_c):
            sent[row] = fine_mean[row] + smoothed(row)
        pass_on()

    sends_done(fine_copies, 0, y_moves)
    sends_done(old_copies, 0, AROUND)
    sends_done(near_copies, 0, x_moves)
    sends_done(far_copies, 0, x_moves)
    pl.when(tm < n_tm - 1)(lambda: sends_done(chain_copies, 1, PLANE))


def closing(levels, rows, turned, change, out_hbm, filled, spread_rows, sem):
    packs = LANES // levels
    part, _, cols = turned.shape
    part_c = part // RATIO
    count_c = cols // RATIO + 2 * EDGE
    coarse_col = lax.broadcasted_iota(jnp.int32, (count_c, cols), 0) - EDGE
    fine_col = lax.broadcasted_iota(jnp.int32, (count_c, cols), 1)
    offset_of = fine_col & (RATIO - 1)
    apart = coarse_col - (fine_col >> (RATIO.bit_length() - 1))
    spreading = jnp.zeros((count_c, cols), jnp.float32)
    for o in range(RATIO):
        for distance, weights in ((-1, weights_low), (0, weights_mid), (1, weights_high)):
            chosen = jnp.logical_and(offset_of == o, apart == distance)
            spreading = jnp.where(chosen, weights[o], spreading)
    spreading = jnp.concatenate([spreading.astype(jnp.bfloat16)] * 3, axis=0)
    def spread_row(row):
        rest, pieces = change[row, pl.ds(FRONT - EDGE, count_c), :], []
        for _ in range(3):
            piece = rest.astype(jnp.bfloat16).astype(jnp.float32)
            pieces.append(piece)
            rest = rest - piece
        split = jnp.concatenate(pieces, axis=0).T.astype(jnp.bfloat16)
        return jnp.dot(split, spreading, preferred_element_type=jnp.float32)

    for row in range(2):
        spread_rows[row] = spread_row(row)
    for row in range(part):
        at, o = row // RATIO, row % RATIO
        if o == 0:
            spread_rows[at + 2] = spread_row(at + 2)
        total = turned[row] + weights_mid[o] * spread_rows[at + 1]
        if weights_low[o]:
            total = total + weights_low[o] * spread_rows[at]
        if weights_high[o]:
            total = total + weights_high[o] * spread_rows[at + 2]
        filled[row] = total
        for p in range(packs):
            x = p * part + row
            pltpu.make_async_copy(filled.at[row, pl.ds(p * levels, levels)], out_hbm.at[:, x], sem).start()
    pltpu.make_async_copy(filled, filled, sem).wait()


def shards(sizes, state_starts, diffusivity, wind):
    _, levels, rows, cols = state_starts.shape
    packs = LANES // levels
    if packs != 2 or levels * packs != LANES:
        raise ValueError(levels)
    part = rows // packs
    part_c = part // RATIO
    cols_c = cols // RATIO
    wide, wide_c = part + 2 * REACH, part_c + 2 * COARSE_REACH
    vmem = functools.partial(pltpu.VMEM, dtype=jnp.float32)
    scratch = [
        vmem((rows, levels, cols)),
        vmem((3, levels)),
        pltpu.SemaphoreType.DMA((2,)),
        pltpu.SemaphoreType.DMA,
        pltpu.SemaphoreType.REGULAR,
        vmem((wide, cols + 2 * FRONT, LANES)),
        vmem((wide, cols + 2 * FRONT, LANES)),
        vmem((2, REACH, levels, cols)),
        vmem((2, part, REACH, LANES)),
        vmem((2, part, REACH, LANES)),
        vmem((2, 2, REACH, REACH, LANES)),
        vmem((wide_c, cols_c + 2 * FRONT, LANES)),
        vmem((wide_c, cols_c + 2 * FRONT, LANES)),
        vmem((wide_c, cols_c + 2 * FRONT, LANES)),
        vmem((wide_c - 2, cols_c + 2 * EDGE, LANES)),
        vmem((part_c, cols_c, LANES)),
        vmem((part_c, cols_c, LANES)),
        vmem((cols_c + 2 * FRONT, LANES)),
        vmem((cols, LANES)),
        pltpu.SemaphoreType.DMA,
    ] + [pltpu.SemaphoreType.DMA((count,)) for count in (2, 2, len(y_moves), len(AROUND), len(PLANE))]
    scratch += [
        vmem((2, cols_c, LANES)),
        vmem((2, cols_c + 2 * FRONT, LANES)),
        vmem((2, COARSE_REACH * part_c, LANES)),
        vmem((2, COARSE_REACH * part_c, LANES)),
        vmem((2, 2, COARSE_REACH, LANES)),
        vmem((2, 2, COARSE_REACH, LANES)),
    ] * 2
    in_vmem = pl.BlockSpec(memory_space=pltpu.VMEM)
    handed = pl.pallas_call(
        functools.partial(kernel, sizes, levels, rows, cols),
        out_shape=(vmem((part, LANES, cols)), vmem((part_c + 2, cols_c + 2 * FRONT, LANES))),
        in_specs=[pl.BlockSpec(memory_space=pl.ANY)] * 3,
        out_specs=(in_vmem, in_vmem),
        scratch_shapes=scratch,
        compiler_params=pltpu.CompilerParams(collective_id=0, has_side_effects=True),
        name="parareal",
    )(state_starts.reshape(levels, rows, cols), diffusivity.reshape(1, levels), wind)
    ending = pl.pallas_call(
        functools.partial(closing, levels, rows),
        out_shape=jax.ShapeDtypeStruct((levels, rows, cols), jnp.float32),
        in_specs=[in_vmem, in_vmem],
        out_specs=pl.BlockSpec(memory_space=pl.ANY),
        scratch_shapes=[
            vmem((part, LANES, cols)),
            vmem((part_c + 2, LANES, cols)),
            pltpu.SemaphoreType.DMA,
        ],
        name="closing",
    )(*(pltpu.with_memory_space_constraint(array, pltpu.VMEM) for array in handed))
    return ending.reshape(1, levels, rows, cols)


def solution(mesh):
    sizes = tuple(mesh.shape[axis] for axis in ("tm", "gx", "gy"))
    placed = (P("tm", None, "gx", "gy"), P(), P())
    return jax.shard_map(
        functools.partial(shards, sizes),
        mesh=mesh, in_specs=placed, out_specs=P("tm", None, "gx", "gy"), check_vma=False,
    )
```

```python
import functools
import math

import jax
import jax.numpy as jnp
from jax import lax
from jax.experimental import pallas as pl
from jax.experimental.pallas import tpu as pltpu
from jax.sharding import PartitionSpec as P

SUB = 4
REACH = SUB
RATIO = 4
LANES = 128
EDGE = 8
FRONT = 2 * EDGE
COARSE_REACH = 2
TALLY = 1024

time_step = 0.2
weights_low = (0.375, 0.125, 0.0, 0.0)
weights_mid = (0.625, 0.875, 0.875, 0.625)
weights_high = (0.0, 0.0, 0.125, 0.375)
mean_side, mean_mid = 0.125, 0.75

PLANE = tuple((dx, dy) for dx in (-1, 0, 1) for dy in (-1, 0, 1))
AROUND = tuple(d for d in PLANE if d != (0, 0))
x_moves = tuple(d for d in AROUND if d[1] == 0)
y_moves = tuple(d for d in AROUND if d[1] != 0)
side_moves = tuple(d for d in y_moves if d[0] == 0)
corner_moves = tuple(d for d in y_moves if d[0] != 0)


def conjunction(conditions):
    total = True
    for condition in conditions:
        total = condition if total is True else jnp.logical_and(total, condition)
    return total


def kernel(
    sizes, levels, rows, cols,
    x_hbm, diff_hbm, wind_hbm, turned, change,
    x_ref, small_ref, load_sems, small_sem, ready,
    first, second, x_recv, y_send, y_recv, corner_recv,
    old_wide, new_wide, extended, old_image,
    sent, fine_mean, line, fine_line, tally,
    out_sem, near_in, far_in, side_in_sem, corner_in_sem, old_in, chain_in, *strip_refs,
):
    n_tm, n_gx, n_gy = sizes
    tm, gx, gy = lax.axis_index("tm"), lax.axis_index("gx"), lax.axis_index("gy")
    packs = LANES // levels
    part = rows // packs
    part_c = part // RATIO
    cols_c = cols // RATIO
    wide = part + 2 * REACH
    wide_c = part_c + 2 * COARSE_REACH
    end = FRONT + cols
    end_c = FRONT + cols_c

    def there(dz, dx, dy):
        tests = []
        for place, move, count in ((tm, dz, n_tm), (gx, dx, n_gx), (gy, dy, n_gy)):
            if move < 0:
                tests.append(place > 0)
            if move > 0:
                tests.append(place < count - 1)
        return conjunction(tests)

    def guarded(condition, action):
        if condition is True:
            action()
        else:
            pl.when(condition)(action)

    def target(dz, dx, dy):
        return (tm + dz, gx + dx, gy + dy)

    rows_first = [*range(REACH), *range(part - REACH, part)]
    rows_later = [*range(REACH, part - REACH)]
    for group, group_rows in enumerate((rows_first, rows_later)):
        for row in group_rows:
            for x in range(row, rows, part):
                pltpu.make_async_copy(x_hbm.at[:, x], x_ref.at[x], load_sems.at[group]).start()
    for source, landing in ((diff_hbm, small_ref.at[pl.ds(0, 1)]), (wind_hbm, small_ref.at[pl.ds(1, 2)])):
        pltpu.make_async_copy(source, landing, small_sem).start()

    barrier = pltpu.get_barrier_semaphore()
    partners = [(0, dx, dy) for dx, dy in AROUND] + [(-1, 0, 0), (1, 0, 0)]
    partners.sort(key=lambda move: -sum(map(abs, move)))
    awaited = jnp.int32(0)
    for move in partners:
        def greet(move=move):
            pl.semaphore_signal(barrier, inc=1, device_id=target(*move), device_id_type=pl.DeviceIdType.MESH)
        guarded(there(*move), greet)
        awaited = awaited + there(*move).astype(jnp.int32)

    def send_all(copies, dz, moves):
        for move in moves:
            guarded(there(dz, *move), lambda move=move: copies[move].start())

    def sends_done(copies, dz, moves):
        for move in moves:
            guarded(there(dz, *move), lambda move=move: copies[move].wait_send())

    stand_ins, sizes_in_rows = {}, {}

    def fill_missing(copies, moves):
        for dx, dy in moves:
            @pl.when(jnp.logical_not(there(0, -dx, -dy)))
            def _(dx=dx, dy=dy):
                pltpu.make_async_copy(*stand_ins[id(copies)][dx, dy]).start()

    def all_arrived(copies, in_sem, moves):
        height = sum(sizes_in_rows[id(copies)][move] for move in moves)
        whole = tally.at[pl.ds(0, height)]
        pltpu.make_async_copy(whole, whole, in_sem).wait()

    def plan(copies, move, source, landing, in_sem, dz=0):
        copies[move] = remote(source, landing, in_sem, (dz, *move))
        stand_ins.setdefault(id(copies), {})[move] = (source, landing, in_sem)
        sizes_in_rows.setdefault(id(copies), {})[move] = math.prod(source.shape[:-1])

    def remote(source, landing, in_sem, move):
        return pltpu.make_async_remote_copy(
            src_ref=source, dst_ref=landing, send_sem=out_sem, recv_sem=in_sem,
            device_id=target(*move), device_id_type=pl.DeviceIdType.MESH,
        )

    fine_copies = {}
    for move in y_moves:
        dx, dy = move
        if dx == 0:
            source, landing, in_sem = y_send.at[(dy + 1) // 2], y_recv.at[(1 - dy) // 2], side_in_sem
        else:
            source = y_send.at[(dy + 1) // 2, pl.ds(0 if dx < 0 else part - REACH, REACH)]
            landing, in_sem = corner_recv.at[(1 - dx) // 2, (1 - dy) // 2], corner_in_sem
        plan(fine_copies, move, source, landing, in_sem)
    near, far = REACH // 2, REACH - REACH // 2
    near_copies, far_copies = {}, {}
    for dx in (-1, 1):
        low = dx < 0
        for copies, start, count, in_sem in (
            (near_copies, 0 if low else far, near, near_in), (far_copies, near if low else 0, far, far_in)
        ):
            source = x_ref.at[pl.ds(start if low else rows - REACH + start, count)]
            landing = x_recv.at[0 if low else 1, pl.ds(start, count)]
            plan(copies, (dx, 0), source, landing, in_sem)

    def coarse_copies(main, wide_in, strips, in_sem, dz):
        row_out, row_in, side_out, side_in, corner_out, corner_in = strips
        copies = {}
        for dx, dy in PLANE if dz else AROUND:
            towards_x, towards_y = (dx + 1) // 2, (dy + 1) // 2
            if dx == 0 and dy == 0:
                source, landing = main, wide_in.at[pl.ds(COARSE_REACH, part_c), pl.ds(FRONT, cols_c)]
            elif dy == 0:
                source, landing = row_out.at[towards_x], row_in.at[towards_x, pl.ds(FRONT, cols_c)]
            elif dx == 0:
                source, landing = side_out.at[towards_y], side_in.at[towards_y]
            else:
                source, landing = corner_out.at[towards_x, towards_y], corner_in.at[towards_x, towards_y]
            plan(copies, (dx, dy), source, landing, in_sem, dz)
        return copies

    old_strips, new_strips = strip_refs[:6], strip_refs[6:]
    old_copies = coarse_copies(None, old_wide, old_strips, old_in, 0)
    chain_copies = coarse_copies(sent, new_wide, new_strips, chain_in, 1)

    lane = lax.broadcasted_iota(jnp.int32, (1, LANES), 1)
    pack = lane // levels

    def packed(row):
        return jnp.concatenate([row] * packs, axis=1)

    def advance(source, row, start, count, consts):
        keep, spread, along_x, along_y = consts
        centre = source[row, pl.ds(start, count), :]
        east = source[row + 1, pl.ds(start, count), :]
        west = source[row - 1, pl.ds(start, count), :]
        north = source[row, pl.ds(start + 1, count), :]
        south = source[row, pl.ds(start - 1, count), :]
        pushed = along_x * (east - west) + along_y * (north - south)
        return centre * (keep - pushed) + spread * ((east + west) + (north + south))

    def native_row(x):
        if x < 0:
            return x_recv[1, x + REACH]
        if x >= rows:
            return x_recv[0, x - rows]
        return x_ref[x]

    def bring_in(row):
        stacked = jnp.concatenate([native_row(p * part + row - REACH) for p in range(packs)], axis=0)
        first[row, pl.ds(FRONT, cols), :] = stacked.T

    low_lanes = lane < levels
    high_lanes = lane >= LANES - levels
    pl.semaphore_wait(barrier, awaited)

    @pl.when(tm > 0)
    def _():
        pl.semaphore_signal(ready, inc=1, device_id=target(-1, 0, 0), device_id_type=pl.DeviceIdType.MESH)

    pltpu.make_async_copy(small_ref, small_ref, small_sem).wait()
    diffuse = packed(small_ref[0:1, :])
    east_wind = packed(small_ref[1:2, :])
    north_wind = packed(small_ref[2:3, :])

    def constants(factor):
        spread = (time_step * factor) * diffuse
        return 1.0 - 4.0 * spread, spread, (0.5 * time_step) * east_wind, (0.5 * time_step) * north_wind

    fine_constants = constants(1.0)
    coarse_constants = constants(0.25)

    def load_done(group, group_rows):
        whole = x_ref.at[pl.ds(0, packs * len(group_rows))]
        pltpu.make_async_copy(whole, whole, load_sems.at[group]).wait()

    def bring_own(group_rows):
        for row in group_rows:
            bring_in(REACH + row)
            y_send[0, row] = first[REACH + row, pl.ds(FRONT, REACH), :]
            y_send[1, row] = first[REACH + row, pl.ds(end - REACH, REACH), :]

    load_done(0, rows_first)
    bring_own(rows_first)
    send_all(fine_copies, 0, corner_moves)
    send_all(near_copies, 0, x_moves)
    load_done(1, rows_later)
    bring_own(rows_later)
    send_all(fine_copies, 0, side_moves)

    def restricted(source, row):
        total = source[REACH + row * RATIO, pl.ds(FRONT, cols), :]
        for r in range(1, RATIO):
            total = total + source[REACH + row * RATIO + r, pl.ds(FRONT, cols), :]
        fine_line[...] = total
        mean = fine_line[pl.ds(0, cols_c, stride=RATIO), :]
        for o in range(1, RATIO):
            mean = mean + fine_line[pl.ds(o, cols_c, stride=RATIO), :]
        return mean * (1.0 / RATIO**2)

    def swapped(value):
        return pltpu.roll(value, levels, 1)

    def pack_strips(row_of, strips):
        row_out, _, side_out, _, corner_out, _ = strips
        row_out[0] = jnp.where(low_lanes, row_of(0, 0, cols_c), swapped(row_of(1, 0, cols_c)))
        row_out[1] = jnp.where(low_lanes, swapped(row_of(part_c - 2, 0, cols_c)), row_of(part_c - 1, 0, cols_c))
        for side, col in ((0, 0), (1, cols_c - COARSE_REACH)):
            for row in range(part_c):
                side_out[side, pl.ds(COARSE_REACH * row, COARSE_REACH), :] = row_of(row, col, COARSE_REACH)
            for towards in range(2):
                corner_out[towards, side] = row_out[towards, pl.ds(col, COARSE_REACH), :]

    def old_row(row, col, count):
        return old_wide[COARSE_REACH + row, pl.ds(FRONT + col, count), :]

    for row in range(part_c):
        old_wide[COARSE_REACH + row, pl.ds(FRONT, cols_c), :] = restricted(first, row)
    pack_strips(old_row, old_strips)
    send_all(old_copies, 0, AROUND)
    send_all(far_copies, 0, x_moves)

    def inside_x(row, reach, length):
        place = (gx * packs + pack) * length + (row - reach)
        return jnp.logical_and(place >= 0, place < n_gx * packs * length)

    def inside_y(start, count, length):
        place = gy * length + (start - FRONT) + lax.broadcasted_iota(jnp.int32, (count, LANES), 0)
        return jnp.logical_and(place >= 0, place < n_gy * length)

    edges = ((FRONT - EDGE, inside_y(FRONT - EDGE, EDGE, cols)), (end, inside_y(end, EDGE, cols)))
    reaches = ((FRONT - REACH, inside_y(FRONT - REACH, REACH, cols)), (end, inside_y(end, REACH, cols)))
    half = cols // 2

    def fill(source, dest, row, start, count, consts):
        dest[row, pl.ds(start, count), :] = advance(source, row, start, count, consts)

    def fill_edges(source, dest, row, consts):
        for start, mask in edges:
            value = advance(source, row, start, EDGE, consts)
            dest[row, pl.ds(start, EDGE), :] = jnp.where(mask, value, 0.0)

    def update(source, dest, row, consts, last):
        for start, count in ((FRONT, half), (FRONT + half, cols - half)):
            fill(source, dest, row, start, count, consts)
        if not last:
            fill_edges(source, dest, row, consts)

    buffers = (first, second)

    def inner_steps(row_update):
        for step in range(1, SUB + 1):
            def inner_row(row, step=step):
                row_update(buffers[(step - 1) % 2], buffers[step % 2], row, step)

            pl.loop(REACH + step, REACH + part - step, unroll=2)(inner_row)

    def centre_update(source, dest, row, step):
        fill(source, dest, row, FRONT + EDGE * step, half - EDGE * step, fine_constants)
        fill(source, dest, row, FRONT + half, cols - half - EDGE * step, fine_constants)

    def sides_update(source, dest, row, step):
        fill(source, dest, row, FRONT, EDGE * step, fine_constants)
        fill(source, dest, row, end - EDGE * step, EDGE * step, fine_constants)
        if step < SUB:
            fill_edges(source, dest, row, fine_constants)

    fill_missing(fine_copies, side_moves)
    fill_missing(fine_copies, corner_moves)
    fill_missing(near_copies, x_moves)
    fill_missing(far_copies, x_moves)
    fill_missing(old_copies, AROUND)
    inner_steps(centre_update)
    all_arrived(fine_copies, side_in_sem, side_moves)
    for side, (start, mask) in enumerate(reaches):
        for row in range(part):
            first[REACH + row, pl.ds(start, REACH), :] = jnp.where(mask, y_recv[side, row], 0.0)
    inner_steps(sides_update)

    def bring_halo(halo_rows):
        for row in halo_rows:
            bring_in(row)
            inner = first[row, pl.ds(FRONT, cols), :]
            first[row, pl.ds(FRONT, cols), :] = jnp.where(inside_x(row, REACH, part), inner, 0.0)
        for side, (start, mask_side) in enumerate(reaches):
            for row in halo_rows:
                if row < REACH:
                    here = jnp.where(high_lanes, corner_recv[0, side, row], y_recv[side, row + part - REACH])
                    here = pltpu.roll(here, levels, 1)
                else:
                    at = row - part - REACH
                    here = pltpu.roll(jnp.where(low_lanes, corner_recv[1, side, at], y_recv[side, at]), LANES - levels, 1)
                mask = jnp.logical_and(mask_side, inside_x(row, REACH, part))
                first[row, pl.ds(start, REACH), :] = jnp.where(mask, here, 0.0)

    def outer_steps(low_shift, high_shift, count):
        for step in range(1, SUB + 1):
            def outer_row(k, step=step):
                for row in (step + low_shift + k, part + REACH - step + high_shift + k):
                    mask_x = inside_x(row, REACH, part)
                    consts = tuple(jnp.where(mask_x, c, 0.0) for c in fine_constants)
                    update(buffers[(step - 1) % 2], buffers[step % 2], row, consts, step == SUB)

            pl.loop(0, count)(outer_row)

    all_arrived(near_copies, near_in, x_moves)
    all_arrived(fine_copies, corner_in_sem, corner_moves)
    bring_halo([*range(far, REACH), *range(REACH + part, REACH + part + near)])
    outer_steps(far, 0, near)

    count_c = cols_c + 2 * EDGE
    begin_c = FRONT - EDGE
    mask_y = inside_y(begin_c, count_c, cols_c)

    def extend(buffer, strips):
        _, row_in, _, side_in, _, corner_in = strips
        for side, col in ((0, end_c), (1, FRONT - COARSE_REACH)):
            for row in range(part_c):
                buffer[COARSE_REACH + row, pl.ds(col, COARSE_REACH), :] = side_in[
                    side, pl.ds(COARSE_REACH * row, COARSE_REACH), :
                ]
            for towards in range(2):
                row_in[towards, pl.ds(col, COARSE_REACH), :] = corner_in[towards, side]

        def own(row):
            return buffer[COARSE_REACH + row, pl.ds(begin_c, count_c), :]

        above, below = (row_in[towards, pl.ds(begin_c, count_c), :] for towards in (0, 1))
        values = [
            jnp.where(low_lanes, below, swapped(own(part_c - 2))),
            swapped(jnp.where(high_lanes, below, own(part_c - 1))),
            *[own(row) for row in range(part_c)],
            swapped(jnp.where(low_lanes, above, own(0))),
            jnp.where(high_lanes, above, swapped(own(1))),
        ]
        for row, value in enumerate(values):
            mask = mask_y
            if not COARSE_REACH <= row < COARSE_REACH + part_c:
                mask = jnp.logical_and(mask_y, inside_x(row, COARSE_REACH, part_c))
            extended[row, pl.ds(begin_c, count_c), :] = jnp.where(mask, value, 0.0)

    all_arrived(old_copies, old_in, AROUND)
    extend(old_wide, old_strips)
    for row in range(1, wide_c - 1):
        old_image[row - 1] = advance(extended, row, begin_c, count_c, coarse_constants)


    def compute_change():
        for row in range(1, wide_c - 1):
            moved = advance(extended, row, begin_c, count_c, coarse_constants) - old_image[row - 1]
            mask = jnp.logical_and(mask_y, inside_x(row, COARSE_REACH, part_c))
            change[row - 1, pl.ds(begin_c, count_c), :] = jnp.where(mask, moved, 0.0)

    def change_row(row):
        return change[row, pl.ds(begin_c, count_c), :]

    def smoothed(row):
        line[pl.ds(begin_c, count_c), :] = (
            mean_side * (change_row(row) + change_row(row + 2)) + mean_mid * change_row(row + 1)
        )
        sides = line[pl.ds(FRONT - 1, cols_c), :] + line[pl.ds(FRONT + 1, cols_c), :]
        return mean_side * sides + mean_mid * line[pl.ds(FRONT, cols_c), :]

    @pl.when(tm == 0)
    def _():
        compute_change()
        for row in range(part_c):
            sent[row] = smoothed(row)

    all_arrived(far_copies, far_in, x_moves)
    bring_halo([*range(far), *range(REACH + part + near, wide)])
    outer_steps(0, near, far)
    fine = buffers[SUB % 2]

    for row in range(part_c):
        fine_mean[row] = restricted(fine, row)

    def write_fine():
        for row in range(part):
            turned[row] = fine[REACH + row, pl.ds(FRONT, cols), :].T

    def pass_on():
        pl.semaphore_wait(ready, 1)
        pack_strips(lambda row, col, count: sent[row, pl.ds(col, count), :], new_strips)
        send_all(chain_copies, 1, AROUND)
        send_all(chain_copies, 1, ((0, 0),))

    @pl.when(jnp.logical_and(tm == 0, tm < n_tm - 1))
    def _():
        for row in range(part_c):
            sent[row] = fine_mean[row] + sent[row]
        pass_on()

    @pl.when(tm > 0)
    def _():
        fill_missing(chain_copies, AROUND)

    write_fine()

    @pl.when(tm > 0)
    def _():
        all_arrived(chain_copies, chain_in, PLANE)
        extend(new_wide, new_strips)
        compute_change()

    @pl.when(jnp.logical_and(tm > 0, tm < n_tm - 1))
    def _():
        for row in range(part_c):
            sent[row] = fine_mean[row] + smoothed(row)
        pass_on()

    sends_done(fine_copies, 0, y_moves)
    sends_done(old_copies, 0, AROUND)
    sends_done(near_copies, 0, x_moves)
    sends_done(far_copies, 0, x_moves)
    pl.when(tm < n_tm - 1)(lambda: sends_done(chain_copies, 1, PLANE))


def closing(levels, rows, turned, change, out_hbm, filled, spread_rows, sem):
    packs = LANES // levels
    part, _, cols = turned.shape
    part_c = part // RATIO
    count_c = cols // RATIO + 2 * EDGE
    coarse_col = lax.broadcasted_iota(jnp.int32, (count_c, cols), 0) - EDGE
    fine_col = lax.broadcasted_iota(jnp.int32, (count_c, cols), 1)
    offset_of = fine_col & (RATIO - 1)
    apart = coarse_col - (fine_col >> (RATIO.bit_length() - 1))
    spreading = jnp.zeros((count_c, cols), jnp.float32)
    for o in range(RATIO):
        for distance, weights in ((-1, weights_low), (0, weights_mid), (1, weights_high)):
            chosen = jnp.logical_and(offset_of == o, apart == distance)
            spreading = jnp.where(chosen, weights[o], spreading)
    spreading = jnp.concatenate([spreading.astype(jnp.bfloat16)] * 3, axis=0)
    def spread_row(row):
        rest, pieces = change[row, pl.ds(FRONT - EDGE, count_c), :], []
        for _ in range(3):
            piece = rest.astype(jnp.bfloat16).astype(jnp.float32)
            pieces.append(piece)
            rest = rest - piece
        split = jnp.concatenate(pieces, axis=0).T.astype(jnp.bfloat16)
        return jnp.dot(split, spreading, preferred_element_type=jnp.float32)

    for row in range(2):
        spread_rows[row] = spread_row(row)
    for row in range(part):
        at, o = row // RATIO, row % RATIO
        if o == 0:
            spread_rows[at + 2] = spread_row(at + 2)
        total = turned[row] + weights_mid[o] * spread_rows[at + 1]
        if weights_low[o]:
            total = total + weights_low[o] * spread_rows[at]
        if weights_high[o]:
            total = total + weights_high[o] * spread_rows[at + 2]
        filled[row] = total
        for p in range(packs):
            x = p * part + row
            pltpu.make_async_copy(filled.at[row, pl.ds(p * levels, levels)], out_hbm.at[:, x], sem).start()
    pltpu.make_async_copy(filled, filled, sem).wait()


def shards(sizes, state_starts, diffusivity, wind):
    _, levels, rows, cols = state_starts.shape
    packs = LANES // levels
    if packs != 2 or levels * packs != LANES:
        raise ValueError(levels)
    part = rows // packs
    part_c = part // RATIO
    cols_c = cols // RATIO
    wide, wide_c = part + 2 * REACH, part_c + 2 * COARSE_REACH
    vmem = functools.partial(pltpu.VMEM, dtype=jnp.float32)
    scratch = [
        vmem((rows, levels, cols)),
        vmem((3, levels)),
        pltpu.SemaphoreType.DMA((2,)),
        pltpu.SemaphoreType.DMA,
        pltpu.SemaphoreType.REGULAR,
        vmem((wide, cols + 2 * FRONT, LANES)),
        vmem((wide, cols + 2 * FRONT, LANES)),
        vmem((2, REACH, levels, cols)),
        vmem((2, part, REACH, LANES)),
        vmem((2, part, REACH, LANES)),
        vmem((2, 2, REACH, REACH, LANES)),
        vmem((wide_c, cols_c + 2 * FRONT, LANES)),
        vmem((wide_c, cols_c + 2 * FRONT, LANES)),
        vmem((wide_c, cols_c + 2 * FRONT, LANES)),
        vmem((wide_c - 2, cols_c + 2 * EDGE, LANES)),
        vmem((part_c, cols_c, LANES)),
        vmem((part_c, cols_c, LANES)),
        vmem((cols_c + 2 * FRONT, LANES)),
        vmem((cols, LANES)),
        vmem((TALLY, LANES)),
    ] + [pltpu.SemaphoreType.DMA] * 7
    scratch += [
        vmem((2, cols_c, LANES)),
        vmem((2, cols_c + 2 * FRONT, LANES)),
        vmem((2, COARSE_REACH * part_c, LANES)),
        vmem((2, COARSE_REACH * part_c, LANES)),
        vmem((2, 2, COARSE_REACH, LANES)),
        vmem((2, 2, COARSE_REACH, LANES)),
    ] * 2
    in_vmem = pl.BlockSpec(memory_space=pltpu.VMEM)
    handed = pl.pallas_call(
        functools.partial(kernel, sizes, levels, rows, cols),
        out_shape=(vmem((part, LANES, cols)), vmem((part_c + 2, cols_c + 2 * FRONT, LANES))),
        in_specs=[pl.BlockSpec(memory_space=pl.ANY)] * 3,
        out_specs=(in_vmem, in_vmem),
        scratch_shapes=scratch,
        compiler_params=pltpu.CompilerParams(collective_id=0, has_side_effects=True),
        name="parareal",
    )(state_starts.reshape(levels, rows, cols), diffusivity.reshape(1, levels), wind)
    ending = pl.pallas_call(
        functools.partial(closing, levels, rows),
        out_shape=jax.ShapeDtypeStruct((levels, rows, cols), jnp.float32),
        in_specs=[in_vmem, in_vmem],
        out_specs=pl.BlockSpec(memory_space=pl.ANY),
        scratch_shapes=[
            vmem((part, LANES, cols)),
            vmem((part_c + 2, LANES, cols)),
            pltpu.SemaphoreType.DMA,
        ],
        name="closing",
    )(*(pltpu.with_memory_space_constraint(array, pltpu.VMEM) for array in handed))
    return ending.reshape(1, levels, rows, cols)


def solution(mesh):
    sizes = tuple(mesh.shape[axis] for axis in ("tm", "gx", "gy"))
    placed = (P("tm", None, "gx", "gy"), P(), P())
    return jax.shard_map(
        functools.partial(shards, sizes),
        mesh=mesh, in_specs=placed, out_specs=P("tm", None, "gx", "gy"), check_vma=False,
    )
```

```python
import functools
import math

import jax
import jax.numpy as jnp
from jax import lax
from jax.experimental import pallas as pl
from jax.experimental.pallas import tpu as pltpu
from jax.sharding import PartitionSpec as P

SUB = 4
REACH = SUB
RATIO = 4
LANES = 128
EDGE = 8
FRONT = 2 * EDGE
COARSE_REACH = 2
LONG_REACH = 2 * COARSE_REACH
TALLY = 1024

time_step = 0.2
weights_low = (0.375, 0.125, 0.0, 0.0)
weights_mid = (0.625, 0.875, 0.875, 0.625)
weights_high = (0.0, 0.0, 0.125, 0.375)
mean_side, mean_mid = 0.125, 0.75

PLANE = tuple((dx, dy) for dx in (-1, 0, 1) for dy in (-1, 0, 1))
AROUND = tuple(d for d in PLANE if d != (0, 0))
x_moves = tuple(d for d in AROUND if d[1] == 0)
y_moves = tuple(d for d in AROUND if d[1] != 0)
side_moves = tuple(d for d in y_moves if d[0] == 0)
corner_moves = tuple(d for d in y_moves if d[0] != 0)


def conjunction(conditions):
    total = True
    for condition in conditions:
        total = condition if total is True else jnp.logical_and(total, condition)
    return total


def kernel(
    sizes, levels, rows, cols,
    x_hbm, diff_hbm, wind_hbm, turned, change,
    x_ref, small_ref, load_sems, small_sem, ready,
    first, second, x_recv, y_send, y_recv, corner_recv,
    old_own, new_own, prior_old_own, prior_new_own, extended, long_extended, old_image, prior_image, prior_change, lift,
    sent, fine_mean, line, fine_line, tally,
    out_sem, near_in, far_in, side_in_sem, corner_in_sem, old_in, chain_in, prior_old_in, prior_new_in, *strip_refs,
):
    n_tm, n_gx, n_gy = sizes
    tm, gx, gy = lax.axis_index("tm"), lax.axis_index("gx"), lax.axis_index("gy")
    packs = LANES // levels
    part = rows // packs
    part_c = part // RATIO
    cols_c = cols // RATIO
    wide = part + 2 * REACH
    wide_c = part_c + 2 * COARSE_REACH
    end = FRONT + cols
    end_c = FRONT + cols_c

    def there(dz, dx, dy):
        tests = []
        for place, move, count in ((tm, dz, n_tm), (gx, dx, n_gx), (gy, dy, n_gy)):
            if move < 0:
                tests.append(place >= -move)
            if move > 0:
                tests.append(place < count - move)
        return conjunction(tests)

    def guarded(condition, action):
        if condition is True:
            action()
        else:
            pl.when(condition)(action)

    def target(dz, dx, dy):
        return (tm + dz, gx + dx, gy + dy)

    rows_first = [*range(REACH), *range(part - REACH, part)]
    rows_later = [*range(REACH, part - REACH)]
    for group, group_rows in enumerate((rows_first, rows_later)):
        for row in group_rows:
            for x in range(row, rows, part):
                pltpu.make_async_copy(x_hbm.at[:, x], x_ref.at[x], load_sems.at[group]).start()
    for source, landing in ((diff_hbm, small_ref.at[pl.ds(0, 1)]), (wind_hbm, small_ref.at[pl.ds(1, 2)])):
        pltpu.make_async_copy(source, landing, small_sem).start()

    barrier = pltpu.get_barrier_semaphore()
    odd = tm % 2 == 1
    partners = [(0, dx, dy) for dx, dy in AROUND] + [(dz, 0, 0) for dz in (-1, 1, -2, 2)]
    partners.sort(key=lambda move: -sum(map(abs, move)))
    awaited = jnp.int32(0)
    for move in partners:
        def greet(move=move):
            pl.semaphore_signal(barrier, inc=1, device_id=target(*move), device_id_type=pl.DeviceIdType.MESH)
        met = jnp.logical_and(odd, there(*move)) if abs(move[0]) == 2 else there(*move)
        guarded(met, greet)
        awaited = awaited + met.astype(jnp.int32)

    def send_all(copies, dz, moves):
        for move in moves:
            guarded(there(dz, *move), lambda move=move: copies[move].start())

    def sends_done(copies, dz, moves):
        for move in moves:
            guarded(there(dz, *move), lambda move=move: copies[move].wait_send())

    stand_ins, sizes_in_rows = {}, {}

    def fill_missing(copies, moves):
        for dx, dy in moves:
            @pl.when(jnp.logical_not(there(0, -dx, -dy)))
            def _(dx=dx, dy=dy):
                pltpu.make_async_copy(*stand_ins[id(copies)][dx, dy]).start()

    def all_arrived(copies, in_sem, moves):
        height = sum(sizes_in_rows[id(copies)][move] for move in moves)
        whole = tally.at[pl.ds(0, height)]
        pltpu.make_async_copy(whole, whole, in_sem).wait()

    def plan(copies, move, source, landing, in_sem, dz=0):
        copies[move] = remote(source, landing, in_sem, (dz, *move))
        stand_ins.setdefault(id(copies), {})[move] = (source, landing, in_sem)
        sizes_in_rows.setdefault(id(copies), {})[move] = math.prod(source.shape[:-1])

    def remote(source, landing, in_sem, move):
        return pltpu.make_async_remote_copy(
            src_ref=source, dst_ref=landing, send_sem=out_sem, recv_sem=in_sem,
            device_id=target(*move), device_id_type=pl.DeviceIdType.MESH,
        )

    fine_copies = {}
    for move in y_moves:
        dx, dy = move
        if dx == 0:
            source, landing, in_sem = y_send.at[(dy + 1) // 2], y_recv.at[(1 - dy) // 2], side_in_sem
        else:
            source = y_send.at[(dy + 1) // 2, pl.ds(0 if dx < 0 else part - REACH, REACH)]
            landing, in_sem = corner_recv.at[(1 - dx) // 2, (1 - dy) // 2], corner_in_sem
        plan(fine_copies, move, source, landing, in_sem)
    near, far = REACH // 2, REACH - REACH // 2
    near_copies, far_copies = {}, {}
    for dx in (-1, 1):
        low = dx < 0
        for copies, start, count, in_sem in (
            (near_copies, 0 if low else far, near, near_in), (far_copies, near if low else 0, far, far_in)
        ):
            source = x_ref.at[pl.ds(start if low else rows - REACH + start, count)]
            landing = x_recv.at[0 if low else 1, pl.ds(start, count)]
            plan(copies, (dx, 0), source, landing, in_sem)

    def coarse_copies(main, own_in, strips, in_sem, dz):
        row_out, row_in, side_out, side_in, corner_out, corner_in = strips
        copies = {}
        for dx, dy in PLANE if dz else AROUND:
            towards_x, towards_y = (dx + 1) // 2, (dy + 1) // 2
            if dx == 0 and dy == 0:
                source, landing = main, own_in.at[:, pl.ds(FRONT, cols_c)]
            elif dy == 0:
                source, landing = row_out.at[towards_x], row_in.at[towards_x, :, pl.ds(FRONT, cols_c)]
            elif dx == 0:
                source, landing = side_out.at[towards_y], side_in.at[towards_y]
            else:
                source, landing = corner_out.at[towards_x, towards_y], corner_in.at[towards_x, towards_y]
            plan(copies, (dx, dy), source, landing, in_sem, dz)
        return copies

    old_strips, new_strips, prior_old_strips, prior_new_strips = (strip_refs[6 * k : 6 * k + 6] for k in range(4))
    old_main = old_own.at[:, pl.ds(FRONT, cols_c)]
    old_copies = coarse_copies(None, old_own, old_strips, old_in, 0)
    chain_copies = coarse_copies(sent, new_own, new_strips, chain_in, 1)
    prior_old_copies = coarse_copies(old_main, prior_old_own, prior_old_strips, prior_old_in, 1)
    prior_new_copies = coarse_copies(sent, prior_new_own, prior_new_strips, prior_new_in, 2)
    has_next, has_second = tm < n_tm - 1, tm < n_tm - 2

    lane = lax.broadcasted_iota(jnp.int32, (1, LANES), 1)
    pack = lane // levels

    def packed(row):
        return jnp.concatenate([row] * packs, axis=1)

    def advance(source, row, start, count, consts):
        keep, spread, along_x, along_y = consts
        centre = source[row, pl.ds(start, count), :]
        east = source[row + 1, pl.ds(start, count), :]
        west = source[row - 1, pl.ds(start, count), :]
        north = source[row, pl.ds(start + 1, count), :]
        south = source[row, pl.ds(start - 1, count), :]
        pushed = along_x * (east - west) + along_y * (north - south)
        return centre * (keep - pushed) + spread * ((east + west) + (north + south))

    def native_row(x):
        if x < 0:
            return x_recv[1, x + REACH]
        if x >= rows:
            return x_recv[0, x - rows]
        return x_ref[x]

    def bring_in(row):
        stacked = jnp.concatenate([native_row(p * part + row - REACH) for p in range(packs)], axis=0)
        first[row, pl.ds(FRONT, cols), :] = stacked.T

    low_lanes = lane < levels
    high_lanes = lane >= LANES - levels
    pl.semaphore_wait(barrier, awaited)

    @pl.when(tm > 0)
    def _():
        pl.semaphore_signal(ready, inc=1, device_id=target(-1, 0, 0), device_id_type=pl.DeviceIdType.MESH)

    @pl.when(jnp.logical_and(odd, tm > 1))
    def _():
        pl.semaphore_signal(ready, inc=1, device_id=target(-2, 0, 0), device_id_type=pl.DeviceIdType.MESH)

    pltpu.make_async_copy(small_ref, small_ref, small_sem).wait()
    diffuse = packed(small_ref[0:1, :])
    east_wind = packed(small_ref[1:2, :])
    north_wind = packed(small_ref[2:3, :])

    def constants(factor):
        spread = (time_step * factor) * diffuse
        return 1.0 - 4.0 * spread, spread, (0.5 * time_step) * east_wind, (0.5 * time_step) * north_wind

    fine_constants = constants(1.0)
    coarse_constants = constants(0.25)

    def load_done(group, group_rows):
        whole = x_ref.at[pl.ds(0, packs * len(group_rows))]
        pltpu.make_async_copy(whole, whole, load_sems.at[group]).wait()

    def bring_own(group_rows):
        for row in group_rows:
            bring_in(REACH + row)
            y_send[0, row] = first[REACH + row, pl.ds(FRONT, REACH), :]
            y_send[1, row] = first[REACH + row, pl.ds(end - REACH, REACH), :]

    load_done(0, rows_first)
    bring_own(rows_first)
    send_all(fine_copies, 0, corner_moves)
    send_all(near_copies, 0, x_moves)
    send_all(far_copies, 0, x_moves)
    load_done(1, rows_later)
    bring_own(rows_later)
    send_all(fine_copies, 0, side_moves)

    def restricted(source, row):
        total = source[REACH + row * RATIO, pl.ds(FRONT, cols), :]
        for r in range(1, RATIO):
            total = total + source[REACH + row * RATIO + r, pl.ds(FRONT, cols), :]
        fine_line[...] = total
        mean = fine_line[pl.ds(0, cols_c, stride=RATIO), :]
        for o in range(1, RATIO):
            mean = mean + fine_line[pl.ds(o, cols_c, stride=RATIO), :]
        return mean * (1.0 / RATIO**2)

    def swapped(value):
        return pltpu.roll(value, levels, 1)

    def pack_strips(row_of, strips, reach):
        row_out, _, side_out, _, corner_out, _ = strips
        for k in range(reach // 2):
            after, before = 2 * k, part_c - 2 * k - 2
            row_out[0, k] = jnp.where(low_lanes, row_of(after, 0, cols_c), swapped(row_of(after + 1, 0, cols_c)))
            row_out[1, k] = jnp.where(low_lanes, swapped(row_of(before, 0, cols_c)), row_of(before + 1, 0, cols_c))
        for side, col in ((0, 0), (1, cols_c - reach)):
            for row in range(part_c):
                side_out[side, row] = row_of(row, col, reach)
            for towards in range(2):
                for k in range(reach // 2):
                    corner_out[towards, side, k] = row_out[towards, k, pl.ds(col, reach), :]

    def old_row(row, col, count):
        return old_own[row, pl.ds(FRONT + col, count), :]

    def sent_row(row, col, count):
        return sent[row, pl.ds(col, count), :]

    for row in range(part_c):
        old_own[row, pl.ds(FRONT, cols_c), :] = restricted(first, row)
    pack_strips(old_row, old_strips, COARSE_REACH)
    send_all(old_copies, 0, AROUND)

    def inside_x(row, reach, length):
        place = (gx * packs + pack) * length + (row - reach)
        return jnp.logical_and(place >= 0, place < n_gx * packs * length)

    def inside_y(start, count, length):
        place = gy * length + (start - FRONT) + lax.broadcasted_iota(jnp.int32, (count, LANES), 0)
        return jnp.logical_and(place >= 0, place < n_gy * length)

    edges = ((FRONT - EDGE, inside_y(FRONT - EDGE, EDGE, cols)), (end, inside_y(end, EDGE, cols)))
    reaches = ((FRONT - REACH, inside_y(FRONT - REACH, REACH, cols)), (end, inside_y(end, REACH, cols)))
    half = cols // 2

    def fill(source, dest, row, start, count, consts):
        dest[row, pl.ds(start, count), :] = advance(source, row, start, count, consts)

    def fill_edges(source, dest, row, consts):
        for start, mask in edges:
            value = advance(source, row, start, EDGE, consts)
            dest[row, pl.ds(start, EDGE), :] = jnp.where(mask, value, 0.0)

    def update(source, dest, row, consts, last):
        for start, count in ((FRONT, half), (FRONT + half, cols - half)):
            fill(source, dest, row, start, count, consts)
        if not last:
            fill_edges(source, dest, row, consts)

    buffers = (first, second)

    def inner_steps(row_update):
        for step in range(1, SUB + 1):
            def inner_row(row, step=step):
                row_update(buffers[(step - 1) % 2], buffers[step % 2], row, step)

            pl.loop(REACH + step, REACH + part - step, unroll=2)(inner_row)

    def centre_update(source, dest, row, step):
        fill(source, dest, row, FRONT + EDGE * step, half - EDGE * step, fine_constants)
        fill(source, dest, row, FRONT + half, cols - half - EDGE * step, fine_constants)

    def sides_update(source, dest, row, step):
        fill(source, dest, row, FRONT, EDGE * step, fine_constants)
        fill(source, dest, row, end - EDGE * step, EDGE * step, fine_constants)
        if step < SUB:
            fill_edges(source, dest, row, fine_constants)

    fill_missing(fine_copies, side_moves)
    fill_missing(fine_copies, corner_moves)
    fill_missing(near_copies, x_moves)
    fill_missing(far_copies, x_moves)
    fill_missing(old_copies, AROUND)
    inner_steps(centre_update)
    all_arrived(fine_copies, side_in_sem, side_moves)
    for side, (start, mask) in enumerate(reaches):
        for row in range(part):
            first[REACH + row, pl.ds(start, REACH), :] = jnp.where(mask, y_recv[side, row], 0.0)
    inner_steps(sides_update)

    @pl.when(odd)
    def _():
        fill_missing(prior_old_copies, AROUND)

    @pl.when(jnp.logical_and(jnp.logical_not(odd), has_next))
    def _():
        pl.semaphore_wait(ready, 1)
        pack_strips(old_row, prior_old_strips, LONG_REACH)
        send_all(prior_old_copies, 1, PLANE)

    def bring_halo(halo_rows):
        for row in halo_rows:
            bring_in(row)
            inner = first[row, pl.ds(FRONT, cols), :]
            first[row, pl.ds(FRONT, cols), :] = jnp.where(inside_x(row, REACH, part), inner, 0.0)
        for side, (start, mask_side) in enumerate(reaches):
            for row in halo_rows:
                if row < REACH:
                    here = jnp.where(high_lanes, corner_recv[0, side, row], y_recv[side, row + part - REACH])
                    here = pltpu.roll(here, levels, 1)
                else:
                    at = row - part - REACH
                    here = pltpu.roll(jnp.where(low_lanes, corner_recv[1, side, at], y_recv[side, at]), LANES - levels, 1)
                mask = jnp.logical_and(mask_side, inside_x(row, REACH, part))
                first[row, pl.ds(start, REACH), :] = jnp.where(mask, here, 0.0)

    def outer_steps(low_shift, high_shift, count):
        for step in range(1, SUB + 1):
            def outer_row(k, step=step):
                for row in (step + low_shift + k, part + REACH - step + high_shift + k):
                    mask_x = inside_x(row, REACH, part)
                    consts = tuple(jnp.where(mask_x, c, 0.0) for c in fine_constants)
                    update(buffers[(step - 1) % 2], buffers[step % 2], row, consts, step == SUB)

            pl.loop(0, count)(outer_row)

    all_arrived(near_copies, near_in, x_moves)
    all_arrived(fine_copies, corner_in_sem, corner_moves)
    bring_halo([*range(far, REACH), *range(REACH + part, REACH + part + near)])
    outer_steps(far, 0, near)

    all_arrived(far_copies, far_in, x_moves)
    bring_halo([*range(far), *range(REACH + part + near, wide)])
    outer_steps(0, near, far)
    fine = buffers[SUB % 2]

    for row in range(part_c):
        fine_mean[row] = restricted(fine, row)

    @pl.when(jnp.logical_and(jnp.logical_not(odd), has_next))
    def _():
        for row in range(part_c):
            sent[row] = fine_mean[row]
        pack_strips(sent_row, new_strips, COARSE_REACH)
        send_all(chain_copies, 1, AROUND)
        send_all(chain_copies, 1, ((0, 0),))

    count_c = cols_c + 2 * EDGE
    begin_c = FRONT - EDGE
    across = pl.ds(begin_c, count_c)
    mask_y = inside_y(begin_c, count_c, cols_c)

    def extend(buffer, strips, target, reach):
        _, row_in, _, side_in, _, corner_in = strips
        for side, col in ((0, end_c), (1, FRONT - reach)):
            for row in range(part_c):
                buffer[row, pl.ds(col, reach), :] = side_in[side, row]
            for towards in range(2):
                for k in range(reach // 2):
                    row_in[towards, k, pl.ds(col, reach), :] = corner_in[towards, side, k]

        def own(row):
            return buffer[row, across, :]

        values = [own(row) for row in range(part_c)]
        for k in range(reach // 2):
            above, below = (row_in[towards, k, across, :] for towards in (0, 1))
            after, before = 2 * k, part_c - 2 * k - 2
            values = [
                jnp.where(low_lanes, below, swapped(own(before))),
                swapped(jnp.where(high_lanes, below, own(before + 1))),
                *values,
                swapped(jnp.where(low_lanes, above, own(after))),
                jnp.where(high_lanes, above, swapped(own(after + 1))),
            ]
        for row, value in enumerate(values):
            mask = mask_y
            if not reach <= row < reach + part_c:
                mask = jnp.logical_and(mask_y, inside_x(row, reach, part_c))
            target[row, across, :] = jnp.where(mask, value, 0.0)

    def image_of(source, image):
        for row in range(image.shape[0]):
            image[row] = advance(source, row + 1, begin_c, count_c, coarse_constants)

    def change_of(source, image, reach, result):
        for row in range(image.shape[0]):
            moved = advance(source, row + 1, begin_c, count_c, coarse_constants) - image[row]
            mask = jnp.logical_and(mask_y, inside_x(row + 1, reach, part_c))
            result[row, across, :] = jnp.where(mask, moved, 0.0)

    def smoothed(source, row, start, count):
        line[across, :] = (
            mean_side * (source[row, across, :] + source[row + 2, across, :]) + mean_mid * source[row + 1, across, :]
        )
        sides = line[pl.ds(start - 1, count), :] + line[pl.ds(start + 1, count), :]
        return mean_side * sides + mean_mid * line[pl.ds(start, count), :]

    def find_lift():
        change_of(long_extended, prior_image, LONG_REACH, prior_change)
        for row in range(wide_c):
            mask = jnp.logical_and(mask_y, inside_x(row, COARSE_REACH, part_c))
            lift[row] = jnp.where(mask, smoothed(prior_change, row, begin_c, count_c), 0.0)

    all_arrived(old_copies, old_in, AROUND)
    extend(old_own, old_strips, extended, COARSE_REACH)
    image_of(extended, old_image)
    pl.when(tm == 0)(lambda: change_of(extended, old_image, COARSE_REACH, change))

    @pl.when(tm > 0)
    def _():
        fill_missing(chain_copies, AROUND)

    @pl.when(jnp.logical_and(odd, tm > 1))
    def _():
        fill_missing(prior_new_copies, AROUND)

    @pl.when(odd)
    def _():
        all_arrived(prior_old_copies, prior_old_in, PLANE)
        extend(prior_old_own, prior_old_strips, long_extended, LONG_REACH)
        image_of(long_extended, prior_image)

    pl.when(tm == 1)(find_lift)

    for row in range(part):
        turned[row] = fine[REACH + row, pl.ds(FRONT, cols), :].T

    @pl.when(tm > 0)
    def _():
        all_arrived(chain_copies, chain_in, PLANE)
        extend(new_own, new_strips, extended, COARSE_REACH)

    @pl.when(jnp.logical_and(odd, tm > 1))
    def _():
        all_arrived(prior_new_copies, prior_new_in, PLANE)
        extend(prior_new_own, prior_new_strips, long_extended, LONG_REACH)
        find_lift()

    @pl.when(odd)
    def _():
        for row in range(wide_c):
            extended[row, across, :] = extended[row, across, :] + lift[row]

    pl.when(tm > 0)(lambda: change_of(extended, old_image, COARSE_REACH, change))

    @pl.when(jnp.logical_and(odd, has_next))
    def _():
        for row in range(part_c):
            sent[row] = fine_mean[row] + smoothed(change, row, FRONT, cols_c)
        pl.semaphore_wait(ready, 1 + has_second.astype(jnp.int32))

        @pl.when(has_second)
        def _():
            pack_strips(sent_row, prior_new_strips, LONG_REACH)
            send_all(prior_new_copies, 2, AROUND)
            send_all(prior_new_copies, 2, ((0, 0),))

        pack_strips(sent_row, new_strips, COARSE_REACH)
        send_all(chain_copies, 1, AROUND)
        send_all(chain_copies, 1, ((0, 0),))

    sends_done(fine_copies, 0, y_moves)
    sends_done(old_copies, 0, AROUND)
    sends_done(near_copies, 0, x_moves)
    sends_done(far_copies, 0, x_moves)
    pl.when(has_next)(lambda: sends_done(chain_copies, 1, PLANE))
    pl.when(jnp.logical_and(jnp.logical_not(odd), has_next))(lambda: sends_done(prior_old_copies, 1, PLANE))
    pl.when(jnp.logical_and(odd, has_second))(lambda: sends_done(prior_new_copies, 2, PLANE))


def closing(levels, rows, turned, change, out_hbm, filled, spread_rows, sem):
    packs = LANES // levels
    part, _, cols = turned.shape
    part_c = part // RATIO
    count_c = cols // RATIO + 2 * EDGE
    coarse_col = lax.broadcasted_iota(jnp.int32, (count_c, cols), 0) - EDGE
    fine_col = lax.broadcasted_iota(jnp.int32, (count_c, cols), 1)
    offset_of = fine_col & (RATIO - 1)
    apart = coarse_col - (fine_col >> (RATIO.bit_length() - 1))
    spreading = jnp.zeros((count_c, cols), jnp.float32)
    for o in range(RATIO):
        for distance, weights in ((-1, weights_low), (0, weights_mid), (1, weights_high)):
            chosen = jnp.logical_and(offset_of == o, apart == distance)
            spreading = jnp.where(chosen, weights[o], spreading)
    spreading = jnp.concatenate([spreading.astype(jnp.bfloat16)] * 3, axis=0)
    def spread_row(row):
        rest, pieces = change[row, pl.ds(FRONT - EDGE, count_c), :], []
        for _ in range(3):
            piece = rest.astype(jnp.bfloat16).astype(jnp.float32)
            pieces.append(piece)
            rest = rest - piece
        split = jnp.concatenate(pieces, axis=0).T.astype(jnp.bfloat16)
        return jnp.dot(split, spreading, preferred_element_type=jnp.float32)

    for row in range(2):
        spread_rows[row] = spread_row(row)
    for row in range(part):
        at, o = row // RATIO, row % RATIO
        if o == 0:
            spread_rows[at + 2] = spread_row(at + 2)
        total = turned[row] + weights_mid[o] * spread_rows[at + 1]
        if weights_low[o]:
            total = total + weights_low[o] * spread_rows[at]
        if weights_high[o]:
            total = total + weights_high[o] * spread_rows[at + 2]
        filled[row] = total
        for p in range(packs):
            x = p * part + row
            pltpu.make_async_copy(filled.at[row, pl.ds(p * levels, levels)], out_hbm.at[:, x], sem).start()
    pltpu.make_async_copy(filled, filled, sem).wait()


def shards(sizes, state_starts, diffusivity, wind):
    _, levels, rows, cols = state_starts.shape
    packs = LANES // levels
    if packs != 2 or levels * packs != LANES:
        raise ValueError(levels)
    part = rows // packs
    part_c = part // RATIO
    cols_c = cols // RATIO
    wide, wide_c, wide_long = part + 2 * REACH, part_c + 2 * COARSE_REACH, part_c + 2 * LONG_REACH
    if part_c < LONG_REACH:
        raise ValueError(part_c)
    vmem = functools.partial(pltpu.VMEM, dtype=jnp.float32)
    scratch = [
        vmem((rows, levels, cols)),
        vmem((3, levels)),
        pltpu.SemaphoreType.DMA((2,)),
        pltpu.SemaphoreType.DMA,
        pltpu.SemaphoreType.REGULAR,
        vmem((wide, cols + 2 * FRONT, LANES)),
        vmem((wide, cols + 2 * FRONT, LANES)),
        vmem((2, REACH, levels, cols)),
        vmem((2, part, REACH, LANES)),
        vmem((2, part, REACH, LANES)),
        vmem((2, 2, REACH, REACH, LANES)),
        *[vmem((part_c, cols_c + 2 * FRONT, LANES))] * 4,
        vmem((wide_c, cols_c + 2 * FRONT, LANES)),
        vmem((wide_long, cols_c + 2 * FRONT, LANES)),
        vmem((wide_c - 2, cols_c + 2 * EDGE, LANES)),
        vmem((wide_long - 2, cols_c + 2 * EDGE, LANES)),
        vmem((wide_long - 2, cols_c + 2 * FRONT, LANES)),
        vmem((wide_c, cols_c + 2 * EDGE, LANES)),
        vmem((part_c, cols_c, LANES)),
        vmem((part_c, cols_c, LANES)),
        vmem((cols_c + 2 * FRONT, LANES)),
        vmem((cols, LANES)),
        vmem((TALLY, LANES)),
    ] + [pltpu.SemaphoreType.DMA] * 9
    for reach in (COARSE_REACH, COARSE_REACH, LONG_REACH, LONG_REACH):
        scratch += [
            vmem((2, reach // 2, cols_c, LANES)),
            vmem((2, reach // 2, cols_c + 2 * FRONT, LANES)),
            vmem((2, part_c, reach, LANES)),
            vmem((2, part_c, reach, LANES)),
            vmem((2, 2, reach // 2, reach, LANES)),
            vmem((2, 2, reach // 2, reach, LANES)),
        ]
    in_vmem = pl.BlockSpec(memory_space=pltpu.VMEM)
    handed = pl.pallas_call(
        functools.partial(kernel, sizes, levels, rows, cols),
        out_shape=(vmem((part, LANES, cols)), vmem((part_c + 2, cols_c + 2 * FRONT, LANES))),
        in_specs=[pl.BlockSpec(memory_space=pl.ANY)] * 3,
        out_specs=(in_vmem, in_vmem),
        scratch_shapes=scratch,
        compiler_params=pltpu.CompilerParams(collective_id=0, has_side_effects=True),
        name="parareal",
    )(state_starts.reshape(levels, rows, cols), diffusivity.reshape(1, levels), wind)
    ending = pl.pallas_call(
        functools.partial(closing, levels, rows),
        out_shape=jax.ShapeDtypeStruct((levels, rows, cols), jnp.float32),
        in_specs=[in_vmem, in_vmem],
        out_specs=pl.BlockSpec(memory_space=pl.ANY),
        scratch_shapes=[
            vmem((part, LANES, cols)),
            vmem((part_c + 2, LANES, cols)),
            pltpu.SemaphoreType.DMA,
        ],
        name="closing",
    )(*(pltpu.with_memory_space_constraint(array, pltpu.VMEM) for array in handed))
    return ending.reshape(1, levels, rows, cols)


def solution(mesh):
    sizes = tuple(mesh.shape[axis] for axis in ("tm", "gx", "gy"))
    placed = (P("tm", None, "gx", "gy"), P(), P())
    return jax.shard_map(
        functools.partial(shards, sizes),
        mesh=mesh, in_specs=placed, out_specs=P("tm", None, "gx", "gy"), check_vma=False,
    )
```

```python
import functools
import math

import jax
import jax.numpy as jnp
from jax import lax
from jax.experimental import pallas as pl
from jax.experimental.pallas import tpu as pltpu
from jax.sharding import PartitionSpec as P

SUB = 4
REACH = SUB
RATIO = 4
LANES = 128
EDGE = 8
FRONT = 2 * EDGE
COARSE_REACH = 2
LONG_REACH = 2 * COARSE_REACH
TALLY = 1024

time_step = 0.2
weights_low = (0.375, 0.125, 0.0, 0.0)
weights_mid = (0.625, 0.875, 0.875, 0.625)
weights_high = (0.0, 0.0, 0.125, 0.375)
mean_side, mean_mid = 0.125, 0.75

PLANE = tuple((dx, dy) for dx in (-1, 0, 1) for dy in (-1, 0, 1))
AROUND = tuple(d for d in PLANE if d != (0, 0))
x_moves = tuple(d for d in AROUND if d[1] == 0)
y_moves = tuple(d for d in AROUND if d[1] != 0)
side_moves = tuple(d for d in y_moves if d[0] == 0)
corner_moves = tuple(d for d in y_moves if d[0] != 0)


def conjunction(conditions):
    total = True
    for condition in conditions:
        total = condition if total is True else jnp.logical_and(total, condition)
    return total


def kernel(
    sizes, levels, rows, cols,
    x_hbm, diff_hbm, wind_hbm, turned, change,
    x_ref, small_ref, load_sems, small_sem, ready,
    first, second, x_recv, y_send, y_recv, corner_recv,
    old_own, new_own, prior_old_own, prior_new_own, extended, long_extended, old_image, prior_image, prior_change, lift,
    sent, fine_mean, line, fine_line, tally,
    out_sem, near_in, far_in, side_in_sem, corner_in_sem, old_in, chain_in, prior_old_in, prior_new_in, *strip_refs,
):
    n_tm, n_gx, n_gy = sizes
    tm, gx, gy = lax.axis_index("tm"), lax.axis_index("gx"), lax.axis_index("gy")
    packs = LANES // levels
    part = rows // packs
    part_c = part // RATIO
    cols_c = cols // RATIO
    wide = part + 2 * REACH
    wide_c = part_c + 2 * COARSE_REACH
    end = FRONT + cols
    end_c = FRONT + cols_c

    def there(dz, dx, dy):
        tests = []
        for place, move, count in ((tm, dz, n_tm), (gx, dx, n_gx), (gy, dy, n_gy)):
            if move < 0:
                tests.append(place >= -move)
            if move > 0:
                tests.append(place < count - move)
        return conjunction(tests)

    def guarded(condition, action):
        if condition is True:
            action()
        else:
            pl.when(condition)(action)

    def target(dz, dx, dy):
        return (tm + dz, gx + dx, gy + dy)

    rows_first = [*range(REACH), *range(part - REACH, part)]
    rows_later = [*range(REACH, part - REACH)]
    for group, group_rows in enumerate((rows_first, rows_later)):
        for row in group_rows:
            for x in range(row, rows, part):
                pltpu.make_async_copy(x_hbm.at[:, x], x_ref.at[x], load_sems.at[group]).start()
    for source, landing in ((diff_hbm, small_ref.at[pl.ds(0, 1)]), (wind_hbm, small_ref.at[pl.ds(1, 2)])):
        pltpu.make_async_copy(source, landing, small_sem).start()

    barrier = pltpu.get_barrier_semaphore()
    partners = [(0, dx, dy) for dx, dy in AROUND] + [(-1, 0, 0), (1, 0, 0)]
    partners.sort(key=lambda move: -sum(map(abs, move)))
    awaited = jnp.int32(0)
    for move in partners:
        def greet(move=move):
            pl.semaphore_signal(barrier, inc=1, device_id=target(*move), device_id_type=pl.DeviceIdType.MESH)
        guarded(there(*move), greet)
        awaited = awaited + there(*move).astype(jnp.int32)

    def send_all(copies, dz, moves):
        for move in moves:
            guarded(there(dz, *move), lambda move=move: copies[move].start())

    def sends_done(copies, dz, moves):
        for move in moves:
            guarded(there(dz, *move), lambda move=move: copies[move].wait_send())

    stand_ins, sizes_in_rows = {}, {}

    def fill_missing(copies, moves):
        for dx, dy in moves:
            @pl.when(jnp.logical_not(there(0, -dx, -dy)))
            def _(dx=dx, dy=dy):
                pltpu.make_async_copy(*stand_ins[id(copies)][dx, dy]).start()

    def all_arrived(copies, in_sem, moves):
        height = sum(sizes_in_rows[id(copies)][move] for move in moves)
        whole = tally.at[pl.ds(0, height)]
        pltpu.make_async_copy(whole, whole, in_sem).wait()

    def plan(copies, move, source, landing, in_sem, dz=0):
        copies[move] = remote(source, landing, in_sem, (dz, *move))
        stand_ins.setdefault(id(copies), {})[move] = (source, landing, in_sem)
        sizes_in_rows.setdefault(id(copies), {})[move] = math.prod(source.shape[:-1])

    def remote(source, landing, in_sem, move):
        return pltpu.make_async_remote_copy(
            src_ref=source, dst_ref=landing, send_sem=out_sem, recv_sem=in_sem,
            device_id=target(*move), device_id_type=pl.DeviceIdType.MESH,
        )

    fine_copies = {}
    for move in y_moves:
        dx, dy = move
        if dx == 0:
            source, landing, in_sem = y_send.at[(dy + 1) // 2], y_recv.at[(1 - dy) // 2], side_in_sem
        else:
            source = y_send.at[(dy + 1) // 2, pl.ds(0 if dx < 0 else part - REACH, REACH)]
            landing, in_sem = corner_recv.at[(1 - dx) // 2, (1 - dy) // 2], corner_in_sem
        plan(fine_copies, move, source, landing, in_sem)
    near, far = REACH // 2, REACH - REACH // 2
    near_copies, far_copies = {}, {}
    for dx in (-1, 1):
        low = dx < 0
        for copies, start, count, in_sem in (
            (near_copies, 0 if low else far, near, near_in), (far_copies, near if low else 0, far, far_in)
        ):
            source = x_ref.at[pl.ds(start if low else rows - REACH + start, count)]
            landing = x_recv.at[0 if low else 1, pl.ds(start, count)]
            plan(copies, (dx, 0), source, landing, in_sem)

    def coarse_copies(main, own_in, strips, in_sem, dz):
        row_out, row_in, side_out, side_in, corner_out, corner_in = strips
        copies = {}
        for dx, dy in PLANE if dz else AROUND:
            towards_x, towards_y = (dx + 1) // 2, (dy + 1) // 2
            if dx == 0 and dy == 0:
                source, landing = main, own_in.at[:, pl.ds(FRONT, cols_c)]
            elif dy == 0:
                source, landing = row_out.at[towards_x], row_in.at[towards_x, :, pl.ds(FRONT, cols_c)]
            elif dx == 0:
                source, landing = side_out.at[towards_y], side_in.at[towards_y]
            else:
                source, landing = corner_out.at[towards_x, towards_y], corner_in.at[towards_x, towards_y]
            plan(copies, (dx, dy), source, landing, in_sem, dz)
        return copies

    old_strips, new_strips, prior_old_strips, prior_new_strips = (strip_refs[6 * k : 6 * k + 6] for k in range(4))
    old_main = old_own.at[:, pl.ds(FRONT, cols_c)]
    old_copies = coarse_copies(None, old_own, old_strips, old_in, 0)
    chain_copies = coarse_copies(fine_mean, new_own, new_strips, chain_in, 1)
    prior_old_copies = coarse_copies(old_main, prior_old_own, prior_old_strips, prior_old_in, 1)
    prior_new_copies = coarse_copies(sent, prior_new_own, prior_new_strips, prior_new_in, 2)
    has_next, has_second = tm < n_tm - 1, tm < n_tm - 2

    lane = lax.broadcasted_iota(jnp.int32, (1, LANES), 1)
    pack = lane // levels

    def packed(row):
        return jnp.concatenate([row] * packs, axis=1)

    def advance(source, row, start, count, consts):
        keep, spread, along_x, along_y = consts
        centre = source[row, pl.ds(start, count), :]
        east = source[row + 1, pl.ds(start, count), :]
        west = source[row - 1, pl.ds(start, count), :]
        north = source[row, pl.ds(start + 1, count), :]
        south = source[row, pl.ds(start - 1, count), :]
        pushed = along_x * (east - west) + along_y * (north - south)
        return centre * (keep - pushed) + spread * ((east + west) + (north + south))

    def native_row(x):
        if x < 0:
            return x_recv[1, x + REACH]
        if x >= rows:
            return x_recv[0, x - rows]
        return x_ref[x]

    def bring_in(row):
        stacked = jnp.concatenate([native_row(p * part + row - REACH) for p in range(packs)], axis=0)
        first[row, pl.ds(FRONT, cols), :] = stacked.T

    low_lanes = lane < levels
    high_lanes = lane >= LANES - levels
    pl.semaphore_wait(barrier, awaited)

    def say_ready(k):
        @pl.when(tm > 0)
        def _():
            pl.semaphore_signal(
                ready.at[k], inc=1, device_id=target(-1, 0, 0), device_id_type=pl.DeviceIdType.MESH
            )

    say_ready(0)
    pltpu.make_async_copy(small_ref, small_ref, small_sem).wait()
    diffuse = packed(small_ref[0:1, :])
    east_wind = packed(small_ref[1:2, :])
    north_wind = packed(small_ref[2:3, :])

    def constants(factor):
        spread = (time_step * factor) * diffuse
        return 1.0 - 4.0 * spread, spread, (0.5 * time_step) * east_wind, (0.5 * time_step) * north_wind

    fine_constants = constants(1.0)
    coarse_constants = constants(0.25)

    def load_done(group, group_rows):
        whole = x_ref.at[pl.ds(0, packs * len(group_rows))]
        pltpu.make_async_copy(whole, whole, load_sems.at[group]).wait()

    def bring_own(group_rows):
        for row in group_rows:
            bring_in(REACH + row)
            y_send[0, row] = first[REACH + row, pl.ds(FRONT, REACH), :]
            y_send[1, row] = first[REACH + row, pl.ds(end - REACH, REACH), :]

    load_done(0, rows_first)
    bring_own(rows_first)
    send_all(fine_copies, 0, corner_moves)
    send_all(near_copies, 0, x_moves)
    send_all(far_copies, 0, x_moves)
    load_done(1, rows_later)
    bring_own(rows_later)
    send_all(fine_copies, 0, side_moves)

    def restricted(source, row):
        total = source[REACH + row * RATIO, pl.ds(FRONT, cols), :]
        for r in range(1, RATIO):
            total = total + source[REACH + row * RATIO + r, pl.ds(FRONT, cols), :]
        fine_line[...] = total
        mean = fine_line[pl.ds(0, cols_c, stride=RATIO), :]
        for o in range(1, RATIO):
            mean = mean + fine_line[pl.ds(o, cols_c, stride=RATIO), :]
        return mean * (1.0 / RATIO**2)

    def swapped(value):
        return pltpu.roll(value, levels, 1)

    def pack_strips(row_of, strips, reach):
        row_out, _, side_out, _, corner_out, _ = strips
        for k in range(reach // 2):
            after, before = 2 * k, part_c - 2 * k - 2
            row_out[0, k] = jnp.where(low_lanes, row_of(after, 0, cols_c), swapped(row_of(after + 1, 0, cols_c)))
            row_out[1, k] = jnp.where(low_lanes, swapped(row_of(before, 0, cols_c)), row_of(before + 1, 0, cols_c))
        for side, col in ((0, 0), (1, cols_c - reach)):
            for row in range(part_c):
                side_out[side, row] = row_of(row, col, reach)
            for towards in range(2):
                for k in range(reach // 2):
                    corner_out[towards, side, k] = row_out[towards, k, pl.ds(col, reach), :]

    def old_row(row, col, count):
        return old_own[row, pl.ds(FRONT + col, count), :]

    for row in range(part_c):
        old_own[row, pl.ds(FRONT, cols_c), :] = restricted(first, row)
    pack_strips(old_row, old_strips, COARSE_REACH)
    send_all(old_copies, 0, AROUND)

    def inside_x(row, reach, length):
        place = (gx * packs + pack) * length + (row - reach)
        return jnp.logical_and(place >= 0, place < n_gx * packs * length)

    def inside_y(start, count, length):
        place = gy * length + (start - FRONT) + lax.broadcasted_iota(jnp.int32, (count, LANES), 0)
        return jnp.logical_and(place >= 0, place < n_gy * length)

    edges = ((FRONT - EDGE, inside_y(FRONT - EDGE, EDGE, cols)), (end, inside_y(end, EDGE, cols)))
    reaches = ((FRONT - REACH, inside_y(FRONT - REACH, REACH, cols)), (end, inside_y(end, REACH, cols)))
    half = cols // 2

    def fill(source, dest, row, start, count, consts):
        dest[row, pl.ds(start, count), :] = advance(source, row, start, count, consts)

    def fill_edges(source, dest, row, consts):
        for start, mask in edges:
            value = advance(source, row, start, EDGE, consts)
            dest[row, pl.ds(start, EDGE), :] = jnp.where(mask, value, 0.0)

    def update(source, dest, row, consts, last):
        for start, count in ((FRONT, half), (FRONT + half, cols - half)):
            fill(source, dest, row, start, count, consts)
        if not last:
            fill_edges(source, dest, row, consts)

    buffers = (first, second)

    def inner_steps(row_update):
        for step in range(1, SUB + 1):
            def inner_row(row, step=step):
                row_update(buffers[(step - 1) % 2], buffers[step % 2], row, step)

            pl.loop(REACH + step, REACH + part - step, unroll=2)(inner_row)

    def centre_update(source, dest, row, step):
        fill(source, dest, row, FRONT + EDGE * step, half - EDGE * step, fine_constants)
        fill(source, dest, row, FRONT + half, cols - half - EDGE * step, fine_constants)

    def sides_update(source, dest, row, step):
        fill(source, dest, row, FRONT, EDGE * step, fine_constants)
        fill(source, dest, row, end - EDGE * step, EDGE * step, fine_constants)
        if step < SUB:
            fill_edges(source, dest, row, fine_constants)

    fill_missing(fine_copies, side_moves)
    fill_missing(fine_copies, corner_moves)
    fill_missing(near_copies, x_moves)
    fill_missing(far_copies, x_moves)
    fill_missing(old_copies, AROUND)
    inner_steps(centre_update)

    @pl.when(has_next)
    def _():
        pl.semaphore_wait(ready.at[0], 1)
        say_ready(1)
        pack_strips(old_row, prior_old_strips, LONG_REACH)
        send_all(prior_old_copies, 1, PLANE)

    @pl.when(tm > 0)
    def _():
        fill_missing(prior_old_copies, AROUND)

    all_arrived(fine_copies, side_in_sem, side_moves)
    for side, (start, mask) in enumerate(reaches):
        for row in range(part):
            first[REACH + row, pl.ds(start, REACH), :] = jnp.where(mask, y_recv[side, row], 0.0)
    inner_steps(sides_update)

    def bring_halo(halo_rows):
        for row in halo_rows:
            bring_in(row)
            inner = first[row, pl.ds(FRONT, cols), :]
            first[row, pl.ds(FRONT, cols), :] = jnp.where(inside_x(row, REACH, part), inner, 0.0)
        for side, (start, mask_side) in enumerate(reaches):
            for row in halo_rows:
                if row < REACH:
                    here = jnp.where(high_lanes, corner_recv[0, side, row], y_recv[side, row + part - REACH])
                    here = pltpu.roll(here, levels, 1)
                else:
                    at = row - part - REACH
                    here = pltpu.roll(jnp.where(low_lanes, corner_recv[1, side, at], y_recv[side, at]), LANES - levels, 1)
                mask = jnp.logical_and(mask_side, inside_x(row, REACH, part))
                first[row, pl.ds(start, REACH), :] = jnp.where(mask, here, 0.0)

    def outer_steps(low_shift, high_shift, count):
        for step in range(1, SUB + 1):
            def outer_row(k, step=step):
                for row in (step + low_shift + k, part + REACH - step + high_shift + k):
                    mask_x = inside_x(row, REACH, part)
                    consts = tuple(jnp.where(mask_x, c, 0.0) for c in fine_constants)
                    update(buffers[(step - 1) % 2], buffers[step % 2], row, consts, step == SUB)

            pl.loop(0, count)(outer_row)

    all_arrived(near_copies, near_in, x_moves)
    all_arrived(fine_copies, corner_in_sem, corner_moves)
    bring_halo([*range(far, REACH), *range(REACH + part, REACH + part + near)])
    outer_steps(far, 0, near)

    all_arrived(far_copies, far_in, x_moves)
    bring_halo([*range(far), *range(REACH + part + near, wide)])
    outer_steps(0, near, far)
    fine = buffers[SUB % 2]

    for row in range(part_c):
        fine_mean[row] = restricted(fine, row)

    @pl.when(has_next)
    def _():
        pack_strips(lambda row, col, count: fine_mean[row, pl.ds(col, count), :], new_strips, COARSE_REACH)
        send_all(chain_copies, 1, AROUND)
        send_all(chain_copies, 1, ((0, 0),))

    count_c = cols_c + 2 * EDGE
    begin_c = FRONT - EDGE
    across = pl.ds(begin_c, count_c)
    mask_y = inside_y(begin_c, count_c, cols_c)

    def extend(buffer, strips, target, reach):
        _, row_in, _, side_in, _, corner_in = strips
        for side, col in ((0, end_c), (1, FRONT - reach)):
            for row in range(part_c):
                buffer[row, pl.ds(col, reach), :] = side_in[side, row]
            for towards in range(2):
                for k in range(reach // 2):
                    row_in[towards, k, pl.ds(col, reach), :] = corner_in[towards, side, k]

        def own(row):
            return buffer[row, across, :]

        values = [own(row) for row in range(part_c)]
        for k in range(reach // 2):
            above, below = (row_in[towards, k, across, :] for towards in (0, 1))
            after, before = 2 * k, part_c - 2 * k - 2
            values = [
                jnp.where(low_lanes, below, swapped(own(before))),
                swapped(jnp.where(high_lanes, below, own(before + 1))),
                *values,
                swapped(jnp.where(low_lanes, above, own(after))),
                jnp.where(high_lanes, above, swapped(own(after + 1))),
            ]
        for row, value in enumerate(values):
            mask = mask_y
            if not reach <= row < reach + part_c:
                mask = jnp.logical_and(mask_y, inside_x(row, reach, part_c))
            target[row, across, :] = jnp.where(mask, value, 0.0)

    def image_of(source, image):
        for row in range(image.shape[0]):
            image[row] = advance(source, row + 1, begin_c, count_c, coarse_constants)

    def change_of(source, image, reach, result):
        for row in range(image.shape[0]):
            moved = advance(source, row + 1, begin_c, count_c, coarse_constants) - image[row]
            mask = jnp.logical_and(mask_y, inside_x(row + 1, reach, part_c))
            result[row, across, :] = jnp.where(mask, moved, 0.0)

    def smoothed(source, row, start, count):
        line[across, :] = (
            mean_side * (source[row, across, :] + source[row + 2, across, :]) + mean_mid * source[row + 1, across, :]
        )
        sides = line[pl.ds(start - 1, count), :] + line[pl.ds(start + 1, count), :]
        return mean_side * sides + mean_mid * line[pl.ds(start, count), :]

    def find_lift():
        change_of(long_extended, prior_image, LONG_REACH, prior_change)
        for row in range(wide_c):
            mask = jnp.logical_and(mask_y, inside_x(row, COARSE_REACH, part_c))
            lift[row] = jnp.where(mask, smoothed(prior_change, row, begin_c, count_c), 0.0)

    all_arrived(old_copies, old_in, AROUND)
    extend(old_own, old_strips, extended, COARSE_REACH)
    image_of(extended, old_image)
    def send_on():
        for row in range(part_c):
            sent[row] = fine_mean[row] + smoothed(change, row, FRONT, cols_c)
        pack_strips(lambda row, col, count: sent[row, pl.ds(col, count), :], prior_new_strips, LONG_REACH)
        pl.semaphore_wait(ready.at[1], 1)
        send_all(prior_new_copies, 2, AROUND)
        send_all(prior_new_copies, 2, ((0, 0),))

    @pl.when(tm == 0)
    def _():
        change_of(extended, old_image, COARSE_REACH, change)
        pl.when(has_second)(send_on)

    @pl.when(tm > 0)
    def _():
        fill_missing(chain_copies, AROUND)

    @pl.when(tm > 1)
    def _():
        fill_missing(prior_new_copies, AROUND)

    for row in range(part):
        turned[row] = fine[REACH + row, pl.ds(FRONT, cols), :].T

    @pl.when(tm > 0)
    def _():
        all_arrived(prior_old_copies, prior_old_in, PLANE)
        extend(prior_old_own, prior_old_strips, long_extended, LONG_REACH)
        image_of(long_extended, prior_image)
        pl.when(tm == 1)(find_lift)
        all_arrived(chain_copies, chain_in, PLANE)
        extend(new_own, new_strips, extended, COARSE_REACH)

        @pl.when(tm > 1)
        def _():
            all_arrived(prior_new_copies, prior_new_in, PLANE)
            extend(prior_new_own, prior_new_strips, long_extended, LONG_REACH)
            find_lift()

        for row in range(wide_c):
            extended[row, across, :] = extended[row, across, :] + lift[row]
        change_of(extended, old_image, COARSE_REACH, change)
        pl.when(has_second)(send_on)

    sends_done(fine_copies, 0, y_moves)
    sends_done(old_copies, 0, AROUND)
    sends_done(near_copies, 0, x_moves)
    sends_done(far_copies, 0, x_moves)
    @pl.when(has_next)
    def _():
        sends_done(chain_copies, 1, PLANE)
        sends_done(prior_old_copies, 1, PLANE)

    pl.when(has_second)(lambda: sends_done(prior_new_copies, 2, PLANE))


def closing(levels, rows, turned, change, out_hbm, filled, spread_rows, sem):
    packs = LANES // levels
    part, _, cols = turned.shape
    part_c = part // RATIO
    count_c = cols // RATIO + 2 * EDGE
    coarse_col = lax.broadcasted_iota(jnp.int32, (count_c, cols), 0) - EDGE
    fine_col = lax.broadcasted_iota(jnp.int32, (count_c, cols), 1)
    offset_of = fine_col & (RATIO - 1)
    apart = coarse_col - (fine_col >> (RATIO.bit_length() - 1))
    spreading = jnp.zeros((count_c, cols), jnp.float32)
    for o in range(RATIO):
        for distance, weights in ((-1, weights_low), (0, weights_mid), (1, weights_high)):
            chosen = jnp.logical_and(offset_of == o, apart == distance)
            spreading = jnp.where(chosen, weights[o], spreading)
    spreading = jnp.concatenate([spreading.astype(jnp.bfloat16)] * 3, axis=0)
    def spread_row(row):
        rest, pieces = change[row, pl.ds(FRONT - EDGE, count_c), :], []
        for _ in range(3):
            piece = rest.astype(jnp.bfloat16).astype(jnp.float32)
            pieces.append(piece)
            rest = rest - piece
        split = jnp.concatenate(pieces, axis=0).T.astype(jnp.bfloat16)
        return jnp.dot(split, spreading, preferred_element_type=jnp.float32)

    for row in range(2):
        spread_rows[row] = spread_row(row)
    for row in range(part):
        at, o = row // RATIO, row % RATIO
        if o == 0:
            spread_rows[at + 2] = spread_row(at + 2)
        total = turned[row] + weights_mid[o] * spread_rows[at + 1]
        if weights_low[o]:
            total = total + weights_low[o] * spread_rows[at]
        if weights_high[o]:
            total = total + weights_high[o] * spread_rows[at + 2]
        filled[row] = total
        for p in range(packs):
            x = p * part + row
            pltpu.make_async_copy(filled.at[row, pl.ds(p * levels, levels)], out_hbm.at[:, x], sem).start()
    pltpu.make_async_copy(filled, filled, sem).wait()


def shards(sizes, state_starts, diffusivity, wind):
    _, levels, rows, cols = state_starts.shape
    packs = LANES // levels
    if packs != 2 or levels * packs != LANES:
        raise ValueError(levels)
    part = rows // packs
    part_c = part // RATIO
    cols_c = cols // RATIO
    wide, wide_c, wide_long = part + 2 * REACH, part_c + 2 * COARSE_REACH, part_c + 2 * LONG_REACH
    if part_c < LONG_REACH:
        raise ValueError(part_c)
    vmem = functools.partial(pltpu.VMEM, dtype=jnp.float32)
    scratch = [
        vmem((rows, levels, cols)),
        vmem((3, levels)),
        pltpu.SemaphoreType.DMA((2,)),
        pltpu.SemaphoreType.DMA,
        pltpu.SemaphoreType.REGULAR((2,)),
        vmem((wide, cols + 2 * FRONT, LANES)),
        vmem((wide, cols + 2 * FRONT, LANES)),
        vmem((2, REACH, levels, cols)),
        vmem((2, part, REACH, LANES)),
        vmem((2, part, REACH, LANES)),
        vmem((2, 2, REACH, REACH, LANES)),
        *[vmem((part_c, cols_c + 2 * FRONT, LANES))] * 4,
        vmem((wide_c, cols_c + 2 * FRONT, LANES)),
        vmem((wide_long, cols_c + 2 * FRONT, LANES)),
        vmem((wide_c - 2, cols_c + 2 * EDGE, LANES)),
        vmem((wide_long - 2, cols_c + 2 * EDGE, LANES)),
        vmem((wide_long - 2, cols_c + 2 * FRONT, LANES)),
        vmem((wide_c, cols_c + 2 * EDGE, LANES)),
        vmem((part_c, cols_c, LANES)),
        vmem((part_c, cols_c, LANES)),
        vmem((cols_c + 2 * FRONT, LANES)),
        vmem((cols, LANES)),
        vmem((TALLY, LANES)),
    ] + [pltpu.SemaphoreType.DMA] * 9
    for reach in (COARSE_REACH, COARSE_REACH, LONG_REACH, LONG_REACH):
        scratch += [
            vmem((2, reach // 2, cols_c, LANES)),
            vmem((2, reach // 2, cols_c + 2 * FRONT, LANES)),
            vmem((2, part_c, reach, LANES)),
            vmem((2, part_c, reach, LANES)),
            vmem((2, 2, reach // 2, reach, LANES)),
            vmem((2, 2, reach // 2, reach, LANES)),
        ]
    in_vmem = pl.BlockSpec(memory_space=pltpu.VMEM)
    handed = pl.pallas_call(
        functools.partial(kernel, sizes, levels, rows, cols),
        out_shape=(vmem((part, LANES, cols)), vmem((part_c + 2, cols_c + 2 * FRONT, LANES))),
        in_specs=[pl.BlockSpec(memory_space=pl.ANY)] * 3,
        out_specs=(in_vmem, in_vmem),
        scratch_shapes=scratch,
        compiler_params=pltpu.CompilerParams(collective_id=0, has_side_effects=True),
        name="parareal",
    )(state_starts.reshape(levels, rows, cols), diffusivity.reshape(1, levels), wind)
    ending = pl.pallas_call(
        functools.partial(closing, levels, rows),
        out_shape=jax.ShapeDtypeStruct((levels, rows, cols), jnp.float32),
        in_specs=[in_vmem, in_vmem],
        out_specs=pl.BlockSpec(memory_space=pl.ANY),
        scratch_shapes=[
            vmem((part, LANES, cols)),
            vmem((part_c + 2, LANES, cols)),
            pltpu.SemaphoreType.DMA,
        ],
        name="closing",
    )(*(pltpu.with_memory_space_constraint(array, pltpu.VMEM) for array in handed))
    return ending.reshape(1, levels, rows, cols)


def solution(mesh):
    sizes = tuple(mesh.shape[axis] for axis in ("tm", "gx", "gy"))
    placed = (P("tm", None, "gx", "gy"), P(), P())
    return jax.shard_map(
        functools.partial(shards, sizes),
        mesh=mesh, in_specs=placed, out_specs=P("tm", None, "gx", "gy"), check_vma=False,
    )
```

```python
import functools
import math

import jax
import jax.numpy as jnp
from jax import lax
from jax.experimental import pallas as pl
from jax.experimental.pallas import tpu as pltpu
from jax.sharding import PartitionSpec as P

SUB = 4
REACH = SUB
RATIO = 4
LANES = 128
EDGE = 8
FRONT = 2 * EDGE
COARSE_REACH = 2
LONG_REACH = 2 * COARSE_REACH
TALLY = 1024

time_step = 0.2
weights_low = (0.375, 0.125, 0.0, 0.0)
weights_mid = (0.625, 0.875, 0.875, 0.625)
weights_high = (0.0, 0.0, 0.125, 0.375)
mean_side, mean_mid = 0.125, 0.75

PLANE = tuple((dx, dy) for dx in (-1, 0, 1) for dy in (-1, 0, 1))
AROUND = tuple(d for d in PLANE if d != (0, 0))
x_moves = tuple(d for d in AROUND if d[1] == 0)
y_moves = tuple(d for d in AROUND if d[1] != 0)
side_moves = tuple(d for d in y_moves if d[0] == 0)
corner_moves = tuple(d for d in y_moves if d[0] != 0)


def conjunction(conditions):
    total = True
    for condition in conditions:
        total = condition if total is True else jnp.logical_and(total, condition)
    return total


def kernel(
    sizes, levels, rows, cols,
    x_hbm, diff_hbm, wind_hbm, turned, change,
    x_ref, small_ref, load_sems, small_sem, ready,
    first, second, x_recv, y_send, y_recv, corner_recv,
    old_own, new_own, prior_old_own, prior_new_own, extended, long_extended, old_image, prior_image, prior_change, lift,
    sent, fine_mean, line, fine_line, tally,
    out_sem, near_in, far_in, side_in_sem, corner_in_sem, old_in, chain_in, prior_old_in, prior_new_in, *strip_refs,
):
    n_tm, n_gx, n_gy = sizes
    tm, gx, gy = lax.axis_index("tm"), lax.axis_index("gx"), lax.axis_index("gy")
    packs = LANES // levels
    part = rows // packs
    part_c = part // RATIO
    cols_c = cols // RATIO
    wide = part + 2 * REACH
    wide_c = part_c + 2 * COARSE_REACH
    end = FRONT + cols
    end_c = FRONT + cols_c

    def there(dz, dx, dy):
        tests = []
        for place, move, count in ((tm, dz, n_tm), (gx, dx, n_gx), (gy, dy, n_gy)):
            if move < 0:
                tests.append(place >= -move)
            if move > 0:
                tests.append(place < count - move)
        return conjunction(tests)

    def guarded(condition, action):
        if condition is True:
            action()
        else:
            pl.when(condition)(action)

    def target(dz, dx, dy):
        return (tm + dz, gx + dx, gy + dy)

    rows_first = [*range(REACH), *range(part - REACH, part)]
    rows_later = [*range(REACH, part - REACH)]
    for group, group_rows in enumerate((rows_first, rows_later)):
        for row in group_rows:
            for x in range(row, rows, part):
                pltpu.make_async_copy(x_hbm.at[:, x], x_ref.at[x], load_sems.at[group]).start()
    for source, landing in ((diff_hbm, small_ref.at[pl.ds(0, 1)]), (wind_hbm, small_ref.at[pl.ds(1, 2)])):
        pltpu.make_async_copy(source, landing, small_sem).start()

    barrier = pltpu.get_barrier_semaphore()
    partners = [(0, dx, dy) for dx, dy in AROUND] + [(-1, 0, 0), (1, 0, 0)]
    partners.sort(key=lambda move: -sum(map(abs, move)))
    awaited = jnp.int32(0)
    for move in partners:
        def greet(move=move):
            pl.semaphore_signal(barrier, inc=1, device_id=target(*move), device_id_type=pl.DeviceIdType.MESH)
        guarded(there(*move), greet)
        awaited = awaited + there(*move).astype(jnp.int32)

    def send_all(copies, dz, moves):
        for move in moves:
            guarded(there(dz, *move), lambda move=move: copies[move].start())

    def sends_done(copies, dz, moves):
        for move in moves:
            guarded(there(dz, *move), lambda move=move: copies[move].wait_send())

    stand_ins, sizes_in_rows = {}, {}

    def fill_missing(copies, moves):
        for dx, dy in moves:
            @pl.when(jnp.logical_not(there(0, -dx, -dy)))
            def _(dx=dx, dy=dy):
                pltpu.make_async_copy(*stand_ins[id(copies)][dx, dy]).start()

    def all_arrived(copies, in_sem, moves):
        height = sum(sizes_in_rows[id(copies)][move] for move in moves)
        whole = tally.at[pl.ds(0, height)]
        pltpu.make_async_copy(whole, whole, in_sem).wait()

    def plan(copies, move, source, landing, in_sem, dz=0):
        copies[move] = remote(source, landing, in_sem, (dz, *move))
        stand_ins.setdefault(id(copies), {})[move] = (source, landing, in_sem)
        sizes_in_rows.setdefault(id(copies), {})[move] = math.prod(source.shape[:-1])

    def remote(source, landing, in_sem, move):
        return pltpu.make_async_remote_copy(
            src_ref=source, dst_ref=landing, send_sem=out_sem, recv_sem=in_sem,
            device_id=target(*move), device_id_type=pl.DeviceIdType.MESH,
        )

    fine_copies = {}
    for move in y_moves:
        dx, dy = move
        if dx == 0:
            source, landing, in_sem = y_send.at[(dy + 1) // 2], y_recv.at[(1 - dy) // 2], side_in_sem
        else:
            source = y_send.at[(dy + 1) // 2, pl.ds(0 if dx < 0 else part - REACH, REACH)]
            landing, in_sem = corner_recv.at[(1 - dx) // 2, (1 - dy) // 2], corner_in_sem
        plan(fine_copies, move, source, landing, in_sem)
    near, far = REACH // 2, REACH - REACH // 2
    near_copies, far_copies = {}, {}
    for dx in (-1, 1):
        low = dx < 0
        for copies, start, count, in_sem in (
            (near_copies, 0 if low else far, near, near_in), (far_copies, near if low else 0, far, far_in)
        ):
            source = x_ref.at[pl.ds(start if low else rows - REACH + start, count)]
            landing = x_recv.at[0 if low else 1, pl.ds(start, count)]
            plan(copies, (dx, 0), source, landing, in_sem)

    def coarse_copies(main, own_in, strips, in_sem, dz):
        row_out, row_in, side_out, side_in, corner_out, corner_in = strips
        copies = {}
        for dx, dy in PLANE if dz else AROUND:
            towards_x, towards_y = (dx + 1) // 2, (dy + 1) // 2
            if dx == 0 and dy == 0:
                source, landing = main, own_in.at[:, pl.ds(FRONT, cols_c)]
            elif dy == 0:
                source, landing = row_out.at[towards_x], row_in.at[towards_x, :, pl.ds(FRONT, cols_c)]
            elif dx == 0:
                source, landing = side_out.at[towards_y], side_in.at[towards_y]
            else:
                source, landing = corner_out.at[towards_x, towards_y], corner_in.at[towards_x, towards_y]
            plan(copies, (dx, dy), source, landing, in_sem, dz)
        return copies

    old_strips, new_strips, prior_old_strips, prior_new_strips = (strip_refs[6 * k : 6 * k + 6] for k in range(4))
    old_main = old_own.at[:, pl.ds(FRONT, cols_c)]
    old_copies = coarse_copies(None, old_own, old_strips, old_in, 0)
    chain_copies = coarse_copies(fine_mean, new_own, new_strips, chain_in, 1)
    prior_old_copies = coarse_copies(old_main, prior_old_own, prior_old_strips, prior_old_in, 1)
    prior_new_copies = coarse_copies(sent, prior_new_own, prior_new_strips, prior_new_in, 2)
    has_next, has_second = tm < n_tm - 1, tm < n_tm - 2

    lane = lax.broadcasted_iota(jnp.int32, (1, LANES), 1)
    pack = lane // levels

    def packed(row):
        return jnp.concatenate([row] * packs, axis=1)

    def advance(source, row, start, count, consts):
        keep, spread, along_x, along_y = consts
        centre = source[row, pl.ds(start, count), :]
        east = source[row + 1, pl.ds(start, count), :]
        west = source[row - 1, pl.ds(start, count), :]
        north = source[row, pl.ds(start + 1, count), :]
        south = source[row, pl.ds(start - 1, count), :]
        pushed = along_x * (east - west) + along_y * (north - south)
        return centre * (keep - pushed) + spread * ((east + west) + (north + south))

    def native_row(x):
        if x < 0:
            return x_recv[1, x + REACH]
        if x >= rows:
            return x_recv[0, x - rows]
        return x_ref[x]

    def bring_in(row):
        stacked = jnp.concatenate([native_row(p * part + row - REACH) for p in range(packs)], axis=0)
        first[row, pl.ds(FRONT, cols), :] = stacked.T

    low_lanes = lane < levels
    high_lanes = lane >= LANES - levels
    pl.semaphore_wait(barrier, awaited)

    def say_ready(k):
        @pl.when(tm > 0)
        def _():
            pl.semaphore_signal(
                ready.at[k], inc=1, device_id=target(-1, 0, 0), device_id_type=pl.DeviceIdType.MESH
            )

    say_ready(0)
    pltpu.make_async_copy(small_ref, small_ref, small_sem).wait()
    diffuse = packed(small_ref[0:1, :])
    east_wind = packed(small_ref[1:2, :])
    north_wind = packed(small_ref[2:3, :])

    def constants(factor):
        spread = (time_step * factor) * diffuse
        return 1.0 - 4.0 * spread, spread, (0.5 * time_step) * east_wind, (0.5 * time_step) * north_wind

    fine_constants = constants(1.0)
    coarse_constants = constants(0.25)

    def load_done(group, group_rows):
        whole = x_ref.at[pl.ds(0, packs * len(group_rows))]
        pltpu.make_async_copy(whole, whole, load_sems.at[group]).wait()

    def bring_own(group_rows):
        for row in group_rows:
            bring_in(REACH + row)
            y_send[0, row] = first[REACH + row, pl.ds(FRONT, REACH), :]
            y_send[1, row] = first[REACH + row, pl.ds(end - REACH, REACH), :]

    load_done(0, rows_first)
    bring_own(rows_first)
    send_all(fine_copies, 0, corner_moves)
    send_all(near_copies, 0, x_moves)
    load_done(1, rows_later)
    bring_own(rows_later)
    send_all(fine_copies, 0, side_moves)

    def restricted(source, row):
        total = source[REACH + row * RATIO, pl.ds(FRONT, cols), :]
        for r in range(1, RATIO):
            total = total + source[REACH + row * RATIO + r, pl.ds(FRONT, cols), :]
        fine_line[...] = total
        mean = fine_line[pl.ds(0, cols_c, stride=RATIO), :]
        for o in range(1, RATIO):
            mean = mean + fine_line[pl.ds(o, cols_c, stride=RATIO), :]
        return mean * (1.0 / RATIO**2)

    def swapped(value):
        return pltpu.roll(value, levels, 1)

    def pack_strips(row_of, strips, reach):
        row_out, _, side_out, _, corner_out, _ = strips
        for k in range(reach // 2):
            after, before = 2 * k, part_c - 2 * k - 2
            row_out[0, k] = jnp.where(low_lanes, row_of(after, 0, cols_c), swapped(row_of(after + 1, 0, cols_c)))
            row_out[1, k] = jnp.where(low_lanes, swapped(row_of(before, 0, cols_c)), row_of(before + 1, 0, cols_c))
        for side, col in ((0, 0), (1, cols_c - reach)):
            for row in range(part_c):
                side_out[side, row] = row_of(row, col, reach)
            for towards in range(2):
                for k in range(reach // 2):
                    corner_out[towards, side, k] = row_out[towards, k, pl.ds(col, reach), :]

    def old_row(row, col, count):
        return old_own[row, pl.ds(FRONT + col, count), :]

    for row in range(part_c):
        old_own[row, pl.ds(FRONT, cols_c), :] = restricted(first, row)
    pack_strips(old_row, old_strips, COARSE_REACH)
    send_all(far_copies, 0, x_moves)
    send_all(old_copies, 0, AROUND)

    def inside_x(row, reach, length):
        place = (gx * packs + pack) * length + (row - reach)
        return jnp.logical_and(place >= 0, place < n_gx * packs * length)

    def inside_y(start, count, length):
        place = gy * length + (start - FRONT) + lax.broadcasted_iota(jnp.int32, (count, LANES), 0)
        return jnp.logical_and(place >= 0, place < n_gy * length)

    edges = ((FRONT - EDGE, inside_y(FRONT - EDGE, EDGE, cols)), (end, inside_y(end, EDGE, cols)))
    reaches = ((FRONT - REACH, inside_y(FRONT - REACH, REACH, cols)), (end, inside_y(end, REACH, cols)))
    half = cols // 2

    def fill(source, dest, row, start, count, consts):
        dest[row, pl.ds(start, count), :] = advance(source, row, start, count, consts)

    def fill_edges(source, dest, row, consts):
        for start, mask in edges:
            value = advance(source, row, start, EDGE, consts)
            dest[row, pl.ds(start, EDGE), :] = jnp.where(mask, value, 0.0)

    def update(source, dest, row, consts, last):
        for start, count in ((FRONT, half), (FRONT + half, cols - half)):
            fill(source, dest, row, start, count, consts)
        if not last:
            fill_edges(source, dest, row, consts)

    buffers = (first, second)

    def inner_steps(row_update):
        for step in range(1, SUB + 1):
            def inner_row(row, step=step):
                row_update(buffers[(step - 1) % 2], buffers[step % 2], row, step)

            pl.loop(REACH + step, REACH + part - step, unroll=2)(inner_row)

    def centre_update(source, dest, row, step):
        fill(source, dest, row, FRONT + EDGE * step, half - EDGE * step, fine_constants)
        fill(source, dest, row, FRONT + half, cols - half - EDGE * step, fine_constants)

    def sides_update(source, dest, row, step):
        fill(source, dest, row, FRONT, EDGE * step, fine_constants)
        fill(source, dest, row, end - EDGE * step, EDGE * step, fine_constants)
        if step < SUB:
            fill_edges(source, dest, row, fine_constants)

    fill_missing(fine_copies, side_moves)
    fill_missing(fine_copies, corner_moves)
    fill_missing(near_copies, x_moves)
    fill_missing(far_copies, x_moves)
    fill_missing(old_copies, AROUND)
    inner_steps(centre_update)

    @pl.when(has_next)
    def _():
        pl.semaphore_wait(ready.at[0], 1)
        say_ready(1)
        pack_strips(old_row, prior_old_strips, LONG_REACH)
        send_all(prior_old_copies, 1, (*side_moves, (0, 0)))

    @pl.when(tm > 0)
    def _():
        fill_missing(prior_old_copies, AROUND)

    all_arrived(fine_copies, side_in_sem, side_moves)
    for side, (start, mask) in enumerate(reaches):
        for row in range(part):
            first[REACH + row, pl.ds(start, REACH), :] = jnp.where(mask, y_recv[side, row], 0.0)
    inner_steps(sides_update)

    def bring_halo(halo_rows):
        for row in halo_rows:
            bring_in(row)
            inner = first[row, pl.ds(FRONT, cols), :]
            first[row, pl.ds(FRONT, cols), :] = jnp.where(inside_x(row, REACH, part), inner, 0.0)
        for side, (start, mask_side) in enumerate(reaches):
            for row in halo_rows:
                if row < REACH:
                    here = jnp.where(high_lanes, corner_recv[0, side, row], y_recv[side, row + part - REACH])
                    here = pltpu.roll(here, levels, 1)
                else:
                    at = row - part - REACH
                    here = pltpu.roll(jnp.where(low_lanes, corner_recv[1, side, at], y_recv[side, at]), LANES - levels, 1)
                mask = jnp.logical_and(mask_side, inside_x(row, REACH, part))
                first[row, pl.ds(start, REACH), :] = jnp.where(mask, here, 0.0)

    def outer_steps(low_shift, high_shift, count):
        for step in range(1, SUB + 1):
            def outer_row(k, step=step):
                for row in (step + low_shift + k, part + REACH - step + high_shift + k):
                    mask_x = inside_x(row, REACH, part)
                    consts = tuple(jnp.where(mask_x, c, 0.0) for c in fine_constants)
                    update(buffers[(step - 1) % 2], buffers[step % 2], row, consts, step == SUB)

            pl.loop(0, count)(outer_row)

    all_arrived(near_copies, near_in, x_moves)
    pl.when(has_next)(lambda: send_all(prior_old_copies, 1, x_moves + corner_moves))
    all_arrived(fine_copies, corner_in_sem, corner_moves)
    bring_halo([*range(far, REACH), *range(REACH + part, REACH + part + near)])
    outer_steps(far, 0, near)

    all_arrived(far_copies, far_in, x_moves)
    bring_halo([*range(far), *range(REACH + part + near, wide)])
    outer_steps(0, near, far)
    fine = buffers[SUB % 2]

    for row in range(part_c):
        fine_mean[row] = restricted(fine, row)

    @pl.when(has_next)
    def _():
        pack_strips(lambda row, col, count: fine_mean[row, pl.ds(col, count), :], new_strips, COARSE_REACH)
        send_all(chain_copies, 1, AROUND)
        send_all(chain_copies, 1, ((0, 0),))

    count_c = cols_c + 2 * EDGE
    begin_c = FRONT - EDGE
    across = pl.ds(begin_c, count_c)
    mask_y = inside_y(begin_c, count_c, cols_c)

    def extend(buffer, strips, target, reach):
        _, row_in, _, side_in, _, corner_in = strips
        for side, col in ((0, end_c), (1, FRONT - reach)):
            for row in range(part_c):
                buffer[row, pl.ds(col, reach), :] = side_in[side, row]
            for towards in range(2):
                for k in range(reach // 2):
                    row_in[towards, k, pl.ds(col, reach), :] = corner_in[towards, side, k]

        def own(row):
            return buffer[row, across, :]

        values = [own(row) for row in range(part_c)]
        for k in range(reach // 2):
            above, below = (row_in[towards, k, across, :] for towards in (0, 1))
            after, before = 2 * k, part_c - 2 * k - 2
            values = [
                jnp.where(low_lanes, below, swapped(own(before))),
                swapped(jnp.where(high_lanes, below, own(before + 1))),
                *values,
                swapped(jnp.where(low_lanes, above, own(after))),
                jnp.where(high_lanes, above, swapped(own(after + 1))),
            ]
        for row, value in enumerate(values):
            mask = mask_y
            if not reach <= row < reach + part_c:
                mask = jnp.logical_and(mask_y, inside_x(row, reach, part_c))
            target[row, across, :] = jnp.where(mask, value, 0.0)

    def image_of(source, image):
        for row in range(image.shape[0]):
            image[row] = advance(source, row + 1, begin_c, count_c, coarse_constants)

    def change_of(source, image, reach, result):
        for row in range(image.shape[0]):
            moved = advance(source, row + 1, begin_c, count_c, coarse_constants) - image[row]
            mask = jnp.logical_and(mask_y, inside_x(row + 1, reach, part_c))
            result[row, across, :] = jnp.where(mask, moved, 0.0)

    def smoothed(source, row, start, count):
        line[across, :] = (
            mean_side * (source[row, across, :] + source[row + 2, across, :]) + mean_mid * source[row + 1, across, :]
        )
        sides = line[pl.ds(start - 1, count), :] + line[pl.ds(start + 1, count), :]
        return mean_side * sides + mean_mid * line[pl.ds(start, count), :]

    def find_lift():
        change_of(long_extended, prior_image, LONG_REACH, prior_change)
        for row in range(wide_c):
            mask = jnp.logical_and(mask_y, inside_x(row, COARSE_REACH, part_c))
            lift[row] = jnp.where(mask, smoothed(prior_change, row, begin_c, count_c), 0.0)

    all_arrived(old_copies, old_in, AROUND)
    extend(old_own, old_strips, extended, COARSE_REACH)
    image_of(extended, old_image)
    def send_on():
        for row in range(part_c):
            sent[row] = fine_mean[row] + smoothed(change, row, FRONT, cols_c)
        pack_strips(lambda row, col, count: sent[row, pl.ds(col, count), :], prior_new_strips, LONG_REACH)
        pl.semaphore_wait(ready.at[1], 1)
        send_all(prior_new_copies, 2, AROUND)
        send_all(prior_new_copies, 2, ((0, 0),))

    @pl.when(tm == 0)
    def _():
        change_of(extended, old_image, COARSE_REACH, change)
        pl.when(has_second)(send_on)

    @pl.when(tm > 0)
    def _():
        fill_missing(chain_copies, AROUND)

    @pl.when(tm > 1)
    def _():
        fill_missing(prior_new_copies, AROUND)

    for row in range(part):
        turned[row] = fine[REACH + row, pl.ds(FRONT, cols), :].T

    @pl.when(tm > 0)
    def _():
        all_arrived(prior_old_copies, prior_old_in, PLANE)
        extend(prior_old_own, prior_old_strips, long_extended, LONG_REACH)
        image_of(long_extended, prior_image)
        pl.when(tm == 1)(find_lift)
        all_arrived(chain_copies, chain_in, PLANE)
        extend(new_own, new_strips, extended, COARSE_REACH)

        @pl.when(tm > 1)
        def _():
            all_arrived(prior_new_copies, prior_new_in, PLANE)
            extend(prior_new_own, prior_new_strips, long_extended, LONG_REACH)
            find_lift()

        for row in range(wide_c):
            extended[row, across, :] = extended[row, across, :] + lift[row]
        change_of(extended, old_image, COARSE_REACH, change)
        pl.when(has_second)(send_on)

    sends_done(fine_copies, 0, y_moves)
    sends_done(old_copies, 0, AROUND)
    sends_done(near_copies, 0, x_moves)
    sends_done(far_copies, 0, x_moves)
    @pl.when(has_next)
    def _():
        sends_done(chain_copies, 1, PLANE)
        sends_done(prior_old_copies, 1, PLANE)

    pl.when(has_second)(lambda: sends_done(prior_new_copies, 2, PLANE))


def closing(levels, rows, turned, change, out_hbm, filled, spread_rows, sem):
    packs = LANES // levels
    part, _, cols = turned.shape
    part_c = part // RATIO
    count_c = cols // RATIO + 2 * EDGE
    coarse_col = lax.broadcasted_iota(jnp.int32, (count_c, cols), 0) - EDGE
    fine_col = lax.broadcasted_iota(jnp.int32, (count_c, cols), 1)
    offset_of = fine_col & (RATIO - 1)
    apart = coarse_col - (fine_col >> (RATIO.bit_length() - 1))
    spreading = jnp.zeros((count_c, cols), jnp.float32)
    for o in range(RATIO):
        for distance, weights in ((-1, weights_low), (0, weights_mid), (1, weights_high)):
            chosen = jnp.logical_and(offset_of == o, apart == distance)
            spreading = jnp.where(chosen, weights[o], spreading)
    spreading = jnp.concatenate([spreading.astype(jnp.bfloat16)] * 3, axis=0)
    def spread_row(row):
        rest, pieces = change[row, pl.ds(FRONT - EDGE, count_c), :], []
        for _ in range(3):
            piece = rest.astype(jnp.bfloat16).astype(jnp.float32)
            pieces.append(piece)
            rest = rest - piece
        split = jnp.concatenate(pieces, axis=0).T.astype(jnp.bfloat16)
        return jnp.dot(split, spreading, preferred_element_type=jnp.float32)

    for row in range(2):
        spread_rows[row] = spread_row(row)
    for row in range(part):
        at, o = row // RATIO, row % RATIO
        if o == 0:
            spread_rows[at + 2] = spread_row(at + 2)
        total = turned[row] + weights_mid[o] * spread_rows[at + 1]
        if weights_low[o]:
            total = total + weights_low[o] * spread_rows[at]
        if weights_high[o]:
            total = total + weights_high[o] * spread_rows[at + 2]
        filled[row] = total
        for p in range(packs):
            x = p * part + row
            pltpu.make_async_copy(filled.at[row, pl.ds(p * levels, levels)], out_hbm.at[:, x], sem).start()
    pltpu.make_async_copy(filled, filled, sem).wait()


def shards(sizes, state_starts, diffusivity, wind):
    _, levels, rows, cols = state_starts.shape
    packs = LANES // levels
    if packs != 2 or levels * packs != LANES:
        raise ValueError(levels)
    part = rows // packs
    part_c = part // RATIO
    cols_c = cols // RATIO
    wide, wide_c, wide_long = part + 2 * REACH, part_c + 2 * COARSE_REACH, part_c + 2 * LONG_REACH
    if part_c < LONG_REACH:
        raise ValueError(part_c)
    vmem = functools.partial(pltpu.VMEM, dtype=jnp.float32)
    scratch = [
        vmem((rows, levels, cols)),
        vmem((3, levels)),
        pltpu.SemaphoreType.DMA((2,)),
        pltpu.SemaphoreType.DMA,
        pltpu.SemaphoreType.REGULAR((2,)),
        vmem((wide, cols + 2 * FRONT, LANES)),
        vmem((wide, cols + 2 * FRONT, LANES)),
        vmem((2, REACH, levels, cols)),
        vmem((2, part, REACH, LANES)),
        vmem((2, part, REACH, LANES)),
        vmem((2, 2, REACH, REACH, LANES)),
        *[vmem((part_c, cols_c + 2 * FRONT, LANES))] * 4,
        vmem((wide_c, cols_c + 2 * FRONT, LANES)),
        vmem((wide_long, cols_c + 2 * FRONT, LANES)),
        vmem((wide_c - 2, cols_c + 2 * EDGE, LANES)),
        vmem((wide_long - 2, cols_c + 2 * EDGE, LANES)),
        vmem((wide_long - 2, cols_c + 2 * FRONT, LANES)),
        vmem((wide_c, cols_c + 2 * EDGE, LANES)),
        vmem((part_c, cols_c, LANES)),
        vmem((part_c, cols_c, LANES)),
        vmem((cols_c + 2 * FRONT, LANES)),
        vmem((cols, LANES)),
        vmem((TALLY, LANES)),
    ] + [pltpu.SemaphoreType.DMA] * 9
    for reach in (COARSE_REACH, COARSE_REACH, LONG_REACH, LONG_REACH):
        scratch += [
            vmem((2, reach // 2, cols_c, LANES)),
            vmem((2, reach // 2, cols_c + 2 * FRONT, LANES)),
            vmem((2, part_c, reach, LANES)),
            vmem((2, part_c, reach, LANES)),
            vmem((2, 2, reach // 2, reach, LANES)),
            vmem((2, 2, reach // 2, reach, LANES)),
        ]
    in_vmem = pl.BlockSpec(memory_space=pltpu.VMEM)
    handed = pl.pallas_call(
        functools.partial(kernel, sizes, levels, rows, cols),
        out_shape=(vmem((part, LANES, cols)), vmem((part_c + 2, cols_c + 2 * FRONT, LANES))),
        in_specs=[pl.BlockSpec(memory_space=pl.ANY)] * 3,
        out_specs=(in_vmem, in_vmem),
        scratch_shapes=scratch,
        compiler_params=pltpu.CompilerParams(collective_id=0, has_side_effects=True),
        name="parareal",
    )(state_starts.reshape(levels, rows, cols), diffusivity.reshape(1, levels), wind)
    ending = pl.pallas_call(
        functools.partial(closing, levels, rows),
        out_shape=jax.ShapeDtypeStruct((levels, rows, cols), jnp.float32),
        in_specs=[in_vmem, in_vmem],
        out_specs=pl.BlockSpec(memory_space=pl.ANY),
        scratch_shapes=[
            vmem((part, LANES, cols)),
            vmem((part_c + 2, LANES, cols)),
            pltpu.SemaphoreType.DMA,
        ],
        name="closing",
    )(*(pltpu.with_memory_space_constraint(array, pltpu.VMEM) for array in handed))
    return ending.reshape(1, levels, rows, cols)


def solution(mesh):
    sizes = tuple(mesh.shape[axis] for axis in ("tm", "gx", "gy"))
    placed = (P("tm", None, "gx", "gy"), P(), P())
    return jax.shard_map(
        functools.partial(shards, sizes),
        mesh=mesh, in_specs=placed, out_specs=P("tm", None, "gx", "gy"), check_vma=False,
    )
```

```python
import functools
import math

import jax
import jax.numpy as jnp
from jax import lax
from jax.experimental import pallas as pl
from jax.experimental.pallas import tpu as pltpu
from jax.sharding import PartitionSpec as P

SUB = 4
REACH = SUB
RATIO = 4
LANES = 128
EDGE = 8
FRONT = 2 * EDGE
COARSE_REACH = 2
LONG_REACH = 2 * COARSE_REACH
TALLY = 1024

time_step = 0.2
weights_low = (0.375, 0.125, 0.0, 0.0)
weights_mid = (0.625, 0.875, 0.875, 0.625)
weights_high = (0.0, 0.0, 0.125, 0.375)
mean_side, mean_mid = 0.125, 0.75

PLANE = tuple((dx, dy) for dx in (-1, 0, 1) for dy in (-1, 0, 1))
AROUND = tuple(d for d in PLANE if d != (0, 0))
x_moves = tuple(d for d in AROUND if d[1] == 0)
y_moves = tuple(d for d in AROUND if d[1] != 0)
side_moves = tuple(d for d in y_moves if d[0] == 0)
corner_moves = tuple(d for d in y_moves if d[0] != 0)


def conjunction(conditions):
    total = True
    for condition in conditions:
        total = condition if total is True else jnp.logical_and(total, condition)
    return total


def kernel(
    sizes, levels, rows, cols,
    x_hbm, diff_hbm, wind_hbm, turned, change,
    x_ref, small_ref, load_sems, small_sem, ready,
    first, second, x_recv, y_send, y_recv, corner_recv,
    old_own, new_own, prior_old_own, prior_new_own, extended, long_extended, old_image, prior_image, prior_change, lift,
    sent, fine_mean, line, fine_line, tally,
    out_sem, near_in, far_in, side_in_sem, corner_in_sem, old_in, chain_in, prior_old_in, prior_new_in, *strip_refs,
):
    n_tm, n_gx, n_gy = sizes
    tm, gx, gy = lax.axis_index("tm"), lax.axis_index("gx"), lax.axis_index("gy")
    packs = LANES // levels
    part = rows // packs
    part_c = part // RATIO
    cols_c = cols // RATIO
    wide = part + 2 * REACH
    wide_c = part_c + 2 * COARSE_REACH
    end = FRONT + cols
    end_c = FRONT + cols_c

    def there(dz, dx, dy):
        tests = []
        for place, move, count in ((tm, dz, n_tm), (gx, dx, n_gx), (gy, dy, n_gy)):
            if move < 0:
                tests.append(place >= -move)
            if move > 0:
                tests.append(place < count - move)
        return conjunction(tests)

    def guarded(condition, action):
        if condition is True:
            action()
        else:
            pl.when(condition)(action)

    def target(dz, dx, dy):
        return (tm + dz, gx + dx, gy + dy)

    rows_first = [*range(REACH), *range(part - REACH, part)]
    rows_later = [*range(REACH, part - REACH)]
    for group, group_rows in enumerate((rows_first, rows_later)):
        for row in group_rows:
            for x in range(row, rows, part):
                pltpu.make_async_copy(x_hbm.at[:, x], x_ref.at[x], load_sems.at[group]).start()
    for source, landing in ((diff_hbm, small_ref.at[pl.ds(0, 1)]), (wind_hbm, small_ref.at[pl.ds(1, 2)])):
        pltpu.make_async_copy(source, landing, small_sem).start()

    barrier = pltpu.get_barrier_semaphore()
    partners = [(0, dx, dy) for dx, dy in AROUND] + [(-1, 0, 0), (1, 0, 0)]
    partners.sort(key=lambda move: -sum(map(abs, move)))
    awaited = jnp.int32(0)
    for move in partners:
        def greet(move=move):
            pl.semaphore_signal(barrier, inc=1, device_id=target(*move), device_id_type=pl.DeviceIdType.MESH)
        guarded(there(*move), greet)
        awaited = awaited + there(*move).astype(jnp.int32)

    def send_all(copies, dz, moves):
        for move in moves:
            guarded(there(dz, *move), lambda move=move: copies[move].start())

    def sends_done(copies, dz, moves):
        for move in moves:
            guarded(there(dz, *move), lambda move=move: copies[move].wait_send())

    stand_ins, sizes_in_rows = {}, {}

    def fill_missing(copies, moves):
        for dx, dy in moves:
            @pl.when(jnp.logical_not(there(0, -dx, -dy)))
            def _(dx=dx, dy=dy):
                pltpu.make_async_copy(*stand_ins[id(copies)][dx, dy]).start()

    def all_arrived(copies, in_sem, moves):
        height = sum(sizes_in_rows[id(copies)][move] for move in moves)
        whole = tally.at[pl.ds(0, height)]
        pltpu.make_async_copy(whole, whole, in_sem).wait()

    def plan(copies, move, source, landing, in_sem, dz=0):
        copies[move] = remote(source, landing, in_sem, (dz, *move))
        stand_ins.setdefault(id(copies), {})[move] = (source, landing, in_sem)
        sizes_in_rows.setdefault(id(copies), {})[move] = math.prod(source.shape[:-1])

    def remote(source, landing, in_sem, move):
        return pltpu.make_async_remote_copy(
            src_ref=source, dst_ref=landing, send_sem=out_sem, recv_sem=in_sem,
            device_id=target(*move), device_id_type=pl.DeviceIdType.MESH,
        )

    fine_copies = {}
    for move in y_moves:
        dx, dy = move
        if dx == 0:
            source, landing, in_sem = y_send.at[(dy + 1) // 2], y_recv.at[(1 - dy) // 2], side_in_sem
        else:
            source = y_send.at[(dy + 1) // 2, pl.ds(0 if dx < 0 else part - REACH, REACH)]
            landing, in_sem = corner_recv.at[(1 - dx) // 2, (1 - dy) // 2], corner_in_sem
        plan(fine_copies, move, source, landing, in_sem)
    near, far = REACH // 2, REACH - REACH // 2
    near_copies, far_copies = {}, {}
    for dx in (-1, 1):
        low = dx < 0
        for copies, start, count, in_sem in (
            (near_copies, 0 if low else far, near, near_in), (far_copies, near if low else 0, far, far_in)
        ):
            source = x_ref.at[pl.ds(start if low else rows - REACH + start, count)]
            landing = x_recv.at[0 if low else 1, pl.ds(start, count)]
            plan(copies, (dx, 0), source, landing, in_sem)

    def coarse_copies(main, own_in, strips, in_sem, dz):
        row_out, row_in, side_out, side_in, corner_out, corner_in = strips
        copies = {}
        for dx, dy in PLANE if dz else AROUND:
            towards_x, towards_y = (dx + 1) // 2, (dy + 1) // 2
            if dx == 0 and dy == 0:
                source, landing = main, own_in.at[:, pl.ds(FRONT, cols_c)]
            elif dy == 0:
                source, landing = row_out.at[towards_x], row_in.at[towards_x, :, pl.ds(FRONT, cols_c)]
            elif dx == 0:
                source, landing = side_out.at[towards_y], side_in.at[towards_y]
            else:
                source, landing = corner_out.at[towards_x, towards_y], corner_in.at[towards_x, towards_y]
            plan(copies, (dx, dy), source, landing, in_sem, dz)
        return copies

    old_strips, new_strips, prior_old_strips, prior_new_strips = (strip_refs[6 * k : 6 * k + 6] for k in range(4))
    old_main = old_own.at[:, pl.ds(FRONT, cols_c)]
    old_copies = coarse_copies(None, old_own, old_strips, old_in, 0)
    chain_copies = coarse_copies(fine_mean, new_own, new_strips, chain_in, 1)
    prior_old_copies = coarse_copies(old_main, prior_old_own, prior_old_strips, prior_old_in, 1)
    prior_new_copies = coarse_copies(sent, prior_new_own, prior_new_strips, prior_new_in, 2)
    has_next, has_second = tm < n_tm - 1, tm < n_tm - 2

    lane = lax.broadcasted_iota(jnp.int32, (1, LANES), 1)
    pack = lane // levels

    def packed(row):
        return jnp.concatenate([row] * packs, axis=1)

    def advance(source, row, start, count, consts):
        keep, spread, along_x, along_y = consts
        centre = source[row, pl.ds(start, count), :]
        east = source[row + 1, pl.ds(start, count), :]
        west = source[row - 1, pl.ds(start, count), :]
        north = source[row, pl.ds(start + 1, count), :]
        south = source[row, pl.ds(start - 1, count), :]
        pushed = along_x * (east - west) + along_y * (north - south)
        return centre * (keep - pushed) + spread * ((east + west) + (north + south))

    def native_row(x):
        if x < 0:
            return x_recv[1, x + REACH]
        if x >= rows:
            return x_recv[0, x - rows]
        return x_ref[x]

    def bring_in(row):
        stacked = jnp.concatenate([native_row(p * part + row - REACH) for p in range(packs)], axis=0)
        first[row, pl.ds(FRONT, cols), :] = stacked.T

    low_lanes = lane < levels
    high_lanes = lane >= LANES - levels
    pl.semaphore_wait(barrier, awaited)

    def say_ready(k):
        @pl.when(tm > 0)
        def _():
            pl.semaphore_signal(
                ready.at[k], inc=1, device_id=target(-1, 0, 0), device_id_type=pl.DeviceIdType.MESH
            )

    say_ready(0)
    pltpu.make_async_copy(small_ref, small_ref, small_sem).wait()
    diffuse = packed(small_ref[0:1, :])
    east_wind = packed(small_ref[1:2, :])
    north_wind = packed(small_ref[2:3, :])

    def constants(factor):
        spread = (time_step * factor) * diffuse
        return 1.0 - 4.0 * spread, spread, (0.5 * time_step) * east_wind, (0.5 * time_step) * north_wind

    fine_constants = constants(1.0)
    coarse_constants = constants(0.25)

    def load_done(group, group_rows):
        whole = x_ref.at[pl.ds(0, packs * len(group_rows))]
        pltpu.make_async_copy(whole, whole, load_sems.at[group]).wait()

    def bring_own(group_rows):
        for row in group_rows:
            bring_in(REACH + row)
            y_send[0, row] = first[REACH + row, pl.ds(FRONT, REACH), :]
            y_send[1, row] = first[REACH + row, pl.ds(end - REACH, REACH), :]

    load_done(0, rows_first)
    bring_own(rows_first)
    send_all(fine_copies, 0, corner_moves)
    send_all(near_copies, 0, x_moves)
    load_done(1, rows_later)
    bring_own(rows_later)
    send_all(fine_copies, 0, side_moves)

    def restricted(source, row):
        total = source[REACH + row * RATIO, pl.ds(FRONT, cols), :]
        for r in range(1, RATIO):
            total = total + source[REACH + row * RATIO + r, pl.ds(FRONT, cols), :]
        fine_line[...] = total
        mean = fine_line[pl.ds(0, cols_c, stride=RATIO), :]
        for o in range(1, RATIO):
            mean = mean + fine_line[pl.ds(o, cols_c, stride=RATIO), :]
        return mean * (1.0 / RATIO**2)

    def swapped(value):
        return pltpu.roll(value, levels, 1)

    def pack_strips(row_of, strips, reach):
        row_out, _, side_out, _, corner_out, _ = strips
        for k in range(reach // 2):
            after, before = 2 * k, part_c - 2 * k - 2
            row_out[0, k] = jnp.where(low_lanes, row_of(after, 0, cols_c), swapped(row_of(after + 1, 0, cols_c)))
            row_out[1, k] = jnp.where(low_lanes, swapped(row_of(before, 0, cols_c)), row_of(before + 1, 0, cols_c))
        for side, col in ((0, 0), (1, cols_c - reach)):
            for row in range(part_c):
                side_out[side, row] = row_of(row, col, reach)
            for towards in range(2):
                for k in range(reach // 2):
                    corner_out[towards, side, k] = row_out[towards, k, pl.ds(col, reach), :]

    def old_row(row, col, count):
        return old_own[row, pl.ds(FRONT + col, count), :]

    for row in range(part_c):
        old_own[row, pl.ds(FRONT, cols_c), :] = restricted(first, row)
    pack_strips(old_row, old_strips, COARSE_REACH)
    send_all(far_copies, 0, x_moves)
    send_all(old_copies, 0, AROUND)

    def inside_x(row, reach, length):
        place = (gx * packs + pack) * length + (row - reach)
        return jnp.logical_and(place >= 0, place < n_gx * packs * length)

    def inside_y(start, count, length):
        place = gy * length + (start - FRONT) + lax.broadcasted_iota(jnp.int32, (count, LANES), 0)
        return jnp.logical_and(place >= 0, place < n_gy * length)

    edges = ((FRONT - EDGE, inside_y(FRONT - EDGE, EDGE, cols)), (end, inside_y(end, EDGE, cols)))
    reaches = ((FRONT - REACH, inside_y(FRONT - REACH, REACH, cols)), (end, inside_y(end, REACH, cols)))
    half = cols // 2

    def fill(source, dest, row, start, count, consts):
        dest[row, pl.ds(start, count), :] = advance(source, row, start, count, consts)

    def fill_edges(source, dest, row, consts):
        for start, mask in edges:
            value = advance(source, row, start, EDGE, consts)
            dest[row, pl.ds(start, EDGE), :] = jnp.where(mask, value, 0.0)

    def update(source, dest, row, consts, last):
        for start, count in ((FRONT, half), (FRONT + half, cols - half)):
            fill(source, dest, row, start, count, consts)
        if not last:
            fill_edges(source, dest, row, consts)

    buffers = (first, second)

    def inner_steps(row_update):
        for step in range(1, SUB + 1):
            def inner_row(row, step=step):
                row_update(buffers[(step - 1) % 2], buffers[step % 2], row, step)

            pl.loop(REACH + step, REACH + part - step, unroll=2)(inner_row)

    def centre_update(source, dest, row, step):
        fill(source, dest, row, FRONT + EDGE * step, half - EDGE * step, fine_constants)
        fill(source, dest, row, FRONT + half, cols - half - EDGE * step, fine_constants)

    def sides_update(source, dest, row, step):
        fill(source, dest, row, FRONT, EDGE * step, fine_constants)
        fill(source, dest, row, end - EDGE * step, EDGE * step, fine_constants)
        if step < SUB:
            fill_edges(source, dest, row, fine_constants)

    fill_missing(fine_copies, side_moves)
    fill_missing(fine_copies, corner_moves)
    fill_missing(near_copies, x_moves)
    fill_missing(far_copies, x_moves)
    fill_missing(old_copies, AROUND)
    inner_steps(centre_update)

    @pl.when(has_next)
    def _():
        pl.semaphore_wait(ready.at[0], 1)
        say_ready(1)
        pack_strips(old_row, prior_old_strips, LONG_REACH)
        send_all(prior_old_copies, 1, (*side_moves, (0, 0)))

    @pl.when(tm > 0)
    def _():
        fill_missing(prior_old_copies, AROUND)

    all_arrived(fine_copies, side_in_sem, side_moves)
    for side, (start, mask) in enumerate(reaches):
        for row in range(part):
            first[REACH + row, pl.ds(start, REACH), :] = jnp.where(mask, y_recv[side, row], 0.0)
    inner_steps(sides_update)

    def bring_halo(halo_rows):
        for row in halo_rows:
            bring_in(row)
            inner = first[row, pl.ds(FRONT, cols), :]
            first[row, pl.ds(FRONT, cols), :] = jnp.where(inside_x(row, REACH, part), inner, 0.0)
        for side, (start, mask_side) in enumerate(reaches):
            for row in halo_rows:
                if row < REACH:
                    here = jnp.where(high_lanes, corner_recv[0, side, row], y_recv[side, row + part - REACH])
                    here = pltpu.roll(here, levels, 1)
                else:
                    at = row - part - REACH
                    here = pltpu.roll(jnp.where(low_lanes, corner_recv[1, side, at], y_recv[side, at]), LANES - levels, 1)
                mask = jnp.logical_and(mask_side, inside_x(row, REACH, part))
                first[row, pl.ds(start, REACH), :] = jnp.where(mask, here, 0.0)

    def outer_steps(low_shift, high_shift, count):
        for step in range(1, SUB + 1):
            def outer_row(k, step=step):
                for row in (step + low_shift + k, part + REACH - step + high_shift + k):
                    mask_x = inside_x(row, REACH, part)
                    consts = tuple(jnp.where(mask_x, c, 0.0) for c in fine_constants)
                    update(buffers[(step - 1) % 2], buffers[step % 2], row, consts, step == SUB)

            pl.loop(0, count)(outer_row)

    all_arrived(near_copies, near_in, x_moves)
    pl.when(has_next)(lambda: send_all(prior_old_copies, 1, x_moves + corner_moves))
    all_arrived(fine_copies, corner_in_sem, corner_moves)
    bring_halo([*range(far, REACH), *range(REACH + part, REACH + part + near)])
    outer_steps(far, 0, near)

    all_arrived(far_copies, far_in, x_moves)
    bring_halo([*range(far), *range(REACH + part + near, wide)])
    outer_steps(0, near, far)
    fine = buffers[SUB % 2]

    for row in range(part_c):
        fine_mean[row] = restricted(fine, row)

    @pl.when(has_next)
    def _():
        pack_strips(lambda row, col, count: fine_mean[row, pl.ds(col, count), :], new_strips, COARSE_REACH)
        send_all(chain_copies, 1, AROUND)
        send_all(chain_copies, 1, ((0, 0),))

    count_c = cols_c + 2 * EDGE
    begin_c = FRONT - EDGE
    across = pl.ds(begin_c, count_c)
    mask_y = inside_y(begin_c, count_c, cols_c)
    place_c = lax.broadcasted_iota(jnp.int32, (count_c, LANES), 0) - EDGE
    mask_near = jnp.logical_and(mask_y, jnp.logical_and(place_c >= -1, place_c <= cols_c))

    def extend(buffer, strips, target, reach):
        _, row_in, _, side_in, _, corner_in = strips
        for side, col in ((0, end_c), (1, FRONT - reach)):
            for row in range(part_c):
                buffer[row, pl.ds(col, reach), :] = side_in[side, row]
            for towards in range(2):
                for k in range(reach // 2):
                    row_in[towards, k, pl.ds(col, reach), :] = corner_in[towards, side, k]

        def own(row):
            return buffer[row, across, :]

        values = [own(row) for row in range(part_c)]
        for k in range(reach // 2):
            above, below = (row_in[towards, k, across, :] for towards in (0, 1))
            after, before = 2 * k, part_c - 2 * k - 2
            values = [
                jnp.where(low_lanes, below, swapped(own(before))),
                swapped(jnp.where(high_lanes, below, own(before + 1))),
                *values,
                swapped(jnp.where(low_lanes, above, own(after))),
                jnp.where(high_lanes, above, swapped(own(after + 1))),
            ]
        for row, value in enumerate(values):
            mask = mask_y
            if not reach <= row < reach + part_c:
                mask = jnp.logical_and(mask_y, inside_x(row, reach, part_c))
            target[row, across, :] = jnp.where(mask, value, 0.0)

    def image_of(source, image):
        for row in range(image.shape[0]):
            image[row] = advance(source, row + 1, begin_c, count_c, coarse_constants)

    def change_of(source, image, reach, result):
        for row in range(image.shape[0]):
            moved = advance(source, row + 1, begin_c, count_c, coarse_constants) - image[row]
            columns = mask_near if reach == COARSE_REACH else mask_y
            mask = jnp.logical_and(columns, inside_x(row + 1, reach, part_c))
            result[row, across, :] = jnp.where(mask, moved, 0.0)

    def smoothed(source, row, start, count):
        line[across, :] = (
            mean_side * (source[row, across, :] + source[row + 2, across, :]) + mean_mid * source[row + 1, across, :]
        )
        sides = line[pl.ds(start - 1, count), :] + line[pl.ds(start + 1, count), :]
        return mean_side * sides + mean_mid * line[pl.ds(start, count), :]

    def find_lift(put):
        change_of(long_extended, prior_image, LONG_REACH, prior_change)
        for row in range(wide_c):
            mask = jnp.logical_and(mask_y, inside_x(row, COARSE_REACH, part_c))
            put(row, jnp.where(mask, smoothed(prior_change, row, begin_c, count_c), 0.0))

    def keep_lift(row, value):
        lift[row] = value

    def add_lift(row, value):
        extended[row, across, :] = extended[row, across, :] + value

    all_arrived(old_copies, old_in, AROUND)
    extend(old_own, old_strips, extended, COARSE_REACH)
    image_of(extended, old_image)
    def send_on():
        for row in range(part_c):
            sent[row] = fine_mean[row] + smoothed(change, row, FRONT, cols_c)
        pack_strips(lambda row, col, count: sent[row, pl.ds(col, count), :], prior_new_strips, LONG_REACH)
        pl.semaphore_wait(ready.at[1], 1)
        send_all(prior_new_copies, 2, AROUND)
        send_all(prior_new_copies, 2, ((0, 0),))

    @pl.when(tm == 0)
    def _():
        change_of(extended, old_image, COARSE_REACH, change)
        pl.when(has_second)(send_on)

    @pl.when(tm > 0)
    def _():
        fill_missing(chain_copies, AROUND)

    @pl.when(tm > 1)
    def _():
        fill_missing(prior_new_copies, AROUND)

    for row in range(part):
        turned[row] = fine[REACH + row, pl.ds(FRONT, cols), :].T

    @pl.when(tm > 0)
    def _():
        all_arrived(prior_old_copies, prior_old_in, PLANE)
        extend(prior_old_own, prior_old_strips, long_extended, LONG_REACH)
        image_of(long_extended, prior_image)
        pl.when(tm == 1)(lambda: find_lift(keep_lift))
        all_arrived(chain_copies, chain_in, PLANE)
        extend(new_own, new_strips, extended, COARSE_REACH)

        @pl.when(tm > 1)
        def _():
            all_arrived(prior_new_copies, prior_new_in, PLANE)
            extend(prior_new_own, prior_new_strips, long_extended, LONG_REACH)
            find_lift(add_lift)

        @pl.when(tm == 1)
        def _():
            for row in range(wide_c):
                add_lift(row, lift[row])

        change_of(extended, old_image, COARSE_REACH, change)
        pl.when(has_second)(send_on)

    sends_done(fine_copies, 0, y_moves)
    sends_done(old_copies, 0, AROUND)
    sends_done(near_copies, 0, x_moves)
    sends_done(far_copies, 0, x_moves)
    @pl.when(has_next)
    def _():
        sends_done(chain_copies, 1, PLANE)
        sends_done(prior_old_copies, 1, PLANE)

    pl.when(has_second)(lambda: sends_done(prior_new_copies, 2, PLANE))


def closing(levels, rows, turned, change, out_hbm, filled, spread_rows, sem):
    packs = LANES // levels
    part, _, cols = turned.shape
    part_c = part // RATIO
    count_c = cols // RATIO + 2 * EDGE
    coarse_col = lax.broadcasted_iota(jnp.int32, (count_c, cols), 0) - EDGE
    fine_col = lax.broadcasted_iota(jnp.int32, (count_c, cols), 1)
    offset_of = fine_col & (RATIO - 1)
    apart = coarse_col - (fine_col >> (RATIO.bit_length() - 1))
    spreading = jnp.zeros((count_c, cols), jnp.float32)
    for o in range(RATIO):
        for distance, weights in ((-1, weights_low), (0, weights_mid), (1, weights_high)):
            chosen = jnp.logical_and(offset_of == o, apart == distance)
            spreading = jnp.where(chosen, weights[o], spreading)
    spreading = spreading.astype(jnp.bfloat16)

    def spread_row(row):
        rest, total = change[row, pl.ds(FRONT - EDGE, count_c), :].T, 0.0
        for _ in range(3):
            piece = rest.astype(jnp.bfloat16)
            total = total + jnp.dot(piece, spreading, preferred_element_type=jnp.float32)
            rest = rest - piece.astype(jnp.float32)
        return total

    for row in range(2):
        spread_rows[row] = spread_row(row)
    for row in range(part):
        at, o = row // RATIO, row % RATIO
        if o == 0:
            spread_rows[at + 2] = spread_row(at + 2)
        total = turned[row] + weights_mid[o] * spread_rows[at + 1]
        if weights_low[o]:
            total = total + weights_low[o] * spread_rows[at]
        if weights_high[o]:
            total = total + weights_high[o] * spread_rows[at + 2]
        filled[row] = total
        for p in range(packs):
            x = p * part + row
            pltpu.make_async_copy(filled.at[row, pl.ds(p * levels, levels)], out_hbm.at[:, x], sem).start()
    pltpu.make_async_copy(filled, filled, sem).wait()


def shards(sizes, state_starts, diffusivity, wind):
    _, levels, rows, cols = state_starts.shape
    packs = LANES // levels
    if packs != 2 or levels * packs != LANES:
        raise ValueError(levels)
    part = rows // packs
    part_c = part // RATIO
    cols_c = cols // RATIO
    wide, wide_c, wide_long = part + 2 * REACH, part_c + 2 * COARSE_REACH, part_c + 2 * LONG_REACH
    if part_c < LONG_REACH:
        raise ValueError(part_c)
    vmem = functools.partial(pltpu.VMEM, dtype=jnp.float32)
    scratch = [
        vmem((rows, levels, cols)),
        vmem((3, levels)),
        pltpu.SemaphoreType.DMA((2,)),
        pltpu.SemaphoreType.DMA,
        pltpu.SemaphoreType.REGULAR((2,)),
        vmem((wide, cols + 2 * FRONT, LANES)),
        vmem((wide, cols + 2 * FRONT, LANES)),
        vmem((2, REACH, levels, cols)),
        vmem((2, part, REACH, LANES)),
        vmem((2, part, REACH, LANES)),
        vmem((2, 2, REACH, REACH, LANES)),
        *[vmem((part_c, cols_c + 2 * FRONT, LANES))] * 4,
        vmem((wide_c, cols_c + 2 * FRONT, LANES)),
        vmem((wide_long, cols_c + 2 * FRONT, LANES)),
        vmem((wide_c - 2, cols_c + 2 * EDGE, LANES)),
        vmem((wide_long - 2, cols_c + 2 * EDGE, LANES)),
        vmem((wide_long - 2, cols_c + 2 * FRONT, LANES)),
        vmem((wide_c, cols_c + 2 * EDGE, LANES)),
        vmem((part_c, cols_c, LANES)),
        vmem((part_c, cols_c, LANES)),
        vmem((cols_c + 2 * FRONT, LANES)),
        vmem((cols, LANES)),
        vmem((TALLY, LANES)),
    ] + [pltpu.SemaphoreType.DMA] * 9
    for reach in (COARSE_REACH, COARSE_REACH, LONG_REACH, LONG_REACH):
        scratch += [
            vmem((2, reach // 2, cols_c, LANES)),
            vmem((2, reach // 2, cols_c + 2 * FRONT, LANES)),
            vmem((2, part_c, reach, LANES)),
            vmem((2, part_c, reach, LANES)),
            vmem((2, 2, reach // 2, reach, LANES)),
            vmem((2, 2, reach // 2, reach, LANES)),
        ]
    in_vmem = pl.BlockSpec(memory_space=pltpu.VMEM)
    handed = pl.pallas_call(
        functools.partial(kernel, sizes, levels, rows, cols),
        out_shape=(vmem((part, LANES, cols)), vmem((part_c + 2, cols_c + 2 * FRONT, LANES))),
        in_specs=[pl.BlockSpec(memory_space=pl.ANY)] * 3,
        out_specs=(in_vmem, in_vmem),
        scratch_shapes=scratch,
        compiler_params=pltpu.CompilerParams(collective_id=0, has_side_effects=True),
        name="parareal",
    )(state_starts.reshape(levels, rows, cols), diffusivity.reshape(1, levels), wind)
    ending = pl.pallas_call(
        functools.partial(closing, levels, rows),
        out_shape=jax.ShapeDtypeStruct((levels, rows, cols), jnp.float32),
        in_specs=[in_vmem, in_vmem],
        out_specs=pl.BlockSpec(memory_space=pl.ANY),
        scratch_shapes=[
            vmem((part, LANES, cols)),
            vmem((part_c + 2, LANES, cols)),
            pltpu.SemaphoreType.DMA,
        ],
        name="closing",
    )(*(pltpu.with_memory_space_constraint(array, pltpu.VMEM) for array in handed))
    return ending.reshape(1, levels, rows, cols)


def solution(mesh):
    sizes = tuple(mesh.shape[axis] for axis in ("tm", "gx", "gy"))
    placed = (P("tm", None, "gx", "gy"), P(), P())
    return jax.shard_map(
        functools.partial(shards, sizes),
        mesh=mesh, in_specs=placed, out_specs=P("tm", None, "gx", "gy"), check_vma=False,
    )
```

```python
import functools
import math

import jax
import jax.numpy as jnp
from jax import lax
from jax.experimental import pallas as pl
from jax.experimental.pallas import tpu as pltpu
from jax.sharding import PartitionSpec as P

SUB = 4
REACH = SUB
RATIO = 4
LANES = 128
EDGE = 8
FRONT = 2 * EDGE
COARSE_REACH = 2
LONG_REACH = 2 * COARSE_REACH
TALLY = 1024

time_step = 0.2
weights_low = (0.375, 0.125, 0.0, 0.0)
weights_mid = (0.625, 0.875, 0.875, 0.625)
weights_high = (0.0, 0.0, 0.125, 0.375)
mean_side, mean_mid = 0.125, 0.75

PLANE = tuple((dx, dy) for dx in (-1, 0, 1) for dy in (-1, 0, 1))
AROUND = tuple(d for d in PLANE if d != (0, 0))
x_moves = tuple(d for d in AROUND if d[1] == 0)
y_moves = tuple(d for d in AROUND if d[1] != 0)
side_moves = tuple(d for d in y_moves if d[0] == 0)
corner_moves = tuple(d for d in y_moves if d[0] != 0)


def conjunction(conditions):
    total = True
    for condition in conditions:
        total = condition if total is True else jnp.logical_and(total, condition)
    return total


def kernel(
    sizes, levels, rows, cols,
    x_hbm, diff_hbm, wind_hbm, turned, change,
    x_ref, small_ref, load_sems, small_sem, ready,
    first, second, x_recv, y_send, y_recv, corner_recv,
    old_own, new_own, prior_old_own, prior_new_own, extended, long_extended, old_image, prior_image, prior_change, lift,
    sent, fine_mean, line, fine_line, tally,
    out_sem, near_in, far_in, side_in_sem, corner_in_sem, old_in, chain_in, prior_old_in, prior_new_in, *strip_refs,
):
    n_tm, n_gx, n_gy = sizes
    tm, gx, gy = lax.axis_index("tm"), lax.axis_index("gx"), lax.axis_index("gy")
    packs = LANES // levels
    part = rows // packs
    part_c = part // RATIO
    cols_c = cols // RATIO
    wide = part + 2 * REACH
    wide_c = part_c + 2 * COARSE_REACH
    end = FRONT + cols
    end_c = FRONT + cols_c

    def there(dz, dx, dy):
        tests = []
        for place, move, count in ((tm, dz, n_tm), (gx, dx, n_gx), (gy, dy, n_gy)):
            if move < 0:
                tests.append(place >= -move)
            if move > 0:
                tests.append(place < count - move)
        return conjunction(tests)

    def guarded(condition, action):
        if condition is True:
            action()
        else:
            pl.when(condition)(action)

    def target(dz, dx, dy):
        return (tm + dz, gx + dx, gy + dy)

    rows_first = [*range(REACH), *range(part - REACH, part)]
    rows_later = [*range(REACH, part - REACH)]
    for group, group_rows in enumerate((rows_first, rows_later)):
        for row in group_rows:
            for x in range(row, rows, part):
                pltpu.make_async_copy(x_hbm.at[:, x], x_ref.at[x], load_sems.at[group]).start()
    for source, landing in ((diff_hbm, small_ref.at[pl.ds(0, 1)]), (wind_hbm, small_ref.at[pl.ds(1, 2)])):
        pltpu.make_async_copy(source, landing, small_sem).start()

    barrier = pltpu.get_barrier_semaphore()
    partners = [(0, dx, dy) for dx, dy in AROUND] + [(-1, 0, 0), (1, 0, 0)]
    partners.sort(key=lambda move: -sum(map(abs, move)))
    awaited = jnp.int32(0)
    for move in partners:
        def greet(move=move):
            pl.semaphore_signal(barrier, inc=1, device_id=target(*move), device_id_type=pl.DeviceIdType.MESH)
        guarded(there(*move), greet)
        awaited = awaited + there(*move).astype(jnp.int32)

    def send_all(copies, dz, moves):
        for move in moves:
            guarded(there(dz, *move), lambda move=move: copies[move].start())

    def sends_done(copies, dz, moves):
        for move in moves:
            guarded(there(dz, *move), lambda move=move: copies[move].wait_send())

    stand_ins, sizes_in_rows = {}, {}

    def fill_missing(copies, moves):
        for dx, dy in moves:
            @pl.when(jnp.logical_not(there(0, -dx, -dy)))
            def _(dx=dx, dy=dy):
                pltpu.make_async_copy(*stand_ins[id(copies)][dx, dy]).start()

    def all_arrived(copies, in_sem, moves):
        height = sum(sizes_in_rows[id(copies)][move] for move in moves)
        whole = tally.at[pl.ds(0, height)]
        pltpu.make_async_copy(whole, whole, in_sem).wait()

    def plan(copies, move, source, landing, in_sem, dz=0):
        copies[move] = remote(source, landing, in_sem, (dz, *move))
        stand_ins.setdefault(id(copies), {})[move] = (source, landing, in_sem)
        sizes_in_rows.setdefault(id(copies), {})[move] = math.prod(source.shape[:-1])

    def remote(source, landing, in_sem, move):
        return pltpu.make_async_remote_copy(
            src_ref=source, dst_ref=landing, send_sem=out_sem, recv_sem=in_sem,
            device_id=target(*move), device_id_type=pl.DeviceIdType.MESH,
        )

    fine_copies = {}
    for move in y_moves:
        dx, dy = move
        if dx == 0:
            source, landing, in_sem = y_send.at[(dy + 1) // 2], y_recv.at[(1 - dy) // 2], side_in_sem
        else:
            source = y_send.at[(dy + 1) // 2, pl.ds(0 if dx < 0 else part - REACH, REACH)]
            landing, in_sem = corner_recv.at[(1 - dx) // 2, (1 - dy) // 2], corner_in_sem
        plan(fine_copies, move, source, landing, in_sem)
    near, far = REACH // 2, REACH - REACH // 2
    near_copies, far_copies = {}, {}
    for dx in (-1, 1):
        low = dx < 0
        for copies, start, count, in_sem in (
            (near_copies, 0 if low else far, near, near_in), (far_copies, near if low else 0, far, far_in)
        ):
            source = x_ref.at[pl.ds(start if low else rows - REACH + start, count)]
            landing = x_recv.at[0 if low else 1, pl.ds(start, count)]
            plan(copies, (dx, 0), source, landing, in_sem)

    def coarse_copies(main, own_in, strips, in_sem, dz):
        row_out, row_in, side_out, side_in, corner_out, corner_in = strips
        copies = {}
        for dx, dy in PLANE if dz else AROUND:
            towards_x, towards_y = (dx + 1) // 2, (dy + 1) // 2
            if dx == 0 and dy == 0:
                source, landing = main, own_in.at[:, pl.ds(FRONT, cols_c)]
            elif dy == 0:
                source, landing = row_out.at[towards_x], row_in.at[towards_x, :, pl.ds(FRONT, cols_c)]
            elif dx == 0:
                source, landing = side_out.at[towards_y], side_in.at[towards_y]
            else:
                source, landing = corner_out.at[towards_x, towards_y], corner_in.at[towards_x, towards_y]
            plan(copies, (dx, dy), source, landing, in_sem, dz)
        return copies

    old_strips, new_strips, prior_old_strips, prior_new_strips = (strip_refs[6 * k : 6 * k + 6] for k in range(4))
    old_main = old_own.at[:, pl.ds(FRONT, cols_c)]
    old_copies = coarse_copies(None, old_own, old_strips, old_in, 0)
    chain_copies = coarse_copies(fine_mean, new_own, new_strips, chain_in, 1)
    prior_old_copies = coarse_copies(old_main, prior_old_own, prior_old_strips, prior_old_in, 1)
    prior_new_copies = coarse_copies(sent, prior_new_own, prior_new_strips, prior_new_in, 2)
    has_next, has_second = tm < n_tm - 1, tm < n_tm - 2

    lane = lax.broadcasted_iota(jnp.int32, (1, LANES), 1)
    pack = lane // levels

    def packed(row):
        return jnp.concatenate([row] * packs, axis=1)

    def advance(source, row, start, count, consts):
        keep, spread, along_x, along_y = consts
        centre = source[row, pl.ds(start, count), :]
        east = source[row + 1, pl.ds(start, count), :]
        west = source[row - 1, pl.ds(start, count), :]
        north = source[row, pl.ds(start + 1, count), :]
        south = source[row, pl.ds(start - 1, count), :]
        pushed = along_x * (east - west) + along_y * (north - south)
        return centre * (keep - pushed) + spread * ((east + west) + (north + south))

    def native_row(x):
        if x < 0:
            return x_recv[1, x + REACH]
        if x >= rows:
            return x_recv[0, x - rows]
        return x_ref[x]

    def bring_in(row):
        stacked = jnp.concatenate([native_row(p * part + row - REACH) for p in range(packs)], axis=0)
        first[row, pl.ds(FRONT, cols), :] = stacked.T

    low_lanes = lane < levels
    high_lanes = lane >= LANES - levels
    pl.semaphore_wait(barrier, awaited)

    def say_ready(k):
        @pl.when(tm > 0)
        def _():
            pl.semaphore_signal(
                ready.at[k], inc=1, device_id=target(-1, 0, 0), device_id_type=pl.DeviceIdType.MESH
            )

    say_ready(0)
    pltpu.make_async_copy(small_ref, small_ref, small_sem).wait()
    diffuse = packed(small_ref[0:1, :])
    east_wind = packed(small_ref[1:2, :])
    north_wind = packed(small_ref[2:3, :])

    def constants(factor):
        spread = (time_step * factor) * diffuse
        return 1.0 - 4.0 * spread, spread, (0.5 * time_step) * east_wind, (0.5 * time_step) * north_wind

    fine_constants = constants(1.0)
    coarse_constants = constants(0.25)

    def load_done(group, group_rows):
        whole = x_ref.at[pl.ds(0, packs * len(group_rows))]
        pltpu.make_async_copy(whole, whole, load_sems.at[group]).wait()

    def bring_own(group_rows):
        for row in group_rows:
            bring_in(REACH + row)
            y_send[0, row] = first[REACH + row, pl.ds(FRONT, REACH), :]
            y_send[1, row] = first[REACH + row, pl.ds(end - REACH, REACH), :]

    load_done(0, rows_first)
    bring_own(rows_first)
    send_all(fine_copies, 0, corner_moves)
    send_all(near_copies, 0, x_moves)
    load_done(1, rows_later)
    bring_own(rows_later)
    send_all(fine_copies, 0, side_moves)

    def restricted(source, row):
        total = source[REACH + row * RATIO, pl.ds(FRONT, cols), :]
        for r in range(1, RATIO):
            total = total + source[REACH + row * RATIO + r, pl.ds(FRONT, cols), :]
        fine_line[...] = total
        mean = fine_line[pl.ds(0, cols_c, stride=RATIO), :]
        for o in range(1, RATIO):
            mean = mean + fine_line[pl.ds(o, cols_c, stride=RATIO), :]
        return mean * (1.0 / RATIO**2)

    def swapped(value):
        return pltpu.roll(value, levels, 1)

    def pack_strips(row_of, strips, reach):
        row_out, _, side_out, _, corner_out, _ = strips
        for k in range(reach // 2):
            after, before = 2 * k, part_c - 2 * k - 2
            row_out[0, k] = jnp.where(low_lanes, row_of(after, 0, cols_c), swapped(row_of(after + 1, 0, cols_c)))
            row_out[1, k] = jnp.where(low_lanes, swapped(row_of(before, 0, cols_c)), row_of(before + 1, 0, cols_c))
        for side, col in ((0, 0), (1, cols_c - reach)):
            for row in range(part_c):
                side_out[side, row] = row_of(row, col, reach)
            for towards in range(2):
                for k in range(reach // 2):
                    corner_out[towards, side, k] = row_out[towards, k, pl.ds(col, reach), :]

    def old_row(row, col, count):
        return old_own[row, pl.ds(FRONT + col, count), :]

    for row in range(part_c):
        old_own[row, pl.ds(FRONT, cols_c), :] = restricted(first, row)
    pack_strips(old_row, old_strips, COARSE_REACH)
    send_all(far_copies, 0, x_moves)
    send_all(old_copies, 0, AROUND)

    def inside_x(row, reach, length):
        place = (gx * packs + pack) * length + (row - reach)
        return jnp.logical_and(place >= 0, place < n_gx * packs * length)

    def inside_y(start, count, length):
        place = gy * length + (start - FRONT) + lax.broadcasted_iota(jnp.int32, (count, LANES), 0)
        return jnp.logical_and(place >= 0, place < n_gy * length)

    edges = ((FRONT - EDGE, inside_y(FRONT - EDGE, EDGE, cols)), (end, inside_y(end, EDGE, cols)))
    reaches = ((FRONT - REACH, inside_y(FRONT - REACH, REACH, cols)), (end, inside_y(end, REACH, cols)))
    half = cols // 2

    def fill(source, dest, row, start, count, consts):
        dest[row, pl.ds(start, count), :] = advance(source, row, start, count, consts)

    def fill_edges(source, dest, row, consts):
        for start, mask in edges:
            value = advance(source, row, start, EDGE, consts)
            dest[row, pl.ds(start, EDGE), :] = jnp.where(mask, value, 0.0)

    def update(source, dest, row, consts, last):
        for start, count in ((FRONT, half), (FRONT + half, cols - half)):
            fill(source, dest, row, start, count, consts)
        if not last:
            fill_edges(source, dest, row, consts)

    buffers = (first, second)

    def inner_steps(row_update):
        for step in range(1, SUB + 1):
            def inner_row(row, step=step):
                row_update(buffers[(step - 1) % 2], buffers[step % 2], row, step)

            pl.loop(REACH + step, REACH + part - step, unroll=2)(inner_row)

    def centre_update(source, dest, row, step):
        fill(source, dest, row, FRONT + EDGE * step, half - EDGE * step, fine_constants)
        fill(source, dest, row, FRONT + half, cols - half - EDGE * step, fine_constants)

    def sides_update(source, dest, row, step):
        fill(source, dest, row, FRONT, EDGE * step, fine_constants)
        fill(source, dest, row, end - EDGE * step, EDGE * step, fine_constants)
        if step < SUB:
            fill_edges(source, dest, row, fine_constants)

    fill_missing(fine_copies, side_moves)
    fill_missing(fine_copies, corner_moves)
    fill_missing(near_copies, x_moves)
    fill_missing(far_copies, x_moves)
    fill_missing(old_copies, AROUND)
    inner_steps(centre_update)

    @pl.when(has_next)
    def _():
        pl.semaphore_wait(ready.at[0], 1)
        say_ready(1)
        pack_strips(old_row, prior_old_strips, LONG_REACH)
        send_all(prior_old_copies, 1, (*side_moves, (0, 0)))

    @pl.when(tm > 0)
    def _():
        fill_missing(prior_old_copies, AROUND)

    all_arrived(fine_copies, side_in_sem, side_moves)
    for side, (start, mask) in enumerate(reaches):
        for row in range(part):
            first[REACH + row, pl.ds(start, REACH), :] = jnp.where(mask, y_recv[side, row], 0.0)
    inner_steps(sides_update)

    def bring_halo(halo_rows):
        for row in halo_rows:
            bring_in(row)
            inner = first[row, pl.ds(FRONT, cols), :]
            first[row, pl.ds(FRONT, cols), :] = jnp.where(inside_x(row, REACH, part), inner, 0.0)
        for side, (start, mask_side) in enumerate(reaches):
            for row in halo_rows:
                if row < REACH:
                    here = jnp.where(high_lanes, corner_recv[0, side, row], y_recv[side, row + part - REACH])
                    here = pltpu.roll(here, levels, 1)
                else:
                    at = row - part - REACH
                    here = pltpu.roll(jnp.where(low_lanes, corner_recv[1, side, at], y_recv[side, at]), LANES - levels, 1)
                mask = jnp.logical_and(mask_side, inside_x(row, REACH, part))
                first[row, pl.ds(start, REACH), :] = jnp.where(mask, here, 0.0)

    def outer_steps(low_shift, high_shift, count):
        for step in range(1, SUB + 1):
            def outer_row(k, step=step):
                for row in (step + low_shift + k, part + REACH - step + high_shift + k):
                    mask_x = inside_x(row, REACH, part)
                    consts = tuple(jnp.where(mask_x, c, 0.0) for c in fine_constants)
                    update(buffers[(step - 1) % 2], buffers[step % 2], row, consts, step == SUB)

            pl.loop(0, count)(outer_row)

    all_arrived(near_copies, near_in, x_moves)
    pl.when(has_next)(lambda: send_all(prior_old_copies, 1, x_moves + corner_moves))
    all_arrived(fine_copies, corner_in_sem, corner_moves)
    bring_halo([*range(far, REACH), *range(REACH + part, REACH + part + near)])
    outer_steps(far, 0, near)

    all_arrived(far_copies, far_in, x_moves)
    bring_halo([*range(far), *range(REACH + part + near, wide)])
    outer_steps(0, near, far)
    fine = buffers[SUB % 2]

    for row in range(part_c):
        fine_mean[row] = restricted(fine, row)

    @pl.when(has_next)
    def _():
        pack_strips(lambda row, col, count: fine_mean[row, pl.ds(col, count), :], new_strips, COARSE_REACH)
        send_all(chain_copies, 1, AROUND)
        send_all(chain_copies, 1, ((0, 0),))

    count_c = cols_c + 2 * EDGE
    begin_c = FRONT - EDGE
    across = pl.ds(begin_c, count_c)
    mask_y = inside_y(begin_c, count_c, cols_c)
    place_c = lax.broadcasted_iota(jnp.int32, (count_c, LANES), 0) - EDGE
    mask_near = jnp.logical_and(mask_y, jnp.logical_and(place_c >= -1, place_c <= cols_c))

    def extend(buffer, strips, target, reach):
        _, row_in, _, side_in, _, corner_in = strips
        for side, col in ((0, end_c), (1, FRONT - reach)):
            for row in range(part_c):
                buffer[row, pl.ds(col, reach), :] = side_in[side, row]
            for towards in range(2):
                for k in range(reach // 2):
                    row_in[towards, k, pl.ds(col, reach), :] = corner_in[towards, side, k]

        def own(row):
            return buffer[row, across, :]

        values = [own(row) for row in range(part_c)]
        for k in range(reach // 2):
            above, below = (row_in[towards, k, across, :] for towards in (0, 1))
            after, before = 2 * k, part_c - 2 * k - 2
            values = [
                jnp.where(low_lanes, below, swapped(own(before))),
                swapped(jnp.where(high_lanes, below, own(before + 1))),
                *values,
                swapped(jnp.where(low_lanes, above, own(after))),
                jnp.where(high_lanes, above, swapped(own(after + 1))),
            ]
        for row, value in enumerate(values):
            mask = mask_y
            if not reach <= row < reach + part_c:
                mask = jnp.logical_and(mask_y, inside_x(row, reach, part_c))
            target[row, across, :] = jnp.where(mask, value, 0.0)

    def image_of(source, image):
        for row in range(image.shape[0]):
            image[row] = advance(source, row + 1, begin_c, count_c, coarse_constants)

    def change_of(source, image, reach, result):
        for row in range(image.shape[0]):
            moved = advance(source, row + 1, begin_c, count_c, coarse_constants) - image[row]
            columns = mask_near if reach == COARSE_REACH else mask_y
            mask = jnp.logical_and(columns, inside_x(row + 1, reach, part_c))
            result[row, across, :] = jnp.where(mask, moved, 0.0)

    def smoothed(source, row, start, count):
        line[across, :] = (
            mean_side * (source[row, across, :] + source[row + 2, across, :]) + mean_mid * source[row + 1, across, :]
        )
        sides = line[pl.ds(start - 1, count), :] + line[pl.ds(start + 1, count), :]
        return mean_side * sides + mean_mid * line[pl.ds(start, count), :]

    def find_lift(put):
        change_of(long_extended, prior_image, LONG_REACH, prior_change)
        for row in range(wide_c):
            mask = jnp.logical_and(mask_y, inside_x(row, COARSE_REACH, part_c))
            put(row, jnp.where(mask, smoothed(prior_change, row, begin_c, count_c), 0.0))

    def keep_lift(row, value):
        lift[row] = value

    def add_lift(row, value):
        extended[row, across, :] = extended[row, across, :] + value

    all_arrived(old_copies, old_in, AROUND)
    extend(old_own, old_strips, extended, COARSE_REACH)
    image_of(extended, old_image)
    def send_on():
        for row in range(part_c):
            sent[row] = fine_mean[row] + smoothed(change, row, FRONT, cols_c)
        pack_strips(lambda row, col, count: sent[row, pl.ds(col, count), :], prior_new_strips, LONG_REACH)
        pl.semaphore_wait(ready.at[1], 1)
        send_all(prior_new_copies, 2, AROUND)
        send_all(prior_new_copies, 2, ((0, 0),))

    @pl.when(tm == 0)
    def _():
        change_of(extended, old_image, COARSE_REACH, change)
        pl.when(has_second)(send_on)

    @pl.when(tm > 0)
    def _():
        fill_missing(chain_copies, AROUND)

    @pl.when(tm > 1)
    def _():
        fill_missing(prior_new_copies, AROUND)

    for row in range(part):
        turned[row] = fine[REACH + row, pl.ds(FRONT, cols), :].T

    @pl.when(tm > 0)
    def _():
        all_arrived(prior_old_copies, prior_old_in, PLANE)
        extend(prior_old_own, prior_old_strips, long_extended, LONG_REACH)
        image_of(long_extended, prior_image)
        pl.when(tm == 1)(lambda: find_lift(keep_lift))
        all_arrived(chain_copies, chain_in, PLANE)
        extend(new_own, new_strips, extended, COARSE_REACH)

        @pl.when(tm > 1)
        def _():
            all_arrived(prior_new_copies, prior_new_in, PLANE)
            extend(prior_new_own, prior_new_strips, long_extended, LONG_REACH)
            find_lift(add_lift)

        @pl.when(tm == 1)
        def _():
            for row in range(wide_c):
                add_lift(row, lift[row])

        change_of(extended, old_image, COARSE_REACH, change)
        pl.when(has_second)(send_on)

    sends_done(fine_copies, 0, y_moves)
    sends_done(old_copies, 0, AROUND)
    sends_done(near_copies, 0, x_moves)
    sends_done(far_copies, 0, x_moves)
    @pl.when(has_next)
    def _():
        sends_done(chain_copies, 1, PLANE)
        sends_done(prior_old_copies, 1, PLANE)

    pl.when(has_second)(lambda: sends_done(prior_new_copies, 2, PLANE))


def closing(levels, rows, turned, change, out_hbm, filled, spread_rows, sem):
    packs = LANES // levels
    part, _, cols = turned.shape
    part_c = part // RATIO
    count_c = cols // RATIO + 2 * EDGE
    coarse_col = lax.broadcasted_iota(jnp.int32, (count_c, cols), 0) - EDGE
    fine_col = lax.broadcasted_iota(jnp.int32, (count_c, cols), 1)
    offset_of = fine_col & (RATIO - 1)
    apart = coarse_col - (fine_col >> (RATIO.bit_length() - 1))
    spreading = jnp.zeros((count_c, cols), jnp.float32)
    for o in range(RATIO):
        for distance, weights in ((-1, weights_low), (0, weights_mid), (1, weights_high)):
            chosen = jnp.logical_and(offset_of == o, apart == distance)
            spreading = jnp.where(chosen, weights[o], spreading)
    spreading = jnp.concatenate([spreading.astype(jnp.bfloat16)] * 3, axis=0)

    def spread_row(row):
        rest, pieces = change[row, pl.ds(FRONT - EDGE, count_c), :], []
        for _ in range(3):
            piece = rest.astype(jnp.bfloat16).astype(jnp.float32)
            pieces.append(piece)
            rest = rest - piece
        split = jnp.concatenate(pieces, axis=0).T.astype(jnp.bfloat16)
        return jnp.dot(split, spreading, preferred_element_type=jnp.float32)

    for row in range(2):
        spread_rows[row] = spread_row(row)
    for row in range(part):
        at, o = row // RATIO, row % RATIO
        if o == 0:
            spread_rows[at + 2] = spread_row(at + 2)
        total = turned[row] + weights_mid[o] * spread_rows[at + 1]
        if weights_low[o]:
            total = total + weights_low[o] * spread_rows[at]
        if weights_high[o]:
            total = total + weights_high[o] * spread_rows[at + 2]
        filled[row] = total
        for p in range(packs):
            x = p * part + row
            pltpu.make_async_copy(filled.at[row, pl.ds(p * levels, levels)], out_hbm.at[:, x], sem).start()
    pltpu.make_async_copy(filled, filled, sem).wait()


def shards(sizes, state_starts, diffusivity, wind):
    _, levels, rows, cols = state_starts.shape
    packs = LANES // levels
    if packs != 2 or levels * packs != LANES:
        raise ValueError(levels)
    part = rows // packs
    part_c = part // RATIO
    cols_c = cols // RATIO
    wide, wide_c, wide_long = part + 2 * REACH, part_c + 2 * COARSE_REACH, part_c + 2 * LONG_REACH
    if part_c < LONG_REACH:
        raise ValueError(part_c)
    vmem = functools.partial(pltpu.VMEM, dtype=jnp.float32)
    scratch = [
        vmem((rows, levels, cols)),
        vmem((3, levels)),
        pltpu.SemaphoreType.DMA((2,)),
        pltpu.SemaphoreType.DMA,
        pltpu.SemaphoreType.REGULAR((2,)),
        vmem((wide, cols + 2 * FRONT, LANES)),
        vmem((wide, cols + 2 * FRONT, LANES)),
        vmem((2, REACH, levels, cols)),
        vmem((2, part, REACH, LANES)),
        vmem((2, part, REACH, LANES)),
        vmem((2, 2, REACH, REACH, LANES)),
        *[vmem((part_c, cols_c + 2 * FRONT, LANES))] * 4,
        vmem((wide_c, cols_c + 2 * FRONT, LANES)),
        vmem((wide_long, cols_c + 2 * FRONT, LANES)),
        vmem((wide_c - 2, cols_c + 2 * EDGE, LANES)),
        vmem((wide_long - 2, cols_c + 2 * EDGE, LANES)),
        vmem((wide_long - 2, cols_c + 2 * FRONT, LANES)),
        vmem((wide_c, cols_c + 2 * EDGE, LANES)),
        vmem((part_c, cols_c, LANES)),
        vmem((part_c, cols_c, LANES)),
        vmem((cols_c + 2 * FRONT, LANES)),
        vmem((cols, LANES)),
        vmem((TALLY, LANES)),
    ] + [pltpu.SemaphoreType.DMA] * 9
    for reach in (COARSE_REACH, COARSE_REACH, LONG_REACH, LONG_REACH):
        scratch += [
            vmem((2, reach // 2, cols_c, LANES)),
            vmem((2, reach // 2, cols_c + 2 * FRONT, LANES)),
            vmem((2, part_c, reach, LANES)),
            vmem((2, part_c, reach, LANES)),
            vmem((2, 2, reach // 2, reach, LANES)),
            vmem((2, 2, reach // 2, reach, LANES)),
        ]
    in_vmem = pl.BlockSpec(memory_space=pltpu.VMEM)
    handed = pl.pallas_call(
        functools.partial(kernel, sizes, levels, rows, cols),
        out_shape=(vmem((part, LANES, cols)), vmem((part_c + 2, cols_c + 2 * FRONT, LANES))),
        in_specs=[pl.BlockSpec(memory_space=pl.ANY)] * 3,
        out_specs=(in_vmem, in_vmem),
        scratch_shapes=scratch,
        compiler_params=pltpu.CompilerParams(collective_id=0, has_side_effects=True),
        name="parareal",
    )(state_starts.reshape(levels, rows, cols), diffusivity.reshape(1, levels), wind)
    ending = pl.pallas_call(
        functools.partial(closing, levels, rows),
        out_shape=jax.ShapeDtypeStruct((levels, rows, cols), jnp.float32),
        in_specs=[in_vmem, in_vmem],
        out_specs=pl.BlockSpec(memory_space=pl.ANY),
        scratch_shapes=[
            vmem((part, LANES, cols)),
            vmem((part_c + 2, LANES, cols)),
            pltpu.SemaphoreType.DMA,
        ],
        name="closing",
    )(*(pltpu.with_memory_space_constraint(array, pltpu.VMEM) for array in handed))
    return ending.reshape(1, levels, rows, cols)


def solution(mesh):
    sizes = tuple(mesh.shape[axis] for axis in ("tm", "gx", "gy"))
    placed = (P("tm", None, "gx", "gy"), P(), P())
    return jax.shard_map(
        functools.partial(shards, sizes),
        mesh=mesh, in_specs=placed, out_specs=P("tm", None, "gx", "gy"), check_vma=False,
    )
```

```python
import functools
import math

import jax
import jax.numpy as jnp
from jax import lax
from jax.experimental import pallas as pl
from jax.experimental.pallas import tpu as pltpu
from jax.sharding import PartitionSpec as P

SUB = 4
REACH = SUB
RATIO = 4
LANES = 128
EDGE = 8
FRONT = 2 * EDGE
COARSE_REACH = 2
LONG_REACH = 2 * COARSE_REACH
TALLY = 1024

time_step = 0.2
weights_low = (0.375, 0.125, 0.0, 0.0)
weights_mid = (0.625, 0.875, 0.875, 0.625)
weights_high = (0.0, 0.0, 0.125, 0.375)
mean_side, mean_mid = 0.125, 0.75

PLANE = tuple((dx, dy) for dx in (-1, 0, 1) for dy in (-1, 0, 1))
AROUND = tuple(d for d in PLANE if d != (0, 0))
x_moves = tuple(d for d in AROUND if d[1] == 0)
y_moves = tuple(d for d in AROUND if d[1] != 0)
side_moves = tuple(d for d in y_moves if d[0] == 0)
corner_moves = tuple(d for d in y_moves if d[0] != 0)


def conjunction(conditions):
    total = True
    for condition in conditions:
        total = condition if total is True else jnp.logical_and(total, condition)
    return total


def kernel(
    sizes, levels, rows, cols,
    x_hbm, diff_hbm, wind_hbm, turned, change,
    x_ref, small_ref, load_sems, small_sem, ready,
    first, second, x_recv, y_send, y_recv, corner_recv,
    old_own, new_own, prior_old_own, prior_new_own, extended, long_extended, old_image, prior_image, prior_change, lift,
    sent, fine_mean, line, fine_line, tally,
    out_sem, near_in, far_in, side_in_sem, corner_in_sem, old_in, chain_in, prior_old_in, prior_new_in, *strip_refs,
):
    n_tm, n_gx, n_gy = sizes
    tm, gx, gy = lax.axis_index("tm"), lax.axis_index("gx"), lax.axis_index("gy")
    packs = LANES // levels
    part = rows // packs
    part_c = part // RATIO
    cols_c = cols // RATIO
    wide = part + 2 * REACH
    wide_c = part_c + 2 * COARSE_REACH
    end = FRONT + cols
    end_c = FRONT + cols_c

    def there(dz, dx, dy):
        tests = []
        for place, move, count in ((tm, dz, n_tm), (gx, dx, n_gx), (gy, dy, n_gy)):
            if move < 0:
                tests.append(place >= -move)
            if move > 0:
                tests.append(place < count - move)
        return conjunction(tests)

    def guarded(condition, action):
        if condition is True:
            action()
        else:
            pl.when(condition)(action)

    def target(dz, dx, dy):
        return (tm + dz, gx + dx, gy + dy)

    rows_first = [*range(REACH), *range(part - REACH, part)]
    rows_later = [*range(REACH, part - REACH)]
    for group, group_rows in enumerate((rows_first, rows_later)):
        for row in group_rows:
            for x in range(row, rows, part):
                pltpu.make_async_copy(x_hbm.at[:, x], x_ref.at[x], load_sems.at[group]).start()
    for source, landing in ((diff_hbm, small_ref.at[pl.ds(0, 1)]), (wind_hbm, small_ref.at[pl.ds(1, 2)])):
        pltpu.make_async_copy(source, landing, small_sem).start()

    barrier = pltpu.get_barrier_semaphore()
    partners = [(0, dx, dy) for dx, dy in AROUND] + [(-1, 0, 0), (1, 0, 0)]
    partners.sort(key=lambda move: -sum(map(abs, move)))
    awaited = jnp.int32(0)
    for move in partners:
        def greet(move=move):
            pl.semaphore_signal(barrier, inc=1, device_id=target(*move), device_id_type=pl.DeviceIdType.MESH)
        guarded(there(*move), greet)
        awaited = awaited + there(*move).astype(jnp.int32)

    def send_all(copies, dz, moves):
        for move in moves:
            guarded(there(dz, *move), lambda move=move: copies[move].start())

    def sends_done(copies, dz, moves):
        for move in moves:
            guarded(there(dz, *move), lambda move=move: copies[move].wait_send())

    stand_ins, sizes_in_rows = {}, {}

    def fill_missing(copies, moves):
        for dx, dy in moves:
            @pl.when(jnp.logical_not(there(0, -dx, -dy)))
            def _(dx=dx, dy=dy):
                pltpu.make_async_copy(*stand_ins[id(copies)][dx, dy]).start()

    def all_arrived(copies, in_sem, moves):
        height = sum(sizes_in_rows[id(copies)][move] for move in moves)
        whole = tally.at[pl.ds(0, height)]
        pltpu.make_async_copy(whole, whole, in_sem).wait()

    def plan(copies, move, source, landing, in_sem, dz=0):
        copies[move] = remote(source, landing, in_sem, (dz, *move))
        stand_ins.setdefault(id(copies), {})[move] = (source, landing, in_sem)
        sizes_in_rows.setdefault(id(copies), {})[move] = math.prod(source.shape[:-1])

    def remote(source, landing, in_sem, move):
        return pltpu.make_async_remote_copy(
            src_ref=source, dst_ref=landing, send_sem=out_sem, recv_sem=in_sem,
            device_id=target(*move), device_id_type=pl.DeviceIdType.MESH,
        )

    fine_copies = {}
    for move in y_moves:
        dx, dy = move
        if dx == 0:
            source, landing, in_sem = y_send.at[(dy + 1) // 2], y_recv.at[(1 - dy) // 2], side_in_sem
        else:
            source = y_send.at[(dy + 1) // 2, pl.ds(0 if dx < 0 else part - REACH, REACH)]
            landing, in_sem = corner_recv.at[(1 - dx) // 2, (1 - dy) // 2], corner_in_sem
        plan(fine_copies, move, source, landing, in_sem)
    near, far = REACH // 2, REACH - REACH // 2
    near_copies, far_copies = {}, {}
    for dx in (-1, 1):
        low = dx < 0
        for copies, start, count, in_sem in (
            (near_copies, 0 if low else far, near, near_in), (far_copies, near if low else 0, far, far_in)
        ):
            source = x_ref.at[pl.ds(start if low else rows - REACH + start, count)]
            landing = x_recv.at[0 if low else 1, pl.ds(start, count)]
            plan(copies, (dx, 0), source, landing, in_sem)

    def coarse_copies(main, own_in, strips, in_sem, dz):
        row_out, row_in, side_out, side_in, corner_out, corner_in = strips
        copies = {}
        for dx, dy in PLANE if dz else AROUND:
            towards_x, towards_y = (dx + 1) // 2, (dy + 1) // 2
            if dx == 0 and dy == 0:
                source, landing = main, own_in.at[:, pl.ds(FRONT, cols_c)]
            elif dy == 0:
                source, landing = row_out.at[towards_x], row_in.at[towards_x, :, pl.ds(FRONT, cols_c)]
            elif dx == 0:
                source, landing = side_out.at[towards_y], side_in.at[towards_y]
            else:
                source, landing = corner_out.at[towards_x, towards_y], corner_in.at[towards_x, towards_y]
            plan(copies, (dx, dy), source, landing, in_sem, dz)
        return copies

    old_strips, new_strips, prior_old_strips, prior_new_strips = (strip_refs[6 * k : 6 * k + 6] for k in range(4))
    old_main = old_own.at[:, pl.ds(FRONT, cols_c)]
    old_copies = coarse_copies(None, old_own, old_strips, old_in, 0)
    chain_copies = coarse_copies(fine_mean, new_own, new_strips, chain_in, 1)
    prior_old_copies = coarse_copies(old_main, prior_old_own, prior_old_strips, prior_old_in, 1)
    prior_new_copies = coarse_copies(sent, prior_new_own, prior_new_strips, prior_new_in, 2)
    has_next, has_second = tm < n_tm - 1, tm < n_tm - 2

    lane = lax.broadcasted_iota(jnp.int32, (1, LANES), 1)
    pack = lane // levels

    def packed(row):
        return jnp.concatenate([row] * packs, axis=1)

    def advance(source, row, start, count, consts):
        keep, spread, along_x, along_y = consts
        centre = source[row, pl.ds(start, count), :]
        east = source[row + 1, pl.ds(start, count), :]
        west = source[row - 1, pl.ds(start, count), :]
        north = source[row, pl.ds(start + 1, count), :]
        south = source[row, pl.ds(start - 1, count), :]
        pushed = along_x * (east - west) + along_y * (north - south)
        return centre * (keep - pushed) + spread * ((east + west) + (north + south))

    def native_row(x):
        if x < 0:
            return x_recv[1, x + REACH]
        if x >= rows:
            return x_recv[0, x - rows]
        return x_ref[x]

    def bring_in(row):
        stacked = jnp.concatenate([native_row(p * part + row - REACH) for p in range(packs)], axis=0)
        first[row, pl.ds(FRONT, cols), :] = stacked.T

    low_lanes = lane < levels
    high_lanes = lane >= LANES - levels
    pl.semaphore_wait(barrier, awaited)

    def say_ready(k):
        @pl.when(tm > 0)
        def _():
            pl.semaphore_signal(
                ready.at[k], inc=1, device_id=target(-1, 0, 0), device_id_type=pl.DeviceIdType.MESH
            )

    say_ready(0)
    pltpu.make_async_copy(small_ref, small_ref, small_sem).wait()
    diffuse = packed(small_ref[0:1, :])
    east_wind = packed(small_ref[1:2, :])
    north_wind = packed(small_ref[2:3, :])

    def constants(factor):
        spread = (time_step * factor) * diffuse
        return 1.0 - 4.0 * spread, spread, (0.5 * time_step) * east_wind, (0.5 * time_step) * north_wind

    fine_constants = constants(1.0)
    coarse_constants = constants(0.25)

    def load_done(group, group_rows):
        whole = x_ref.at[pl.ds(0, packs * len(group_rows))]
        pltpu.make_async_copy(whole, whole, load_sems.at[group]).wait()

    def bring_own(group_rows):
        for row in group_rows:
            bring_in(REACH + row)
            y_send[0, row] = first[REACH + row, pl.ds(FRONT, REACH), :]
            y_send[1, row] = first[REACH + row, pl.ds(end - REACH, REACH), :]

    load_done(0, rows_first)
    bring_own(rows_first)
    send_all(fine_copies, 0, corner_moves)
    send_all(near_copies, 0, x_moves)
    load_done(1, rows_later)
    bring_own(rows_later)
    send_all(fine_copies, 0, side_moves)

    def restricted(source, row):
        total = source[REACH + row * RATIO, pl.ds(FRONT, cols), :]
        for r in range(1, RATIO):
            total = total + source[REACH + row * RATIO + r, pl.ds(FRONT, cols), :]
        fine_line[...] = total
        mean = fine_line[pl.ds(0, cols_c, stride=RATIO), :]
        for o in range(1, RATIO):
            mean = mean + fine_line[pl.ds(o, cols_c, stride=RATIO), :]
        return mean * (1.0 / RATIO**2)

    def swapped(value):
        return pltpu.roll(value, levels, 1)

    def pack_strips(row_of, strips, reach):
        row_out, _, side_out, _, corner_out, _ = strips
        for k in range(reach // 2):
            after, before = 2 * k, part_c - 2 * k - 2
            row_out[0, k] = jnp.where(low_lanes, row_of(after, 0, cols_c), swapped(row_of(after + 1, 0, cols_c)))
            row_out[1, k] = jnp.where(low_lanes, swapped(row_of(before, 0, cols_c)), row_of(before + 1, 0, cols_c))
        for side, col in ((0, 0), (1, cols_c - reach)):
            for row in range(part_c):
                side_out[side, row] = row_of(row, col, reach)
            for towards in range(2):
                for k in range(reach // 2):
                    corner_out[towards, side, k] = row_out[towards, k, pl.ds(col, reach), :]

    def old_row(row, col, count):
        return old_own[row, pl.ds(FRONT + col, count), :]

    for row in range(part_c):
        old_own[row, pl.ds(FRONT, cols_c), :] = restricted(first, row)
    pack_strips(old_row, old_strips, COARSE_REACH)
    send_all(far_copies, 0, x_moves)
    send_all(old_copies, 0, AROUND)

    def inside_x(row, reach, length):
        place = (gx * packs + pack) * length + (row - reach)
        return jnp.logical_and(place >= 0, place < n_gx * packs * length)

    def inside_y(start, count, length):
        place = gy * length + (start - FRONT) + lax.broadcasted_iota(jnp.int32, (count, LANES), 0)
        return jnp.logical_and(place >= 0, place < n_gy * length)

    edges = ((FRONT - EDGE, inside_y(FRONT - EDGE, EDGE, cols)), (end, inside_y(end, EDGE, cols)))
    reaches = ((FRONT - REACH, inside_y(FRONT - REACH, REACH, cols)), (end, inside_y(end, REACH, cols)))
    half = cols // 2

    def fill(source, dest, row, start, count, consts):
        dest[row, pl.ds(start, count), :] = advance(source, row, start, count, consts)

    def fill_edges(source, dest, row, consts):
        for start, mask in edges:
            value = advance(source, row, start, EDGE, consts)
            dest[row, pl.ds(start, EDGE), :] = jnp.where(mask, value, 0.0)

    def update(source, dest, row, consts, last):
        for start, count in ((FRONT, half), (FRONT + half, cols - half)):
            fill(source, dest, row, start, count, consts)
        if not last:
            fill_edges(source, dest, row, consts)

    buffers = (first, second)

    def inner_steps(row_update):
        for step in range(1, SUB + 1):
            def inner_row(row, step=step):
                row_update(buffers[(step - 1) % 2], buffers[step % 2], row, step)

            pl.loop(REACH + step, REACH + part - step, unroll=2)(inner_row)

    def centre_update(source, dest, row, step):
        fill(source, dest, row, FRONT + EDGE * step, half - EDGE * step, fine_constants)
        fill(source, dest, row, FRONT + half, cols - half - EDGE * step, fine_constants)

    def sides_update(source, dest, row, step):
        fill(source, dest, row, FRONT, EDGE * step, fine_constants)
        fill(source, dest, row, end - EDGE * step, EDGE * step, fine_constants)
        if step < SUB:
            fill_edges(source, dest, row, fine_constants)

    fill_missing(fine_copies, side_moves)
    fill_missing(fine_copies, corner_moves)
    fill_missing(near_copies, x_moves)
    fill_missing(far_copies, x_moves)
    fill_missing(old_copies, AROUND)
    inner_steps(centre_update)

    @pl.when(has_next)
    def _():
        pl.semaphore_wait(ready.at[0], 1)
        say_ready(1)
        pack_strips(old_row, prior_old_strips, LONG_REACH)
        send_all(prior_old_copies, 1, (*side_moves, (0, 0)))

    @pl.when(tm > 0)
    def _():
        fill_missing(prior_old_copies, AROUND)

    all_arrived(fine_copies, side_in_sem, side_moves)
    for side, (start, mask) in enumerate(reaches):
        for row in range(part):
            first[REACH + row, pl.ds(start, REACH), :] = jnp.where(mask, y_recv[side, row], 0.0)
    inner_steps(sides_update)

    def bring_halo(halo_rows):
        for row in halo_rows:
            bring_in(row)
            inner = first[row, pl.ds(FRONT, cols), :]
            first[row, pl.ds(FRONT, cols), :] = jnp.where(inside_x(row, REACH, part), inner, 0.0)
        for side, (start, mask_side) in enumerate(reaches):
            for row in halo_rows:
                if row < REACH:
                    here = jnp.where(high_lanes, corner_recv[0, side, row], y_recv[side, row + part - REACH])
                    here = pltpu.roll(here, levels, 1)
                else:
                    at = row - part - REACH
                    here = pltpu.roll(jnp.where(low_lanes, corner_recv[1, side, at], y_recv[side, at]), LANES - levels, 1)
                mask = jnp.logical_and(mask_side, inside_x(row, REACH, part))
                first[row, pl.ds(start, REACH), :] = jnp.where(mask, here, 0.0)

    def outer_steps(low_shift, high_shift, count):
        for step in range(1, SUB + 1):
            def outer_row(k, step=step):
                for row in (step + low_shift + k, part + REACH - step + high_shift + k):
                    mask_x = inside_x(row, REACH, part)
                    consts = tuple(jnp.where(mask_x, c, 0.0) for c in fine_constants)
                    update(buffers[(step - 1) % 2], buffers[step % 2], row, consts, step == SUB)

            pl.loop(0, count)(outer_row)

    all_arrived(near_copies, near_in, x_moves)
    pl.when(has_next)(lambda: send_all(prior_old_copies, 1, x_moves + corner_moves))
    all_arrived(fine_copies, corner_in_sem, corner_moves)
    bring_halo([*range(far, REACH), *range(REACH + part, REACH + part + near)])
    outer_steps(far, 0, near)

    all_arrived(far_copies, far_in, x_moves)
    bring_halo([*range(far), *range(REACH + part + near, wide)])
    outer_steps(0, near, far)
    fine = buffers[SUB % 2]

    for row in range(part_c):
        fine_mean[row] = restricted(fine, row)

    @pl.when(has_next)
    def _():
        pack_strips(lambda row, col, count: fine_mean[row, pl.ds(col, count), :], new_strips, COARSE_REACH)
        send_all(chain_copies, 1, AROUND)
        send_all(chain_copies, 1, ((0, 0),))

    count_c = cols_c + 2 * EDGE
    begin_c = FRONT - EDGE
    across = pl.ds(begin_c, count_c)
    mask_y = inside_y(begin_c, count_c, cols_c)
    place_c = lax.broadcasted_iota(jnp.int32, (count_c, LANES), 0) - EDGE
    mask_near = jnp.logical_and(mask_y, jnp.logical_and(place_c >= -1, place_c <= cols_c))

    def extend(buffer, strips, target, reach):
        _, row_in, _, side_in, _, corner_in = strips
        for side, col in ((0, end_c), (1, FRONT - reach)):
            for row in range(part_c):
                buffer[row, pl.ds(col, reach), :] = side_in[side, row]
            for towards in range(2):
                for k in range(reach // 2):
                    row_in[towards, k, pl.ds(col, reach), :] = corner_in[towards, side, k]

        def own(row):
            return buffer[row, across, :]

        values = [own(row) for row in range(part_c)]
        for k in range(reach // 2):
            above, below = (row_in[towards, k, across, :] for towards in (0, 1))
            after, before = 2 * k, part_c - 2 * k - 2
            values = [
                jnp.where(low_lanes, below, swapped(own(before))),
                swapped(jnp.where(high_lanes, below, own(before + 1))),
                *values,
                swapped(jnp.where(low_lanes, above, own(after))),
                jnp.where(high_lanes, above, swapped(own(after + 1))),
            ]
        for row, value in enumerate(values):
            mask = mask_y
            if not reach <= row < reach + part_c:
                mask = jnp.logical_and(mask_y, inside_x(row, reach, part_c))
            target[row, across, :] = jnp.where(mask, value, 0.0)

    def image_of(source, image):
        for row in range(image.shape[0]):
            image[row] = advance(source, row + 1, begin_c, count_c, coarse_constants)

    def change_of(source, image, reach, result):
        for row in range(image.shape[0]):
            moved = advance(source, row + 1, begin_c, count_c, coarse_constants) - image[row]
            columns = mask_near if reach == COARSE_REACH else mask_y
            mask = jnp.logical_and(columns, inside_x(row + 1, reach, part_c))
            result[row, across, :] = jnp.where(mask, moved, 0.0)

    def smoothed(source, row, start, count):
        line[across, :] = (
            mean_side * (source[row, across, :] + source[row + 2, across, :]) + mean_mid * source[row + 1, across, :]
        )
        sides = line[pl.ds(start - 1, count), :] + line[pl.ds(start + 1, count), :]
        return mean_side * sides + mean_mid * line[pl.ds(start, count), :]

    def find_lift(put):
        change_of(long_extended, prior_image, LONG_REACH, prior_change)
        for row in range(wide_c):
            mask = jnp.logical_and(mask_y, inside_x(row, COARSE_REACH, part_c))
            put(row, jnp.where(mask, smoothed(prior_change, row, begin_c, count_c), 0.0))

    def keep_lift(row, value):
        lift[row] = value

    def add_lift(row, value):
        extended[row, across, :] = extended[row, across, :] + value

    all_arrived(old_copies, old_in, AROUND)
    extend(old_own, old_strips, extended, COARSE_REACH)
    image_of(extended, old_image)
    def send_on():
        for row in range(part_c):
            sent[row] = fine_mean[row] + smoothed(change, row, FRONT, cols_c)
        pack_strips(lambda row, col, count: sent[row, pl.ds(col, count), :], prior_new_strips, LONG_REACH)
        pl.semaphore_wait(ready.at[1], 1)
        send_all(prior_new_copies, 2, AROUND)
        send_all(prior_new_copies, 2, ((0, 0),))

    @pl.when(tm == 0)
    def _():
        change_of(extended, old_image, COARSE_REACH, change)

    @pl.when(tm > 0)
    def _():
        fill_missing(chain_copies, AROUND)

    @pl.when(tm > 1)
    def _():
        fill_missing(prior_new_copies, AROUND)

    for row in range(part):
        turned[row] = fine[REACH + row, pl.ds(FRONT, cols), :].T

    pl.when(jnp.logical_and(tm == 0, has_second))(send_on)

    @pl.when(tm > 0)
    def _():
        all_arrived(prior_old_copies, prior_old_in, PLANE)
        extend(prior_old_own, prior_old_strips, long_extended, LONG_REACH)
        image_of(long_extended, prior_image)
        pl.when(tm == 1)(lambda: find_lift(keep_lift))
        all_arrived(chain_copies, chain_in, PLANE)
        extend(new_own, new_strips, extended, COARSE_REACH)

        @pl.when(tm > 1)
        def _():
            all_arrived(prior_new_copies, prior_new_in, PLANE)
            extend(prior_new_own, prior_new_strips, long_extended, LONG_REACH)
            find_lift(add_lift)

        @pl.when(tm == 1)
        def _():
            for row in range(wide_c):
                add_lift(row, lift[row])

        change_of(extended, old_image, COARSE_REACH, change)
        pl.when(has_second)(send_on)

    sends_done(fine_copies, 0, y_moves)
    sends_done(old_copies, 0, AROUND)
    sends_done(near_copies, 0, x_moves)
    sends_done(far_copies, 0, x_moves)
    @pl.when(has_next)
    def _():
        sends_done(chain_copies, 1, PLANE)
        sends_done(prior_old_copies, 1, PLANE)

    pl.when(has_second)(lambda: sends_done(prior_new_copies, 2, PLANE))


def closing(levels, rows, turned, change, out_hbm, filled, spread_rows, sem):
    packs = LANES // levels
    part, _, cols = turned.shape
    part_c = part // RATIO
    count_c = cols // RATIO + 2 * EDGE
    coarse_col = lax.broadcasted_iota(jnp.int32, (count_c, cols), 0) - EDGE
    fine_col = lax.broadcasted_iota(jnp.int32, (count_c, cols), 1)
    offset_of = fine_col & (RATIO - 1)
    apart = coarse_col - (fine_col >> (RATIO.bit_length() - 1))
    spreading = jnp.zeros((count_c, cols), jnp.float32)
    for o in range(RATIO):
        for distance, weights in ((-1, weights_low), (0, weights_mid), (1, weights_high)):
            chosen = jnp.logical_and(offset_of == o, apart == distance)
            spreading = jnp.where(chosen, weights[o], spreading)
    spreading = jnp.concatenate([spreading.astype(jnp.bfloat16)] * 3, axis=0)

    def spread_row(row):
        rest, pieces = change[row, pl.ds(FRONT - EDGE, count_c), :], []
        for _ in range(3):
            piece = rest.astype(jnp.bfloat16).astype(jnp.float32)
            pieces.append(piece)
            rest = rest - piece
        split = jnp.concatenate(pieces, axis=0).T.astype(jnp.bfloat16)
        return jnp.dot(split, spreading, preferred_element_type=jnp.float32)

    for row in range(2):
        spread_rows[row] = spread_row(row)
    for row in range(part):
        at, o = row // RATIO, row % RATIO
        if o == 0:
            spread_rows[at + 2] = spread_row(at + 2)
        total = turned[row] + weights_mid[o] * spread_rows[at + 1]
        if weights_low[o]:
            total = total + weights_low[o] * spread_rows[at]
        if weights_high[o]:
            total = total + weights_high[o] * spread_rows[at + 2]
        filled[row] = total
        for p in range(packs):
            x = p * part + row
            pltpu.make_async_copy(filled.at[row, pl.ds(p * levels, levels)], out_hbm.at[:, x], sem).start()
    pltpu.make_async_copy(filled, filled, sem).wait()


def shards(sizes, state_starts, diffusivity, wind):
    _, levels, rows, cols = state_starts.shape
    packs = LANES // levels
    if packs != 2 or levels * packs != LANES:
        raise ValueError(levels)
    part = rows // packs
    part_c = part // RATIO
    cols_c = cols // RATIO
    wide, wide_c, wide_long = part + 2 * REACH, part_c + 2 * COARSE_REACH, part_c + 2 * LONG_REACH
    if part_c < LONG_REACH:
        raise ValueError(part_c)
    vmem = functools.partial(pltpu.VMEM, dtype=jnp.float32)
    scratch = [
        vmem((rows, levels, cols)),
        vmem((3, levels)),
        pltpu.SemaphoreType.DMA((2,)),
        pltpu.SemaphoreType.DMA,
        pltpu.SemaphoreType.REGULAR((2,)),
        vmem((wide, cols + 2 * FRONT, LANES)),
        vmem((wide, cols + 2 * FRONT, LANES)),
        vmem((2, REACH, levels, cols)),
        vmem((2, part, REACH, LANES)),
        vmem((2, part, REACH, LANES)),
        vmem((2, 2, REACH, REACH, LANES)),
        *[vmem((part_c, cols_c + 2 * FRONT, LANES))] * 4,
        vmem((wide_c, cols_c + 2 * FRONT, LANES)),
        vmem((wide_long, cols_c + 2 * FRONT, LANES)),
        vmem((wide_c - 2, cols_c + 2 * EDGE, LANES)),
        vmem((wide_long - 2, cols_c + 2 * EDGE, LANES)),
        vmem((wide_long - 2, cols_c + 2 * FRONT, LANES)),
        vmem((wide_c, cols_c + 2 * EDGE, LANES)),
        vmem((part_c, cols_c, LANES)),
        vmem((part_c, cols_c, LANES)),
        vmem((cols_c + 2 * FRONT, LANES)),
        vmem((cols, LANES)),
        vmem((TALLY, LANES)),
    ] + [pltpu.SemaphoreType.DMA] * 9
    for reach in (COARSE_REACH, COARSE_REACH, LONG_REACH, LONG_REACH):
        scratch += [
            vmem((2, reach // 2, cols_c, LANES)),
            vmem((2, reach // 2, cols_c + 2 * FRONT, LANES)),
            vmem((2, part_c, reach, LANES)),
            vmem((2, part_c, reach, LANES)),
            vmem((2, 2, reach // 2, reach, LANES)),
            vmem((2, 2, reach // 2, reach, LANES)),
        ]
    in_vmem = pl.BlockSpec(memory_space=pltpu.VMEM)
    handed = pl.pallas_call(
        functools.partial(kernel, sizes, levels, rows, cols),
        out_shape=(vmem((part, LANES, cols)), vmem((part_c + 2, cols_c + 2 * FRONT, LANES))),
        in_specs=[pl.BlockSpec(memory_space=pl.ANY)] * 3,
        out_specs=(in_vmem, in_vmem),
        scratch_shapes=scratch,
        compiler_params=pltpu.CompilerParams(collective_id=0, has_side_effects=True),
        name="parareal",
    )(state_starts.reshape(levels, rows, cols), diffusivity.reshape(1, levels), wind)
    ending = pl.pallas_call(
        functools.partial(closing, levels, rows),
        out_shape=jax.ShapeDtypeStruct((levels, rows, cols), jnp.float32),
        in_specs=[in_vmem, in_vmem],
        out_specs=pl.BlockSpec(memory_space=pl.ANY),
        scratch_shapes=[
            vmem((part, LANES, cols)),
            vmem((part_c + 2, LANES, cols)),
            pltpu.SemaphoreType.DMA,
        ],
        name="closing",
    )(*(pltpu.with_memory_space_constraint(array, pltpu.VMEM) for array in handed))
    return ending.reshape(1, levels, rows, cols)


def solution(mesh):
    sizes = tuple(mesh.shape[axis] for axis in ("tm", "gx", "gy"))
    placed = (P("tm", None, "gx", "gy"), P(), P())
    return jax.shard_map(
        functools.partial(shards, sizes),
        mesh=mesh, in_specs=placed, out_specs=P("tm", None, "gx", "gy"), check_vma=False,
    )
```
